512 devices in a mesh: slab: 128 (over x, z, core), ctrl: 4 (over y).
Axes of the slice: x: 4, y: 4, z: 16, core: 2. Of those that a mesh axis runs over, the one named last changes fastest.
Arguments:
- face_pressure: float32 [2097152], P(('slab', 'ctrl')), may hold values from 0 to 18
- face_area: float32 [3, 2097152], P(None, ('slab', 'ctrl')), may hold values from -0.00390625 to 0.00390625
- face_center: float32 [3, 2097152], P(None, ('slab', 'ctrl')), may hold values from -6 to 6
- motion: float32 [6], replicated, may hold values from -1 to 1
- inverse_mass: float32 [6], replicated, may hold values from 0.5 to 2
- control_points: float32 [3, 8192], P(None, ('slab', 'ctrl')), may hold values from -4 to 4
- control_modes: float32 [18, 8192], P(None, ('slab', 'ctrl')), may hold values from -0.25 to 0.25
- node_points: float32 [3, 1024, 32, 128], P(None, 'slab', 'ctrl'), may hold values from -5 to 5
- tile_list: int32 [1024, 32, 16], P('slab', 'ctrl'), may hold values from 0 to 63, as said below
- tile_count: int32 [1024, 32], P('slab', 'ctrl'), may hold values from 0 to 16, as said below
Outputs:
- node_shift: float32 [3, 1024, 32, 128], P(None, 'slab', 'ctrl')
- cell_volume: float32 [1024, 32, 128], P('slab', 'ctrl')
- volume_change: float32 [1024, 32, 128], P('slab', 'ctrl')
- new_state: float32 [6], replicated
The draws below stay inside these ranges and needn't reach their ends.
Inputs may be any that keep to these rules, and one draw needn't show every extreme that they name: `tile_list`: the entries of one line are distinct tile numbers; only the first tile_count entries of a line are live, the others are to be ignored. `tile_count`: every line in the planes x with 3072 <= 8 x < 5120 has 16 live entries; every other line has at most 4.
All inputs are finite; a program needn't handle non-finite values.
Results may differ from the reference program's by a relative error of at most 0.0003.
Values sent between devices are 32-bit elements; how exact they have to be, the bound alone decides.
A program may use at most 64 MiB of HBM per device.

```python
import math
import jax
import jax.numpy as jnp
from jax import lax

NZ = 128
NCTRL = 8192
TILE = 128
KMAX = 16
NTILE = 64
FACES = 2097152
NX = 1024
NY = 32


def draw_face_pressure(key, part):
    position = jnp.arange(FACES, dtype=jnp.float32)
    ramp_up = 1.0 + 2.0 * position / FACES
    base_level = jnp.clip(1.0 + 0.25 * jax.random.normal(key, (FACES,), jnp.float32), 0.25, 1.75)
    return ramp_up * base_level


def tile_draws(key):
    score_key = jax.random.fold_in(key, 101)
    light_key = jax.random.fold_in(key, 202)
    scores = jax.random.randint(score_key, (NX, NY, NTILE), 0, 1 << 20, dtype=jnp.int32) * NTILE
    scores = scores + jnp.arange(NTILE, dtype=jnp.int32)
    ranking = jnp.argsort(scores, axis=-1, stable=True)
    tile_ids = ranking[:, :, :KMAX].astype(jnp.int32)
    planes = jnp.arange(NX, dtype=jnp.int32)
    heavy_rows = (8 * planes >= 3 * NX) & (8 * planes < 5 * NX)
    light_count = jax.random.randint(light_key, (NX, NY), 0, KMAX // 4 + 1, dtype=jnp.int32)
    counts = jnp.where(heavy_rows[:, None], KMAX, light_count).astype(jnp.int32)
    return (tile_ids, counts)


def draw_tile_list(key, part):
    return tile_draws(key)[0]


def draw_tile_count(key, part):
    return tile_draws(key)[1]


def steps_of(rng, dims, cuts, low, high):
    def one(dim, parts):
        heights = jax.random.uniform(jax.random.fold_in(jax.random.fold_in(rng, 6), dim), (parts,), jnp.float32, low / len(cuts), high / len(cuts))
        return jnp.repeat(jnp.exp(heights), dims[dim] // parts).reshape((-1,) + (1,) * (len(dims) - dim - 1))

    level = one(*cuts[0])
    for cut in cuts[1:]:
        level = level * one(*cut)
    return level


def centred(key, extent, spread, limit, cuts=(), kind=jnp.bfloat16):
    values = spread * jax.random.normal(key, extent, jnp.float32)
    if cuts:
        values = values * steps_of(key, extent, cuts, -0.22, 0.18)
    return jnp.clip(values, -limit, limit).astype(kind)


def setup_inputs(seed: int = 0) -> dict:
    streams_of = jax.random.split(jax.random.key(seed), 11)
    face_pressure = draw_face_pressure(jax.random.fold_in(streams_of[10], 71), 0)
    face_area = centred(streams_of[1], (3, FACES), FACES ** -0.5, 0.00390625, ((1, 512),), jnp.float32)
    face_center = centred(streams_of[2], (3, FACES), 1.0, 6.0, ((1, 512),), jnp.float32)
    motion = jnp.clip(jax.random.uniform(streams_of[3], (6,), jnp.float32, -1.0, 1.0), -1.0, 1.0)
    inverse_mass = jnp.clip(jnp.exp(jax.random.uniform(streams_of[4], (6,), jnp.float32, math.log(0.5), math.log(2.0))), 0.5, 2.0)
    control_points = centred(streams_of[5], (3, NCTRL), 0.7, 4.0, ((1, 512),), jnp.float32)
    control_modes = centred(streams_of[6], (18, NCTRL), (4 * TILE) ** -0.5, 0.25, ((1, 512),), jnp.float32)
    node_points = centred(streams_of[7], (3, NX, NY, NZ), 1.0, 5.0, ((1, 128), (2, 4)), jnp.float32)
    tile_list = draw_tile_list(jax.random.fold_in(streams_of[10], 71), 0)
    tile_count = draw_tile_count(jax.random.fold_in(streams_of[10], 71), 0)
    return dict(face_pressure=face_pressure, face_area=face_area, face_center=face_center, motion=motion, inverse_mass=inverse_mass, control_points=control_points, control_modes=control_modes, node_points=node_points, tile_list=tile_list, tile_count=tile_count)


TIME_STEP = 0.5
RADIUS = 4.0
GRAVITY = (0.0, 0.0, -0.5, 0.0, 0.0, 0.0)

def surface_loads(pressure, area, center):
    pushed = pressure[None, :] * area
    forces = lax.optimization_barrier(jnp.sum(pushed, axis=1))
    moment_x = jnp.sum(center[1] * pushed[2] - center[2] * pushed[1])
    moment_y = jnp.sum(center[2] * pushed[0] - center[0] * pushed[2])
    moment_z = jnp.sum(center[0] * pushed[1] - center[1] * pushed[0])
    return jnp.concatenate([forces, jnp.stack([moment_x, moment_y, moment_z])])

def advance(total_loads, motion, inverse_mass):
    acceleration = inverse_mass * total_loads + jnp.array(GRAVITY, dtype=jnp.float32)
    new_state = motion + TIME_STEP * acceleration
    rigid_step = TIME_STEP * motion + 0.5 * TIME_STEP * TIME_STEP * acceleration
    return (new_state, rigid_step)

def mode_mix(rigid_step, modes):
    shaped = modes.reshape(6, 3, modes.shape[1])
    return jnp.einsum('k,kcj->cj', rigid_step, shaped, precision=lax.Precision.HIGHEST)

def kernel_sum(points, tile_ids, counts, center_tiles, coeff_tiles):
    longest = jnp.max(counts)

    def accumulate(entry_id, running):
        picked = jnp.take(tile_ids, entry_id, axis=1)
        centers = jnp.take(center_tiles, picked, axis=1)
        coeffs = jnp.take(coeff_tiles, picked, axis=1)
        square = jnp.zeros((points.shape[1], points.shape[2], centers.shape[2]), jnp.float32)
        for axis_id in range(3):
            offset = points[axis_id][:, :, None] - centers[axis_id][:, None, :]
            square = square + offset * offset
        radial = jnp.sqrt(square) / RADIUS
        falloff = jnp.maximum(1.0 - radial, 0.0)
        fourth = falloff * falloff
        fourth = fourth * fourth
        kernel = fourth * (4.0 * radial + 1.0)
        alive_mask = (entry_id < counts)[:, None, None]
        kernel = jnp.where(alive_mask, kernel, 0.0)
        return running + jnp.einsum('lnj,clj->cln', kernel, coeffs, precision=lax.Precision.HIGHEST)
    start = jnp.zeros((3, points.shape[1], points.shape[2]), jnp.float32)
    return lax.fori_loop(0, longest, accumulate, start)

def cell_volumes(lattice):
    span_x = lattice.shape[-3] - 1
    span_y = lattice.shape[-2] - 1

    def corner(shift_x, shift_y, shift_z):
        sliced = lattice[..., shift_x:shift_x + span_x, shift_y:shift_y + span_y, :]
        if shift_z == 1:
            sliced = jnp.concatenate([sliced[..., 1:], jnp.zeros_like(sliced[..., :1])], axis=-1)
        return sliced
    corners = {}
    for shift_x in range(2):
        for shift_y in range(2):
            for shift_z in range(2):
                corners[shift_x, shift_y, shift_z] = corner(shift_x, shift_y, shift_z)
    edge_x = 0.0
    edge_y = 0.0
    edge_z = 0.0
    for first in range(2):
        for second in range(2):
            edge_x = edge_x + corners[1, first, second] - corners[0, first, second]
            edge_y = edge_y + corners[first, 1, second] - corners[first, 0, second]
            edge_z = edge_z + corners[first, second, 1] - corners[first, second, 0]
    edge_x = 0.25 * edge_x
    edge_y = 0.25 * edge_y
    edge_z = 0.25 * edge_z
    ex0, ex1, ex2 = (edge_x[..., 0, :, :, :], edge_x[..., 1, :, :, :], edge_x[..., 2, :, :, :])
    ey0, ey1, ey2 = (edge_y[..., 0, :, :, :], edge_y[..., 1, :, :, :], edge_y[..., 2, :, :, :])
    ez0, ez1, ez2 = (edge_z[..., 0, :, :, :], edge_z[..., 1, :, :, :], edge_z[..., 2, :, :, :])
    return ex0 * (ey1 * ez2 - ey2 * ez1) + ex1 * (ey2 * ez0 - ey0 * ez2) + ex2 * (ey0 * ez1 - ey1 * ez0)

def reference(face_pressure, face_area, face_center, motion, inverse_mass, control_points, control_modes, node_points, tile_list, tile_count):
    total_loads = surface_loads(face_pressure, face_area, face_center)
    new_state, rigid_step = advance(total_loads, motion, inverse_mass)
    coefficients = mode_mix(rigid_step, control_modes)
    center_tiles = control_points.reshape(3, NTILE, TILE)
    coeff_tiles = coefficients.reshape(3, NTILE, TILE)

    def one_plane(pieces):
        plane_points, plane_ids, plane_counts = pieces
        return kernel_sum(plane_points, plane_ids, plane_counts, center_tiles, coeff_tiles)
    shifted = lax.map(one_plane, (jnp.moveaxis(node_points, 1, 0), tile_list, tile_count))
    node_shift = jnp.moveaxis(shifted, 0, 1)
    displaced = node_points + node_shift
    stacked = jnp.stack([node_points, displaced])
    padded = jnp.pad(stacked, ((0, 0), (0, 0), (0, 1), (0, 1), (0, 0)))
    volumes = cell_volumes(padded)
    inside = (jnp.arange(NX, dtype=jnp.int32) < NX - 1)[:, None, None]
    inside = inside & (jnp.arange(NY, dtype=jnp.int32) < NY - 1)[None, :, None]
    inside = inside & (jnp.arange(NZ, dtype=jnp.int32) < NZ - 1)[None, None, :]
    volumes = jnp.where(inside[None], volumes, 0.0)
    return (node_shift, volumes[1], volumes[1] - volumes[0], new_state)
```

```python
import functools

import jax
import jax.numpy as jnp
from jax import lax
from jax.experimental import pallas as pl
from jax.experimental.pallas import tpu as pltpu
from jax.sharding import PartitionSpec as P

MESH = pl.DeviceIdType.MESH
TILE = 128
NTILE = 64
F32 = jnp.float32
BF16 = jnp.bfloat16
TIME_STEP = 0.5
GRAVITY = (0.0, 0.0, -0.5, 0.0, 0.0, 0.0)
XS, YS, ZS, CORES = 4, 4, 16, 2
LOAD_LANE = 80


def iota(shape, axis):
    return lax.broadcasted_iota(jnp.int32, shape, axis)


def place():
    slab = lax.axis_index("slab")
    return slab // (ZS * CORES), lax.axis_index("ctrl"), (slab // CORES) % ZS, slab % CORES


def device(x, y, z, core):
    return {"slab": (x % XS * ZS + z % ZS) * CORES + core, "ctrl": y % YS}


def gather_kernel(packed, pressure, area, center, buf, own, send, recv):
    x, y, z, core = place()
    group = core * YS + y
    plane = [(i * core, i * (1 - core)) for i in range(1, 4)]
    turned = [(i * (1 - core), i * core) for i in range(1, 4)]

    barrier = pltpu.get_barrier_semaphore()
    greet = [device(x, y, z + d, core) for d in (1, -1, 2, -2, 3, -3, 4, -4)]
    greet += [device(x + dx, y + dy, z, core) for dx, dy in plane + turned]
    greet += [device(x, y, z, 1 - core)]
    for target in greet:
        pl.semaphore_signal(barrier, inc=1, device_id=target, device_id_type=MESH)

    force = jnp.zeros((3, 128), F32)
    moment = jnp.zeros((3, 128), F32)
    for i in range(pressure.shape[1] // 128):
        at = pl.ds(i * 128, 128)
        pushed = area[:, at] * pressure[:, at]
        c = center[:, at]
        force = force + pushed
        moment = moment + jnp.concatenate(
            [
                c[1:2] * pushed[2:3] - c[2:3] * pushed[1:2],
                c[2:3] * pushed[0:1] - c[0:1] * pushed[2:3],
                c[0:1] * pushed[1:2] - c[1:2] * pushed[0:1],
            ],
            axis=0,
        )
    sums = jnp.sum(jnp.concatenate([force, moment], axis=0), axis=1, keepdims=True)
    lane = iota((6, 128), 1)
    row = iota((6, 128), 0)
    loads = jnp.sum(jnp.where(lane == row + LOAD_LANE, sums, 0.0), axis=0, keepdims=True)
    own[0] = packed[0]
    own[1] = packed[1]
    own[2] = packed[2] + loads
    for r in range(3):
        buf[x, z, r, group] = own[r]

    pl.semaphore_wait(barrier, len(greet))

    pending = []

    def put(src, dst, slot, target):
        copy = pltpu.make_async_remote_copy(
            src_ref=src,
            dst_ref=dst,
            send_sem=send.at[slot],
            recv_sem=recv.at[slot],
            device_id=target,
            device_id_type=MESH,
        )
        copy.start()
        pending.append(copy)
        return copy

    def block(zz):
        return buf.at[x, zz % ZS, :, group]

    near = {}
    for d in (4, 3, 2, 1):
        near[d] = put(own, block(z), d - 1, device(x, y, z + d, core))
        near[-d] = put(own, block(z), d + 3, device(x, y, z - d, core))
    far = []
    for d in (1, 2, 3, 4):
        near[d].wait_recv()
        far.append(put(block(z - d), block(z - d), d + 7, device(x, y, z + 4, core)))
        near[-d].wait_recv()
        if d < 4:
            far.append(put(block(z + d), block(z + d), d + 11, device(x, y, z - 4, core)))
    for copy in far:
        copy.wait_recv()

    first = [
        put(buf.at[x, :, :, group], buf.at[x, :, :, group], 15 + i, device(x + dx, y + dy, z, core))
        for i, (dx, dy) in enumerate(plane)
    ]
    for copy in first:
        copy.wait_recv()

    def cross(i, dx, dy, start):
        target = device(x + dx, y + dy, z, core)

        def make(ref):
            return pltpu.make_async_remote_copy(
                src_ref=ref,
                dst_ref=ref,
                send_sem=send.at[18 + i],
                recv_sem=recv.at[18 + i],
                device_id=target,
                device_id_type=MESH,
            )

        @pl.when(core == 0)
        def _():
            copy = make(buf.at[x, :, :, pl.ds(0, YS)])
            copy.start() if start else copy.wait()

        @pl.when(core == 1)
        def _():
            copy = make(buf.at[:, :, :, group])
            copy.start() if start else copy.wait()

    for i, (dx, dy) in enumerate(turned):
        cross(i, dx, dy, True)
    for i, (dx, dy) in enumerate(turned):
        cross(i, dx, dy, False)

    half = buf.at[:, :, :, pl.ds(core * YS, YS)]
    put(half, half, 21, device(x, y, z, 1 - core)).wait_recv()
    for copy in pending:
        copy.wait_send()


def gather(packed, pressure, area, center):
    vmem = pl.BlockSpec(memory_space=pltpu.VMEM)
    return pl.pallas_call(
        gather_kernel,
        out_shape=jax.ShapeDtypeStruct((XS, ZS, 3, 8, 1, 128), F32),
        in_specs=[vmem] * 4,
        out_specs=vmem,
        scratch_shapes=[
            pltpu.VMEM((3, 1, 128), F32),
            pltpu.SemaphoreType.DMA((22,)),
            pltpu.SemaphoreType.DMA((22,)),
        ],
        compiler_params=pltpu.CompilerParams(collective_id=0, has_side_effects=True),
        name="gather",
    )(packed, pressure, area, center)


def split3(value):
    hi = value.astype(BF16).astype(F32)
    rest = value - hi
    mid = rest.astype(BF16).astype(F32)
    return hi, mid, rest - mid


def regroup(v):
    sub = iota((8, 128), 0)
    grp = iota((8, 128), 1) // 16
    for bit in (1, 2, 4):
        below = pltpu.roll(pltpu.roll(v, 8 - bit, 0), 16 * bit, 1)
        above = pltpu.roll(pltpu.roll(v, bit, 0), 128 - 16 * bit, 1) if bit < 4 else below
        low = (sub & bit) == 0
        same = low == ((grp & bit) == 0)
        v = jnp.where(same, v, jnp.where(low, below, above))
    return v


def pair_kernel(ids, counts, motion, inverse_mass, raw, nodes, shift, state, feats, left, mix):
    def unpack(t, total):
        v = [regroup(raw[t, r]) for r in range(3)]
        for r in range(3):
            feats[t, pl.ds(8 * r, 8), :] = v[r]
        return total + v[2]

    total = lax.fori_loop(0, NTILE, unpack, jnp.zeros((8, 128), F32))
    total = jnp.broadcast_to(total[5:6, :], (8, 128))
    for by in (16, 32, 64):
        total = total + pltpu.roll(total, by, 1)
    rigid = []
    for k in range(6):
        load = jnp.broadcast_to(total[:, k : k + 1], (8, 128))
        acceleration = inverse_mass[k] * load + GRAVITY[k]
        state[k, :, :] = motion[k] + TIME_STEP * acceleration
        rigid.append((TIME_STEP * motion[k] + 0.5 * TIME_STEP * TIME_STEP * acceleration)[0:3])

    sub = iota((8, 128), 0)

    def prepare(t, _):
        p = feats[t, 0:8, :]
        p = jnp.where(sub < 3, p, 0.0)
        square = jnp.sum(p * p, axis=0, keepdims=True)
        hi, mid, lo = split3(jnp.where(sub < 3, p, jnp.where(sub == 3, square, jnp.where(sub == 4, 1.0, 0.0))))
        columns = jnp.concatenate([hi, hi, mid, mid, hi, lo], axis=0)
        left[t] = jnp.transpose(columns, (1, 0)).astype(BF16)
        c = jnp.zeros((3, 128), F32)
        for k in range(6):
            c = c + rigid[k] * feats[t, 3 + 3 * k : 6 + 3 * k, :]
        c = jnp.concatenate([c * (1.0 / 256.0), jnp.zeros((5, 128), F32)], axis=0)
        c_hi = c.astype(BF16).astype(F32)
        mix[t] = jnp.concatenate([c_hi, c - c_hi], axis=0).astype(BF16)
        return 0

    lax.fori_loop(0, NTILE, prepare, 0)

    unroll = 4

    def line(i, _):
        p, r = i // 8, i % 8
        x0 = nodes[0, p, pl.ds(r, 1), :]
        x1 = nodes[1, p, pl.ds(r, 1), :]
        x2 = nodes[2, p, pl.ds(r, 1), :]
        square = x0 * x0 + x1 * x1 + x2 * x2
        rows = jnp.where(sub == 0, -2.0 * x0, 0.0)
        rows = jnp.where(sub == 1, -2.0 * x1, rows)
        rows = jnp.where(sub == 2, -2.0 * x2, rows)
        rows = jnp.where(sub == 3, 1.0, rows)
        rows = jnp.where(sub == 4, square, rows)
        hi, mid, lo = split3(rows)
        right = jnp.concatenate([hi, mid, hi, mid, lo, hi], axis=0).astype(BF16)
        count = counts[p, r]

        def some(g, acc):
            for u in range(unroll):
                e = g * unroll + u
                t = ids[p, r, e]
                s = jnp.dot(left[t], right, preferred_element_type=F32)
                s = jnp.minimum(jnp.maximum(s, 1e-30), 16.0)
                d = s * lax.rsqrt(s)
                v = 4.0 - d
                v = v * v
                k = v * v * (1.0 + d)
                k_hi = k.astype(BF16)
                k_lo = (k - k_hi.astype(F32)).astype(BF16)
                m = mix[t] * jnp.where(e < count, 1.0, 0.0).astype(BF16)
                acc = acc + jnp.dot(m, k_hi, preferred_element_type=F32)
                acc = acc + jnp.dot(m, k_lo, preferred_element_type=F32)
            return acc

        acc = lax.fori_loop(0, (count + unroll - 1) // unroll, some, jnp.zeros((16, 128), F32))
        acc = acc[0:8] + acc[8:16]
        for c in range(3):
            shift[c, p, pl.ds(r, 1), :] = acc[c : c + 1, :]
        return 0

    lax.fori_loop(0, 64, line, 0)


def pair_sums(ids, counts, motion, inverse_mass, raw, nodes):
    vmem = pl.BlockSpec(memory_space=pltpu.VMEM)
    smem = pl.BlockSpec(memory_space=pltpu.SMEM)
    return pl.pallas_call(
        pair_kernel,
        out_shape=(
            jax.ShapeDtypeStruct(nodes.shape, F32),
            jax.ShapeDtypeStruct((6, 8, 128), F32),
        ),
        in_specs=[smem, smem, smem, smem, vmem, vmem],
        out_specs=(vmem, vmem),
        scratch_shapes=[
            pltpu.VMEM((NTILE, 24, 128), F32),
            pltpu.VMEM((NTILE, 128, 48), BF16),
            pltpu.VMEM((NTILE, 16, 128), BF16),
        ],
        name="pairs",
    )(ids, counts, motion, inverse_mass, raw, nodes)


def shifted(value, axis, by):
    devices = lax.axis_size(axis)
    pairs = [(i, i + by) for i in range(devices) if 0 <= i + by < devices]
    return lax.ppermute(value, axis, pairs)


def cell_volumes(lattice):
    span_x = lattice.shape[-3] - 1
    span_y = lattice.shape[-2] - 1
    corners = {}
    for shift_x in range(2):
        for shift_y in range(2):
            for shift_z in range(2):
                sliced = lattice[..., shift_x : shift_x + span_x, shift_y : shift_y + span_y, :]
                if shift_z == 1:
                    sliced = jnp.concatenate([sliced[..., 1:], jnp.zeros_like(sliced[..., :1])], axis=-1)
                corners[shift_x, shift_y, shift_z] = sliced
    edge_x = 0.0
    edge_y = 0.0
    edge_z = 0.0
    for first in range(2):
        for second in range(2):
            edge_x = edge_x + corners[1, first, second] - corners[0, first, second]
            edge_y = edge_y + corners[first, 1, second] - corners[first, 0, second]
            edge_z = edge_z + corners[first, second, 1] - corners[first, second, 0]
    edge_x = 0.25 * edge_x
    edge_y = 0.25 * edge_y
    edge_z = 0.25 * edge_z
    ex0, ex1, ex2 = (edge_x[..., 0, :, :, :], edge_x[..., 1, :, :, :], edge_x[..., 2, :, :, :])
    ey0, ey1, ey2 = (edge_y[..., 0, :, :, :], edge_y[..., 1, :, :, :], edge_y[..., 2, :, :, :])
    ez0, ez1, ez2 = (edge_z[..., 0, :, :, :], edge_z[..., 1, :, :, :], edge_z[..., 2, :, :, :])
    return (
        ex0 * (ey1 * ez2 - ey2 * ez1)
        + ex1 * (ey2 * ez0 - ey0 * ez2)
        + ex2 * (ey0 * ez1 - ey1 * ez0)
    )


def local(
    face_pressure,
    face_area,
    face_center,
    motion,
    inverse_mass,
    control_points,
    control_modes,
    node_points,
    tile_list,
    tile_count,
):
    packed = jnp.concatenate([control_points, control_modes, jnp.zeros((3, 16), F32)], axis=0).reshape(3, 1, 128)
    raw = gather(packed, face_pressure.reshape(1, -1), face_area, face_center)
    node_shift, state = pair_sums(
        tile_list, tile_count, motion, inverse_mass, raw.reshape(NTILE, 3, 8, 128), node_points
    )
    new_state = state[:, 0, 0]

    plane_count = node_points.shape[1]
    row_count = node_points.shape[2]
    line_nodes = node_points.shape[3]
    displaced = node_points + node_shift
    stacked = jnp.stack([node_points, displaced])
    next_plane = shifted(stacked[:, :, :1], "slab", -1)
    widened = jnp.concatenate([stacked, next_plane], axis=2)
    next_row = shifted(widened[:, :, :, :1], "ctrl", -1)
    extended = jnp.concatenate([widened, next_row], axis=3)
    volumes = cell_volumes(extended)
    plane_total = plane_count * lax.axis_size("slab")
    row_total = row_count * lax.axis_size("ctrl")
    plane_ids = lax.axis_index("slab") * plane_count + jnp.arange(plane_count, dtype=jnp.int32)
    row_ids = lax.axis_index("ctrl") * row_count + jnp.arange(row_count, dtype=jnp.int32)
    depth_ids = jnp.arange(line_nodes, dtype=jnp.int32)
    inside = (plane_ids < plane_total - 1)[:, None, None]
    inside = inside & (row_ids < row_total - 1)[None, :, None]
    inside = inside & (depth_ids < line_nodes - 1)[None, None, :]
    volumes = jnp.where(inside[None], volumes, 0.0)
    return (node_shift, volumes[1], volumes[1] - volumes[0], new_state)


def solution(mesh):
    placed = (
        P(("slab", "ctrl")),
        P(None, ("slab", "ctrl")),
        P(None, ("slab", "ctrl")),
        P(),
        P(),
        P(None, ("slab", "ctrl")),
        P(None, ("slab", "ctrl")),
        P(None, "slab", "ctrl", None),
        P("slab", "ctrl", None),
        P("slab", "ctrl"),
    )
    return jax.shard_map(
        local,
        mesh=mesh,
        in_specs=placed,
        out_specs=(
            P(None, "slab", "ctrl", None),
            P("slab", "ctrl", None),
            P("slab", "ctrl", None),
            P(),
        ),
        check_vma=False,
    )
```

```python
import functools

import jax
import jax.numpy as jnp
from jax import lax
from jax.experimental import pallas as pl
from jax.experimental.pallas import tpu as pltpu
from jax.sharding import PartitionSpec as P

MESH = pl.DeviceIdType.MESH
TILE = 128
NTILE = 64
F32 = jnp.float32
BF16 = jnp.bfloat16
TIME_STEP = 0.5
GRAVITY = (0.0, 0.0, -0.5, 0.0, 0.0, 0.0)
XS, YS, ZS, CORES = 4, 4, 16, 2
LOAD_LANE = 80


def iota(shape, axis):
    return lax.broadcasted_iota(jnp.int32, shape, axis)


def place():
    slab = lax.axis_index("slab")
    return slab // (ZS * CORES), lax.axis_index("ctrl"), (slab // CORES) % ZS, slab % CORES


def device(x, y, z, core):
    return {"slab": (x % XS * ZS + z % ZS) * CORES + core, "ctrl": y % YS}


def gather_kernel(packed, pressure, area, center, buf, own, send, recv):
    x, y, z, core = place()
    group = core * YS + y
    plane = [(i * core, i * (1 - core)) for i in range(1, 4)]
    turned = [(i * (1 - core), i * core) for i in range(1, 4)]

    barrier = pltpu.get_barrier_semaphore()
    greet = [device(x, y, z + d, core) for d in (1, -1, 2, -2, 3, -3, 4, -4)]
    greet += [device(x + dx, y + dy, z, core) for dx, dy in plane + turned]
    greet += [device(x, y, z, 1 - core)]
    for target in greet:
        pl.semaphore_signal(barrier, inc=1, device_id=target, device_id_type=MESH)

    force = jnp.zeros((3, 128), F32)
    moment = jnp.zeros((3, 128), F32)
    for i in range(pressure.shape[1] // 128):
        at = pl.ds(i * 128, 128)
        pushed = area[:, at] * pressure[:, at]
        c = center[:, at]
        force = force + pushed
        moment = moment + jnp.concatenate(
            [
                c[1:2] * pushed[2:3] - c[2:3] * pushed[1:2],
                c[2:3] * pushed[0:1] - c[0:1] * pushed[2:3],
                c[0:1] * pushed[1:2] - c[1:2] * pushed[0:1],
            ],
            axis=0,
        )
    sums = jnp.sum(jnp.concatenate([force, moment], axis=0), axis=1, keepdims=True)
    lane = iota((6, 128), 1)
    row = iota((6, 128), 0)
    loads = jnp.sum(jnp.where(lane == row + LOAD_LANE, sums, 0.0), axis=0, keepdims=True)
    own[0] = packed[0]
    own[1] = packed[1]
    own[2] = packed[2] + loads
    for r in range(3):
        buf[x, z, r, group] = own[r]

    pl.semaphore_wait(barrier, len(greet))

    pending = []

    def put(src, dst, slot, target):
        copy = pltpu.make_async_remote_copy(
            src_ref=src,
            dst_ref=dst,
            send_sem=send.at[slot],
            recv_sem=recv.at[slot],
            device_id=target,
            device_id_type=MESH,
        )
        copy.start()
        pending.append(copy)
        return copy

    def block(zz):
        return buf.at[x, zz % ZS, :, group]

    near = {}
    for d in (4, 3, 2, 1):
        near[d] = put(own, block(z), d - 1, device(x, y, z + d, core))
        near[-d] = put(own, block(z), d + 3, device(x, y, z - d, core))
    far = []
    for d in (1, 2, 3, 4):
        near[d].wait_recv()
        far.append(put(block(z - d), block(z - d), d + 7, device(x, y, z + 4, core)))
        near[-d].wait_recv()
        if d < 4:
            far.append(put(block(z + d), block(z + d), d + 11, device(x, y, z - 4, core)))
    for copy in far:
        copy.wait_recv()

    first = [
        put(buf.at[x, :, :, group], buf.at[x, :, :, group], 15 + i, device(x + dx, y + dy, z, core))
        for i, (dx, dy) in enumerate(plane)
    ]
    for copy in first:
        copy.wait_recv()

    def cross(i, dx, dy, start):
        target = device(x + dx, y + dy, z, core)

        def make(ref):
            return pltpu.make_async_remote_copy(
                src_ref=ref,
                dst_ref=ref,
                send_sem=send.at[18 + i],
                recv_sem=recv.at[18 + i],
                device_id=target,
                device_id_type=MESH,
            )

        @pl.when(core == 0)
        def _():
            copy = make(buf.at[x, :, :, pl.ds(0, YS)])
            copy.start() if start else copy.wait()

        @pl.when(core == 1)
        def _():
            copy = make(buf.at[:, :, :, group])
            copy.start() if start else copy.wait()

    for i, (dx, dy) in enumerate(turned):
        cross(i, dx, dy, True)
    for i, (dx, dy) in enumerate(turned):
        cross(i, dx, dy, False)

    half = buf.at[:, :, :, pl.ds(core * YS, YS)]
    put(half, half, 21, device(x, y, z, 1 - core)).wait_recv()
    for copy in pending:
        copy.wait_send()


def gather(packed, pressure, area, center):
    vmem = pl.BlockSpec(memory_space=pltpu.VMEM)
    return pl.pallas_call(
        gather_kernel,
        out_shape=jax.ShapeDtypeStruct((XS, ZS, 3, 8, 1, 128), F32),
        in_specs=[vmem] * 4,
        out_specs=vmem,
        scratch_shapes=[
            pltpu.VMEM((3, 1, 128), F32),
            pltpu.SemaphoreType.DMA((22,)),
            pltpu.SemaphoreType.DMA((22,)),
        ],
        compiler_params=pltpu.CompilerParams(collective_id=0, has_side_effects=True),
        name="gather",
    )(packed, pressure, area, center)


def split3(value):
    hi = value.astype(BF16).astype(F32)
    rest = value - hi
    mid = rest.astype(BF16).astype(F32)
    return hi, mid, rest - mid


def regroup(v):
    sub = iota((8, 128), 0)
    grp = iota((8, 128), 1) // 16
    for bit in (1, 2, 4):
        below = pltpu.roll(pltpu.roll(v, 8 - bit, 0), 16 * bit, 1)
        above = pltpu.roll(pltpu.roll(v, bit, 0), 128 - 16 * bit, 1) if bit < 4 else below
        low = (sub & bit) == 0
        same = low == ((grp & bit) == 0)
        v = jnp.where(same, v, jnp.where(low, below, above))
    return v


def node_rows(nodes, p, r):
    sub = iota((8, 128), 0)
    x = [nodes[c, p, pl.ds(r, 1), :] for c in range(3)]
    square = x[0] * x[0] + x[1] * x[1] + x[2] * x[2]
    rows = jnp.where((sub == 0) | (sub == 3), -2.0 * x[0], 0.0)
    rows = jnp.where((sub == 1) | (sub == 4), -2.0 * x[1], rows)
    rows = jnp.where((sub == 2) | (sub == 5), -2.0 * x[2], rows)
    rows = jnp.where(sub == 7, square, rows)
    hi, mid, lo = split3(rows)
    one = sub == 6
    second = (sub >= 3) & (sub < 6)
    parts = [
        jnp.where(one, 1.0, jnp.where(second, mid, hi)),
        jnp.where(one, 1.0, jnp.where(sub < 3, hi, mid)),
        jnp.where(one, 1.0, jnp.where(second, hi, lo)),
        jnp.zeros((8, 128), F32),
    ]
    return jnp.concatenate(parts, axis=0).astype(BF16)


def control_rows(p):
    sub = iota((8, 128), 0)
    p = jnp.where(sub < 3, p, 0.0)
    square = jnp.sum(p * p, axis=0, keepdims=True)
    rows = p + pltpu.roll(p, 3, 0) + jnp.where(sub == 6, square, 0.0)
    hi, mid, lo = split3(rows)
    one = sub == 7
    parts = [
        jnp.where(one, 1.0, hi),
        jnp.where(one, 1.0, mid),
        jnp.where(one, 1.0, jnp.where(sub < 3, hi, lo)),
        jnp.zeros((8, 128), F32),
    ]
    return parts


BLOCK = 32


def pair_kernel(
    ids, counts, motion, inverse_mass, raw, nodes, shift, state, feats, left_a, left_b, mix_a, mix_b, right, sums, tile_of, line_of
):
    lines = nodes.shape[1] * 8
    sub = iota((8, 128), 0)

    def unpack(t, carry):
        total, n = carry
        v = [regroup(raw[t, r]) for r in range(3)]
        for r in range(3):
            feats[t, pl.ds(8 * r, 8), :] = v[r]
        p, r = t // 8, t % 8
        for e in range(16):
            tile_of[n + e] = ids[p, r, e]
            line_of[n + e] = t
        return total + v[2], n + counts[p, r]

    total, n = lax.fori_loop(0, NTILE, unpack, (jnp.zeros((8, 128), F32), 0), unroll=4)
    for e in range(BLOCK):
        tile_of[n + e] = 0
        line_of[n + e] = lines
    total = jnp.broadcast_to(total[5:6, :], (8, 128))
    for by in (16, 32, 64):
        total = total + pltpu.roll(total, by, 1)
    rigid = []
    for k in range(6):
        load = jnp.broadcast_to(total[:, k : k + 1], (8, 128))
        acceleration = inverse_mass[k] * load + GRAVITY[k]
        state[k, :, :] = motion[k] + TIME_STEP * acceleration
        rigid.append((TIME_STEP * motion[k] + 0.5 * TIME_STEP * TIME_STEP * acceleration)[0:3])

    wide = iota((128, 64), 1) < 32

    def prepare(t, _):
        parts = control_rows(feats[t, 0:8, :])
        columns = jnp.transpose(jnp.concatenate(parts + parts, axis=0), (1, 0))
        left_a[t] = jnp.where(wide, columns, 0.0).astype(BF16)
        left_b[t] = jnp.where(wide, 0.0, columns).astype(BF16)
        c = jnp.zeros((3, 128), F32)
        for k in range(6):
            c = c + rigid[k] * feats[t, 3 + 3 * k : 6 + 3 * k, :]
        c = c * (1.0 / 256.0)
        c = jnp.concatenate([c, c, jnp.zeros((2, 128), F32)], axis=0)
        c_hi = c.astype(BF16).astype(F32)
        c = jnp.where(sub < 3, c_hi, c - c_hi)
        zero = jnp.zeros((8, 128), F32)
        mix_a[t] = jnp.concatenate([c, zero], axis=0).astype(BF16)
        mix_b[t] = jnp.concatenate([zero, c], axis=0).astype(BF16)
        right[t] = node_rows(nodes, t // 8, t % 8)
        sums[t] = zero
        return 0

    lax.fori_loop(0, NTILE, prepare, 0, unroll=4)
    right[lines] = jnp.zeros((32, 128), BF16)
    sums[lines] = jnp.zeros((8, 128), F32)

    gap = jnp.zeros((32, 128), BF16)

    def block(g, _):
        for u in range(0, BLOCK, 2):
            i = g * BLOCK + u
            t1, t2 = tile_of[i], tile_of[i + 1]
            l1, l2 = line_of[i], line_of[i + 1]
            rhs = jnp.concatenate(
                [jnp.concatenate([right[l1], gap], axis=1), jnp.concatenate([gap, right[l2]], axis=1)], axis=0
            )
            s = jnp.dot(left_a[t1] + left_b[t2], rhs, preferred_element_type=F32)
            s = jnp.minimum(jnp.maximum(s, 1e-30), 16.0)
            d = s * lax.rsqrt(s)
            v = 4.0 - d
            v = v * v
            k = v * v * (1.0 + d)
            hi = k.astype(BF16)
            lo = (k - hi.astype(F32)).astype(BF16)
            m = mix_a[t1] + mix_b[t2]
            out = jnp.dot(
                jnp.concatenate([m, m], axis=1), jnp.concatenate([hi, lo], axis=0), preferred_element_type=F32
            )
            sums[l1] += out[0:8, 0:128]
            sums[l2] += out[8:16, 128:256]
        return 0

    lax.fori_loop(0, (n + BLOCK - 1) // BLOCK, block, 0)

    def finish(i, _):
        v = sums[i]
        v = v + pltpu.roll(v, 5, 0)
        for c in range(3):
            shift[c, i // 8, pl.ds(i % 8, 1), :] = v[c : c + 1, :]
        return 0

    lax.fori_loop(0, lines, finish, 0, unroll=8)


def pair_sums(ids, counts, motion, inverse_mass, raw, nodes):
    vmem = pl.BlockSpec(memory_space=pltpu.VMEM)
    smem = pl.BlockSpec(memory_space=pltpu.SMEM)
    lines = nodes.shape[1] * 8
    return pl.pallas_call(
        pair_kernel,
        out_shape=(
            jax.ShapeDtypeStruct(nodes.shape, F32),
            jax.ShapeDtypeStruct((6, 8, 128), F32),
        ),
        in_specs=[smem, smem, smem, smem, vmem, vmem],
        out_specs=(vmem, vmem),
        scratch_shapes=[
            pltpu.VMEM((NTILE, 24, 128), F32),
            pltpu.VMEM((NTILE, 128, 64), BF16),
            pltpu.VMEM((NTILE, 128, 64), BF16),
            pltpu.VMEM((NTILE, 16, 128), BF16),
            pltpu.VMEM((NTILE, 16, 128), BF16),
            pltpu.VMEM((lines + 1, 32, 128), BF16),
            pltpu.VMEM((lines + 1, 8, 128), F32),
            pltpu.SMEM((16 * lines + BLOCK,), jnp.int32),
            pltpu.SMEM((16 * lines + BLOCK,), jnp.int32),
        ],
        name="pairs",
    )(ids, counts, motion, inverse_mass, raw, nodes)


def shifted(value, axis, by):
    devices = lax.axis_size(axis)
    pairs = [(i, i + by) for i in range(devices) if 0 <= i + by < devices]
    return lax.ppermute(value, axis, pairs)


def cell_volumes(lattice):
    span_x = lattice.shape[-3] - 1
    span_y = lattice.shape[-2] - 1
    corners = {}
    for shift_x in range(2):
        for shift_y in range(2):
            for shift_z in range(2):
                sliced = lattice[..., shift_x : shift_x + span_x, shift_y : shift_y + span_y, :]
                if shift_z == 1:
                    sliced = jnp.concatenate([sliced[..., 1:], jnp.zeros_like(sliced[..., :1])], axis=-1)
                corners[shift_x, shift_y, shift_z] = sliced
    edge_x = 0.0
    edge_y = 0.0
    edge_z = 0.0
    for first in range(2):
        for second in range(2):
            edge_x = edge_x + corners[1, first, second] - corners[0, first, second]
            edge_y = edge_y + corners[first, 1, second] - corners[first, 0, second]
            edge_z = edge_z + corners[first, second, 1] - corners[first, second, 0]
    edge_x = 0.25 * edge_x
    edge_y = 0.25 * edge_y
    edge_z = 0.25 * edge_z
    ex0, ex1, ex2 = (edge_x[..., 0, :, :, :], edge_x[..., 1, :, :, :], edge_x[..., 2, :, :, :])
    ey0, ey1, ey2 = (edge_y[..., 0, :, :, :], edge_y[..., 1, :, :, :], edge_y[..., 2, :, :, :])
    ez0, ez1, ez2 = (edge_z[..., 0, :, :, :], edge_z[..., 1, :, :, :], edge_z[..., 2, :, :, :])
    return (
        ex0 * (ey1 * ez2 - ey2 * ez1)
        + ex1 * (ey2 * ez0 - ey0 * ez2)
        + ex2 * (ey0 * ez1 - ey1 * ez0)
    )


def local(
    face_pressure,
    face_area,
    face_center,
    motion,
    inverse_mass,
    control_points,
    control_modes,
    node_points,
    tile_list,
    tile_count,
):
    packed = jnp.concatenate([control_points, control_modes, jnp.zeros((3, 16), F32)], axis=0).reshape(3, 1, 128)
    raw = gather(packed, face_pressure.reshape(1, -1), face_area, face_center)
    node_shift, state = pair_sums(
        tile_list, tile_count, motion, inverse_mass, raw.reshape(NTILE, 3, 8, 128), node_points
    )
    new_state = state[:, 0, 0]

    plane_count = node_points.shape[1]
    row_count = node_points.shape[2]
    line_nodes = node_points.shape[3]
    displaced = node_points + node_shift
    stacked = jnp.stack([node_points, displaced])
    next_plane = shifted(stacked[:, :, :1], "slab", -1)
    widened = jnp.concatenate([stacked, next_plane], axis=2)
    next_row = shifted(widened[:, :, :, :1], "ctrl", -1)
    extended = jnp.concatenate([widened, next_row], axis=3)
    volumes = cell_volumes(extended)
    plane_total = plane_count * lax.axis_size("slab")
    row_total = row_count * lax.axis_size("ctrl")
    plane_ids = lax.axis_index("slab") * plane_count + jnp.arange(plane_count, dtype=jnp.int32)
    row_ids = lax.axis_index("ctrl") * row_count + jnp.arange(row_count, dtype=jnp.int32)
    depth_ids = jnp.arange(line_nodes, dtype=jnp.int32)
    inside = (plane_ids < plane_total - 1)[:, None, None]
    inside = inside & (row_ids < row_total - 1)[None, :, None]
    inside = inside & (depth_ids < line_nodes - 1)[None, None, :]
    volumes = jnp.where(inside[None], volumes, 0.0)
    return (node_shift, volumes[1], volumes[1] - volumes[0], new_state)


def solution(mesh):
    placed = (
        P(("slab", "ctrl")),
        P(None, ("slab", "ctrl")),
        P(None, ("slab", "ctrl")),
        P(),
        P(),
        P(None, ("slab", "ctrl")),
        P(None, ("slab", "ctrl")),
        P(None, "slab", "ctrl", None),
        P("slab", "ctrl", None),
        P("slab", "ctrl"),
    )
    return jax.shard_map(
        local,
        mesh=mesh,
        in_specs=placed,
        out_specs=(
            P(None, "slab", "ctrl", None),
            P("slab", "ctrl", None),
            P("slab", "ctrl", None),
            P(),
        ),
        check_vma=False,
    )
```

```python
import functools

import jax
import jax.numpy as jnp
from jax import lax
from jax.experimental import pallas as pl
from jax.experimental.pallas import tpu as pltpu
from jax.sharding import PartitionSpec as P

MESH = pl.DeviceIdType.MESH
TILE = 128
NTILE = 64
F32 = jnp.float32
BF16 = jnp.bfloat16
TIME_STEP = 0.5
GRAVITY = (0.0, 0.0, -0.5, 0.0, 0.0, 0.0)
XS, YS, ZS, CORES = 4, 4, 16, 2
LOAD_LANE = 80


def iota(shape, axis):
    return lax.broadcasted_iota(jnp.int32, shape, axis)


def place():
    slab = lax.axis_index("slab")
    return slab // (ZS * CORES), lax.axis_index("ctrl"), (slab // CORES) % ZS, slab % CORES


def device(x, y, z, core):
    return {"slab": (x % XS * ZS + z % ZS) * CORES + core, "ctrl": y % YS}


def is_heavy():
    slab = lax.axis_index("slab")
    return jnp.logical_and(slab >= 48, slab < 80)


def heavy_x(z):
    return 2 - z // 8


def gather_kernel(packed, pressure, area, center, nodes, ids, buf, more_nodes, more_ids, own, send, recv):
    x, y, z, core = place()
    group = core * YS + y
    plane = [(i * core, i * (1 - core)) for i in range(1, 4)]
    turned = [(i * (1 - core), i * core) for i in range(1, 4)]

    barrier = pltpu.get_barrier_semaphore()
    greet = [device(x, y, z + d, core) for d in (1, -1, 2, -2, 3, -3, 4, -4)]
    greet += [device(x + dx, y + dy, z, core) for dx, dy in plane + turned]
    greet += [device(x, y, z, 1 - core)]
    for target in greet:
        pl.semaphore_signal(barrier, inc=1, device_id=target, device_id_type=MESH)

    force = jnp.zeros((3, 128), F32)
    moment = jnp.zeros((3, 128), F32)
    for i in range(pressure.shape[1] // 128):
        at = pl.ds(i * 128, 128)
        pushed = area[:, at] * pressure[:, at]
        c = center[:, at]
        force = force + pushed
        moment = moment + jnp.concatenate(
            [
                c[1:2] * pushed[2:3] - c[2:3] * pushed[1:2],
                c[2:3] * pushed[0:1] - c[0:1] * pushed[2:3],
                c[0:1] * pushed[1:2] - c[1:2] * pushed[0:1],
            ],
            axis=0,
        )
    sums = jnp.sum(jnp.concatenate([force, moment], axis=0), axis=1, keepdims=True)
    lane = iota((6, 128), 1)
    row = iota((6, 128), 0)
    loads = jnp.sum(jnp.where(lane == row + LOAD_LANE, sums, 0.0), axis=0, keepdims=True)
    own[0] = packed[0]
    own[1] = packed[1]
    own[2] = packed[2] + loads
    for r in range(3):
        buf[x, z, r, group] = own[r]

    pl.semaphore_wait(barrier, len(greet))

    heavy = is_heavy()

    def hand(h, src_plane):
        target = device(heavy_x(z) + 1 + h, y, z, core)
        parts = []
        for i, (src, dst) in enumerate(
            ((nodes.at[:, pl.ds(src_plane, 2)], more_nodes), (ids.at[pl.ds(src_plane, 2)], more_ids))
        ):
            parts.append(
                pltpu.make_async_remote_copy(
                    src_ref=src,
                    dst_ref=dst,
                    send_sem=send.at[22 + 2 * h + i],
                    recv_sem=recv.at[22 + i],
                    device_id=target,
                    device_id_type=MESH,
                )
            )
        return parts

    pending = []

    def put(src, dst, slot, target):
        copy = pltpu.make_async_remote_copy(
            src_ref=src,
            dst_ref=dst,
            send_sem=send.at[slot],
            recv_sem=recv.at[slot],
            device_id=target,
            device_id_type=MESH,
        )
        copy.start()
        pending.append(copy)
        return copy

    def block(zz):
        return buf.at[x, zz % ZS, :, group]

    near = {}
    for d in (4, 3, 2, 1):
        near[d] = put(own, block(z), d - 1, device(x, y, z + d, core))
        near[-d] = put(own, block(z), d + 3, device(x, y, z - d, core))

    @pl.when(heavy)
    def _():
        more_nodes[...] = jnp.zeros(more_nodes.shape, F32)
        more_ids[...] = jnp.zeros(more_ids.shape, jnp.int32)
        for h in range(3):
            for copy in hand(h, 1 + 2 * h):
                copy.start()

    far = []
    for d in (1, 2, 3, 4):
        near[d].wait_recv()
        far.append(put(block(z - d), block(z - d), d + 7, device(x, y, z + 4, core)))
        near[-d].wait_recv()
        if d < 4:
            far.append(put(block(z + d), block(z + d), d + 11, device(x, y, z - 4, core)))
    for copy in far:
        copy.wait_recv()

    first = [
        put(buf.at[x, :, :, group], buf.at[x, :, :, group], 15 + i, device(x + dx, y + dy, z, core))
        for i, (dx, dy) in enumerate(plane)
    ]
    for copy in first:
        copy.wait_recv()

    def cross(i, dx, dy, start):
        target = device(x + dx, y + dy, z, core)

        def make(ref):
            return pltpu.make_async_remote_copy(
                src_ref=ref,
                dst_ref=ref,
                send_sem=send.at[18 + i],
                recv_sem=recv.at[18 + i],
                device_id=target,
                device_id_type=MESH,
            )

        @pl.when(core == 0)
        def _():
            copy = make(buf.at[x, :, :, pl.ds(0, YS)])
            copy.start() if start else copy.wait()

        @pl.when(core == 1)
        def _():
            copy = make(buf.at[:, :, :, group])
            copy.start() if start else copy.wait()

    for i, (dx, dy) in enumerate(turned):
        cross(i, dx, dy, True)
    for i, (dx, dy) in enumerate(turned):
        cross(i, dx, dy, False)

    half = buf.at[:, :, :, pl.ds(core * YS, YS)]
    put(half, half, 21, device(x, y, z, 1 - core)).wait_recv()
    for copy in pending:
        copy.wait_send()

    @pl.when(heavy)
    def _():
        for h in range(3):
            for copy in hand(h, 1 + 2 * h):
                copy.wait_send()

    @pl.when(jnp.logical_not(heavy))
    def _():
        for copy in hand(0, 1):
            copy.wait_recv()


def gather(packed, pressure, area, center, nodes, ids):
    vmem = pl.BlockSpec(memory_space=pltpu.VMEM)
    return pl.pallas_call(
        gather_kernel,
        out_shape=(
            jax.ShapeDtypeStruct((XS, ZS, 3, 8, 1, 128), F32),
            jax.ShapeDtypeStruct((3, 2, 8, 128), F32),
            jax.ShapeDtypeStruct((2, 8, 16), jnp.int32),
        ),
        in_specs=[vmem] * 6,
        out_specs=(vmem, vmem, vmem),
        scratch_shapes=[
            pltpu.VMEM((3, 1, 128), F32),
            pltpu.SemaphoreType.DMA((28,)),
            pltpu.SemaphoreType.DMA((24,)),
        ],
        compiler_params=pltpu.CompilerParams(collective_id=0, has_side_effects=True),
        name="gather",
    )(packed, pressure, area, center, nodes, ids)


def split3(value):
    hi = value.astype(BF16).astype(F32)
    rest = value - hi
    mid = rest.astype(BF16).astype(F32)
    return hi, mid, rest - mid


def regroup(v):
    sub = iota((8, 128), 0)
    grp = iota((8, 128), 1) // 16
    for bit in (1, 2, 4):
        below = pltpu.roll(pltpu.roll(v, 8 - bit, 0), 16 * bit, 1)
        above = pltpu.roll(pltpu.roll(v, bit, 0), 128 - 16 * bit, 1) if bit < 4 else below
        low = (sub & bit) == 0
        same = low == ((grp & bit) == 0)
        v = jnp.where(same, v, jnp.where(low, below, above))
    return v


def node_rows(nodes, p, r):
    sub = iota((8, 128), 0)
    x = [nodes[c, p, pl.ds(r, 1), :] for c in range(3)]
    square = x[0] * x[0] + x[1] * x[1] + x[2] * x[2]
    rows = jnp.where((sub == 0) | (sub == 3), -2.0 * x[0], 0.0)
    rows = jnp.where((sub == 1) | (sub == 4), -2.0 * x[1], rows)
    rows = jnp.where((sub == 2) | (sub == 5), -2.0 * x[2], rows)
    rows = jnp.where(sub == 7, square, rows)
    hi, mid, lo = split3(rows)
    one = sub == 6
    second = (sub >= 3) & (sub < 6)
    parts = [
        jnp.where(one, 1.0, jnp.where(second, mid, hi)),
        jnp.where(one, 1.0, jnp.where(sub < 3, hi, mid)),
        jnp.where(one, 1.0, jnp.where(second, hi, lo)),
        jnp.zeros((8, 128), F32),
    ]
    return jnp.concatenate(parts, axis=0).astype(BF16)


def control_rows(p):
    sub = iota((8, 128), 0)
    p = jnp.where(sub < 3, p, 0.0)
    square = jnp.sum(p * p, axis=0, keepdims=True)
    rows = p + pltpu.roll(p, 3, 0) + jnp.where(sub == 6, square, 0.0)
    hi, mid, lo = split3(rows)
    one = sub == 7
    parts = [
        jnp.where(one, 1.0, hi),
        jnp.where(one, 1.0, mid),
        jnp.where(one, 1.0, jnp.where(sub < 3, hi, lo)),
        jnp.zeros((8, 128), F32),
    ]
    return parts


BLOCK = 32


def pair_kernel(
    role,
    ids,
    more_ids,
    counts,
    motion,
    inverse_mass,
    raw,
    nodes,
    more_nodes,
    shift,
    more_shift,
    plane_edge,
    row_edge,
    state,
    feats,
    left_a,
    left_b,
    mix_a,
    mix_b,
    right,
    sums,
    tile_of,
    line_of,
):
    lines = LINES + MORE
    heavy = role[0] == 1
    sub = iota((8, 128), 0)

    def unpack(t, carry):
        total, n = carry
        v = [regroup(raw[t, r]) for r in range(3)]
        for r in range(3):
            feats[t, pl.ds(8 * r, 8), :] = v[r]
        i = t // 2
        kept = jnp.minimum(jnp.where(i < 8, i, jnp.where(i < 15, (i - 7) * 8, i + 42)), LINES - 1)
        q = t // 4
        hp, hr = jnp.minimum(q // 7, 1), q % 7 + 1
        line1 = jnp.where(heavy, kept, t)
        line2 = jnp.where(heavy, kept, LINES + hp * 8 + hr)
        start1 = jnp.where(heavy, 8 * (t % 2), 0)
        keep = jnp.where(t < 44, 4, 0)
        for e in range(4):
            tile_of[n + e] = ids[line1 // 8, line1 % 8, start1 + e]
            line_of[n + e] = line1
        n = n + jnp.where(heavy, keep, counts[t // 8, t % 8])
        for e in range(4):
            tile_of[n + e] = jnp.where(heavy, ids[kept // 8, kept % 8, start1 + 4 + e], more_ids[hp, hr, 4 * (t % 4) + e])
            line_of[n + e] = line2
        n = n + jnp.where(heavy, keep, jnp.where(t < 56, 4, 0))
        return total + v[2], n

    total, n = lax.fori_loop(0, NTILE, unpack, (jnp.zeros((8, 128), F32), 0), unroll=4)
    for e in range(BLOCK):
        tile_of[n + e] = 0
        line_of[n + e] = lines
    total = jnp.broadcast_to(total[5:6, :], (8, 128))
    for by in (16, 32, 64):
        total = total + pltpu.roll(total, by, 1)
    rigid = []
    for k in range(6):
        load = jnp.broadcast_to(total[:, k : k + 1], (8, 128))
        acceleration = inverse_mass[k] * load + GRAVITY[k]
        state[k, :, :] = motion[k] + TIME_STEP * acceleration
        rigid.append((TIME_STEP * motion[k] + 0.5 * TIME_STEP * TIME_STEP * acceleration)[0:3])

    wide = iota((128, 64), 1) < 32

    def prepare(t, _):
        parts = control_rows(feats[t, 0:8, :])
        columns = jnp.transpose(jnp.concatenate(parts + parts, axis=0), (1, 0))
        left_a[t] = jnp.where(wide, columns, 0.0).astype(BF16)
        left_b[t] = jnp.where(wide, 0.0, columns).astype(BF16)
        c = jnp.zeros((3, 128), F32)
        for k in range(6):
            c = c + rigid[k] * feats[t, 3 + 3 * k : 6 + 3 * k, :]
        c = c * (1.0 / 256.0)
        c = jnp.concatenate([c, c, jnp.zeros((2, 128), F32)], axis=0)
        c_hi = c.astype(BF16).astype(F32)
        c = jnp.where(sub < 3, c_hi, c - c_hi)
        zero = jnp.zeros((8, 128), F32)
        mix_a[t] = jnp.concatenate([c, zero], axis=0).astype(BF16)
        mix_b[t] = jnp.concatenate([zero, c], axis=0).astype(BF16)
        right[t] = node_rows(nodes, t // 8, t % 8)
        sums[t] = zero
        return 0

    lax.fori_loop(0, NTILE, prepare, 0, unroll=4)

    def prepare_more(i, _):
        right[LINES + i] = node_rows(more_nodes, i // 8, i % 8)
        sums[LINES + i] = jnp.zeros((8, 128), F32)
        return 0

    lax.fori_loop(0, MORE, prepare_more, 0, unroll=4)
    right[lines] = jnp.zeros((32, 128), BF16)
    sums[lines] = jnp.zeros((8, 128), F32)

    gap = jnp.zeros((32, 128), BF16)

    def block(g, _):
        for u in range(0, BLOCK, 2):
            i = g * BLOCK + u
            t1, t2 = tile_of[i], tile_of[i + 1]
            l1, l2 = line_of[i], line_of[i + 1]
            rhs = jnp.concatenate(
                [jnp.concatenate([right[l1], gap], axis=1), jnp.concatenate([gap, right[l2]], axis=1)], axis=0
            )
            s = jnp.dot(left_a[t1] + left_b[t2], rhs, preferred_element_type=F32)
            s = jnp.minimum(jnp.maximum(s, 1e-30), 16.0)
            d = s * lax.rsqrt(s)
            v = 4.0 - d
            v = v * v
            k = v * v * (1.0 + d)
            hi = k.astype(BF16)
            lo = (k - hi.astype(F32)).astype(BF16)
            m = mix_a[t1] + mix_b[t2]
            out = jnp.dot(
                jnp.concatenate([m, m], axis=1), jnp.concatenate([hi, lo], axis=0), preferred_element_type=F32
            )
            sums[l1] += out[0:8, 0:128]
            sums[l2] += out[8:16, 128:256]
        return 0

    lax.fori_loop(0, (n + BLOCK - 1) // BLOCK, block, 0)

    def finish(i, _):
        v = sums[i]
        v = v + pltpu.roll(v, 5, 0)
        for c in range(3):
            shift[c, i // 8, pl.ds(i % 8, 1), :] = v[c : c + 1, :]
        return 0

    lax.fori_loop(0, LINES, finish, 0, unroll=8)

    def finish_more(i, _):
        v = sums[LINES + i]
        v = v + pltpu.roll(v, 5, 0)
        for c in range(3):
            more_shift[c, i // 8, pl.ds(i % 8, 1), :] = v[c : c + 1, :]
        return 0

    lax.fori_loop(0, MORE, finish_more, 0, unroll=8)
    for c in range(3):
        plane_edge[0, c] = nodes[c, 0]
        plane_edge[1, c] = nodes[c, 0] + shift[c, 0]
        for p in range(8):
            row_edge[0, c, p : p + 1, :] = nodes[c, p, 0:1, :]
            row_edge[1, c, p : p + 1, :] = nodes[c, p, 0:1, :] + shift[c, p, 0:1, :]


LINES = 64
MORE = 16


def pair_sums(role, ids, more_ids, counts, motion, inverse_mass, raw, nodes, more_nodes):
    vmem = pl.BlockSpec(memory_space=pltpu.VMEM)
    smem = pl.BlockSpec(memory_space=pltpu.SMEM)
    lines = LINES + MORE
    units = 4 * LINES + 14 * 16 + 2 * BLOCK
    return pl.pallas_call(
        pair_kernel,
        out_shape=(
            jax.ShapeDtypeStruct((3, 8, 8, 128), F32),
            jax.ShapeDtypeStruct((3, 2, 8, 128), F32),
            jax.ShapeDtypeStruct((2, 3, 8, 128), F32),
            jax.ShapeDtypeStruct((2, 3, 8, 128), F32),
            jax.ShapeDtypeStruct((6, 8, 128), F32),
        ),
        in_specs=[smem] * 6 + [vmem] * 3,
        out_specs=(vmem,) * 5,
        scratch_shapes=[
            pltpu.VMEM((NTILE, 24, 128), F32),
            pltpu.VMEM((NTILE, 128, 64), BF16),
            pltpu.VMEM((NTILE, 128, 64), BF16),
            pltpu.VMEM((NTILE, 16, 128), BF16),
            pltpu.VMEM((NTILE, 16, 128), BF16),
            pltpu.VMEM((lines + 1, 32, 128), BF16),
            pltpu.VMEM((lines + 1, 8, 128), F32),
            pltpu.SMEM((units,), jnp.int32),
            pltpu.SMEM((units,), jnp.int32),
        ],
        name="pairs",
    )(role, ids, more_ids, counts, motion, inverse_mass, raw, nodes, more_nodes)


def volume_kernel(
    nodes, shift, more_shift, plane_edge, row_edge, out_shift, volume, change, back, planes, rows, corners, send, recv
):
    x, y, z, core = place()
    slab = lax.axis_index("slab")
    heavy = is_heavy()
    last = XS * ZS * CORES

    def at(ds, dy):
        return {"slab": (slab + ds + last) % last, "ctrl": (y + dy + YS) % YS}

    barrier = pltpu.get_barrier_semaphore()
    greet = [at(1, 0), at(-1, 0), at(0, 1), at(0, -1), at(1, 1), at(-1, -1)]
    greet += [device(x + i, y, z, core) for i in (1, 2, 3)]
    for target in greet:
        pl.semaphore_signal(barrier, inc=1, device_id=target, device_id_type=MESH)
    pl.semaphore_wait(barrier, len(greet))

    def put(src, dst, slot, target):
        return pltpu.make_async_remote_copy(
            src_ref=src,
            dst_ref=dst,
            send_sem=send.at[slot],
            recv_sem=recv.at[slot],
            device_id=target,
            device_id_type=MESH,
        )

    def give(h):
        return pltpu.make_async_remote_copy(
            src_ref=more_shift,
            dst_ref=back.at[h],
            send_sem=send.at[3],
            recv_sem=recv.at[3 + h],
            device_id=device(heavy_x(z), y, z, core),
            device_id_type=MESH,
        )

    mine = (x - heavy_x(z) + 3) % XS

    @pl.when(jnp.logical_not(heavy))
    def _():
        give(jnp.minimum(mine, 2)).start()

    edges = [
        put(plane_edge, corners, 2, at(-1, -1)),
        put(plane_edge, planes, 0, at(-1, 0)),
        put(row_edge, rows, 1, at(0, -1)),
    ]
    for copy in edges:
        copy.start()
    out_shift[...] = shift[...]

    @pl.when(heavy)
    def _():
        row = iota((8, 128), 0)
        for h in range(3):
            give(h).wait_recv()
            for c in range(3):
                for i in range(2):
                    p = 1 + 2 * h + i
                    out_shift[c, p] = jnp.where(row == 0, shift[c, p], back[h, c, i])

    @pl.when(jnp.logical_not(heavy))
    def _():
        give(jnp.minimum(mine, 2)).wait_send()

    for copy in edges:
        copy.wait()

    bottom = iota((8, 128), 0) == 7

    def faces(field, c, p):
        if p < 8:
            a = nodes[c, p]
            if field:
                a = a + out_shift[c, p]
            edge = rows[field, c, p : p + 1, :]
        else:
            a = planes[field, c]
            edge = corners[field, c, 0:1, :]
        b = jnp.where(bottom, edge, pltpu.roll(a, 7, 0))
        az = pltpu.roll(a, 127, 1)
        bz = pltpu.roll(b, 127, 1)
        near, far = a + b, az + bz
        return near + far, (b + bz) - (a + az), far - near

    row = iota((8, 128), 0) + y * 8
    inside = jnp.logical_and(row < 31, iota((8, 128), 1) < 127)
    held = {}
    for p in range(9):
        for field in range(2):
            for c in range(3):
                held[field, c, p % 2] = faces(field, c, p)
        if p == 0:
            continue
        both = []
        for field in range(2):
            now = [held[field, c, p % 2] for c in range(3)]
            before = [held[field, c, (p - 1) % 2] for c in range(3)]
            ex = [0.25 * (n[0] - b[0]) for n, b in zip(now, before)]
            ey = [0.25 * (n[1] + b[1]) for n, b in zip(now, before)]
            ez = [0.25 * (n[2] + b[2]) for n, b in zip(now, before)]
            both.append(
                ex[0] * (ey[1] * ez[2] - ey[2] * ez[1])
                + ex[1] * (ey[2] * ez[0] - ey[0] * ez[2])
                + ex[2] * (ey[0] * ez[1] - ey[1] * ez[0])
            )
        ok = jnp.logical_and(inside, slab * 8 + p - 1 < 1023)
        old, new = (jnp.where(ok, v, 0.0) for v in both)
        volume[p - 1] = new
        change[p - 1] = new - old


def volumes(nodes, shift, more_shift, plane_edge, row_edge):
    vmem = pl.BlockSpec(memory_space=pltpu.VMEM)
    edge = pltpu.VMEM((2, 3, 8, 128), F32)
    return pl.pallas_call(
        volume_kernel,
        out_shape=(
            jax.ShapeDtypeStruct((3, 8, 8, 128), F32),
            jax.ShapeDtypeStruct((8, 8, 128), F32),
            jax.ShapeDtypeStruct((8, 8, 128), F32),
        ),
        in_specs=[vmem] * 5,
        out_specs=(vmem,) * 3,
        scratch_shapes=[
            pltpu.VMEM((3, 3, 2, 8, 128), F32),
            edge,
            edge,
            edge,
            pltpu.SemaphoreType.DMA((4,)),
            pltpu.SemaphoreType.DMA((6,)),
        ],
        compiler_params=pltpu.CompilerParams(collective_id=1, has_side_effects=True),
        name="volumes",
    )(nodes, shift, more_shift, plane_edge, row_edge)


def local(
    face_pressure,
    face_area,
    face_center,
    motion,
    inverse_mass,
    control_points,
    control_modes,
    node_points,
    tile_list,
    tile_count,
):
    packed = jnp.concatenate([control_points, control_modes, jnp.zeros((3, 16), F32)], axis=0).reshape(3, 1, 128)
    raw, more_nodes, more_ids = gather(
        packed, face_pressure.reshape(1, -1), face_area, face_center, node_points, tile_list
    )
    role = is_heavy().astype(jnp.int32).reshape(1)
    shift, more_shift, plane_edge, row_edge, state = pair_sums(
        role,
        tile_list,
        more_ids,
        tile_count,
        motion,
        inverse_mass,
        raw.reshape(NTILE, 3, 8, 128),
        node_points,
        more_nodes,
    )
    node_shift, volume, change = volumes(node_points, shift, more_shift, plane_edge, row_edge)
    return node_shift, volume, change, state[:, 0, 0]


def solution(mesh):
    placed = (
        P(("slab", "ctrl")),
        P(None, ("slab", "ctrl")),
        P(None, ("slab", "ctrl")),
        P(),
        P(),
        P(None, ("slab", "ctrl")),
        P(None, ("slab", "ctrl")),
        P(None, "slab", "ctrl", None),
        P("slab", "ctrl", None),
        P("slab", "ctrl"),
    )
    return jax.shard_map(
        local,
        mesh=mesh,
        in_specs=placed,
        out_specs=(
            P(None, "slab", "ctrl", None),
            P("slab", "ctrl", None),
            P("slab", "ctrl", None),
            P(),
        ),
        check_vma=False,
    )
```

```python
import functools

import jax
import jax.numpy as jnp
from jax import lax
from jax.experimental import pallas as pl
from jax.experimental.pallas import tpu as pltpu
from jax.sharding import PartitionSpec as P

MESH = pl.DeviceIdType.MESH
TILE = 128
NTILE = 64
F32 = jnp.float32
BF16 = jnp.bfloat16
TIME_STEP = 0.5
GRAVITY = (0.0, 0.0, -0.5, 0.0, 0.0, 0.0)
XS, YS, ZS, CORES = 4, 4, 16, 2
LOAD_LANE = 80


def iota(shape, axis):
    return lax.broadcasted_iota(jnp.int32, shape, axis)


def place():
    slab = lax.axis_index("slab")
    return slab // (ZS * CORES), lax.axis_index("ctrl"), (slab // CORES) % ZS, slab % CORES


def device(x, y, z, core):
    return {"slab": (x % XS * ZS + z % ZS) * CORES + core, "ctrl": y % YS}


def is_heavy():
    slab = lax.axis_index("slab")
    return jnp.logical_and(slab >= 48, slab < 80)


def heavy_x(z):
    return 2 - z // 8


def gather_kernel(
    points,
    modes,
    pressure_hbm,
    area_hbm,
    center_hbm,
    nodes,
    ids,
    buf,
    more_nodes,
    more_ids,
    pressure,
    area,
    center,
    pack,
    own,
    fetch,
    send,
    recv,
):
    x, y, z, core = place()
    group = core * YS + y
    plane = [(i * core, i * (1 - core)) for i in range(1, 4)]
    turned = [(i * (1 - core), i * core) for i in range(1, 4)]

    barrier = pltpu.get_barrier_semaphore()
    greet = [device(x, y, z + d, core) for d in (1, -1, 2, -2, 3, -3, 4, -4)]
    greet += [device(x + dx, y + dy, z, core) for dx, dy in plane + turned]
    greet += [device(x, y, z, 1 - core)]
    for target in greet:
        pl.semaphore_signal(barrier, inc=1, device_id=target, device_id_type=MESH)

    fetches = [
        pltpu.make_async_copy(src, dst, fetch.at[i])
        for i, (src, dst) in enumerate(((pressure_hbm, pressure), (area_hbm, area), (center_hbm, center)))
    ]
    for copy in fetches:
        copy.start()

    pack[...] = jnp.zeros((24, 128), F32)
    pack[0:3, 0:16] = points[...]
    pack[3:21, 0:16] = modes[...]
    packed = []
    for r in range(3):
        v = pack[8 * r : 8 * r + 8, :]
        for bit in (1, 2, 4):
            v = jnp.where((iota((8, 128), 0) & bit) == 0, v, pltpu.roll(v, 16 * bit, 1))
        packed.append(jnp.sum(v, axis=0, keepdims=True))

    for copy in fetches:
        copy.wait()
    force = jnp.zeros((3, 128), F32)
    moment = jnp.zeros((3, 128), F32)
    for i in range(pressure.shape[0]):
        at = pl.ds(i * 128, 128)
        pushed = area[:, at] * pressure[i : i + 1, :]
        c = center[:, at]
        force = force + pushed
        moment = moment + jnp.concatenate(
            [
                c[1:2] * pushed[2:3] - c[2:3] * pushed[1:2],
                c[2:3] * pushed[0:1] - c[0:1] * pushed[2:3],
                c[0:1] * pushed[1:2] - c[1:2] * pushed[0:1],
            ],
            axis=0,
        )
    sums = jnp.sum(jnp.concatenate([force, moment], axis=0), axis=1, keepdims=True)
    lane = iota((6, 128), 1)
    row = iota((6, 128), 0)
    loads = jnp.sum(jnp.where(lane == row + LOAD_LANE, sums, 0.0), axis=0, keepdims=True)
    own[0] = packed[0]
    own[1] = packed[1]
    own[2] = packed[2] + loads
    for r in range(3):
        buf[x, z, r, group] = own[r]

    pl.semaphore_wait(barrier, len(greet))

    heavy = is_heavy()

    def hand(h, src_plane):
        target = device(heavy_x(z) + 1 + h, y, z, core)
        parts = []
        for i, (src, dst) in enumerate(
            ((nodes.at[:, pl.ds(src_plane, 2)], more_nodes), (ids.at[pl.ds(src_plane, 2)], more_ids))
        ):
            parts.append(
                pltpu.make_async_remote_copy(
                    src_ref=src,
                    dst_ref=dst,
                    send_sem=send.at[22 + 2 * h + i],
                    recv_sem=recv.at[22 + i],
                    device_id=target,
                    device_id_type=MESH,
                )
            )
        return parts

    pending = []

    def put(src, dst, slot, target):
        copy = pltpu.make_async_remote_copy(
            src_ref=src,
            dst_ref=dst,
            send_sem=send.at[slot],
            recv_sem=recv.at[slot],
            device_id=target,
            device_id_type=MESH,
        )
        copy.start()
        pending.append(copy)
        return copy

    def block(zz):
        return buf.at[x, zz % ZS, :, group]

    near = {}
    for d in (4, 3, 2, 1):
        near[d] = put(own, block(z), d - 1, device(x, y, z + d, core))
        near[-d] = put(own, block(z), d + 3, device(x, y, z - d, core))

    @pl.when(heavy)
    def _():
        for h in range(3):
            for copy in hand(h, 1 + 2 * h):
                copy.start()

    far = []
    for d in (1, 2, 3, 4):
        near[d].wait_recv()
        far.append(put(block(z - d), block(z - d), d + 7, device(x, y, z + 4, core)))
        near[-d].wait_recv()
        if d < 4:
            far.append(put(block(z + d), block(z + d), d + 11, device(x, y, z - 4, core)))
    for copy in far:
        copy.wait_recv()

    first = [
        put(buf.at[x, :, :, group], buf.at[x, :, :, group], 15 + i, device(x + dx, y + dy, z, core))
        for i, (dx, dy) in enumerate(plane)
    ]
    for copy in first:
        copy.wait_recv()

    def cross(i, dx, dy, start):
        target = device(x + dx, y + dy, z, core)

        def make(ref):
            return pltpu.make_async_remote_copy(
                src_ref=ref,
                dst_ref=ref,
                send_sem=send.at[18 + i],
                recv_sem=recv.at[18 + i],
                device_id=target,
                device_id_type=MESH,
            )

        @pl.when(core == 0)
        def _():
            copy = make(buf.at[x, :, :, pl.ds(0, YS)])
            copy.start() if start else copy.wait()

        @pl.when(core == 1)
        def _():
            copy = make(buf.at[:, :, :, group])
            copy.start() if start else copy.wait()

    for i, (dx, dy) in enumerate(turned):
        cross(i, dx, dy, True)
    for i, (dx, dy) in enumerate(turned):
        cross(i, dx, dy, False)

    half = buf.at[:, :, :, pl.ds(core * YS, YS)]
    put(half, half, 21, device(x, y, z, 1 - core)).wait_recv()
    for copy in pending:
        copy.wait_send()

    @pl.when(heavy)
    def _():
        for h in range(3):
            for copy in hand(h, 1 + 2 * h):
                copy.wait_send()

    @pl.when(jnp.logical_not(heavy))
    def _():
        for copy in hand(0, 1):
            copy.wait_recv()


def gather(points, modes, pressure, area, center, nodes, ids):
    vmem = pl.BlockSpec(memory_space=pltpu.VMEM)
    hbm = pl.BlockSpec(memory_space=pl.ANY)
    return pl.pallas_call(
        gather_kernel,
        out_shape=(
            jax.ShapeDtypeStruct((XS, ZS, 3, 8, 1, 128), F32),
            jax.ShapeDtypeStruct((3, 2, 8, 128), F32),
            jax.ShapeDtypeStruct((2, 8, 16), jnp.int32),
        ),
        in_specs=[vmem, vmem] + [hbm] * 5,
        out_specs=(vmem, hbm, hbm),
        scratch_shapes=[
            pltpu.VMEM(pressure.shape, F32),
            pltpu.VMEM(area.shape, F32),
            pltpu.VMEM(center.shape, F32),
            pltpu.VMEM((24, 128), F32),
            pltpu.VMEM((3, 1, 128), F32),
            pltpu.SemaphoreType.DMA((3,)),
            pltpu.SemaphoreType.DMA((28,)),
            pltpu.SemaphoreType.DMA((24,)),
        ],
        compiler_params=pltpu.CompilerParams(
            collective_id=0, has_side_effects=True, vmem_limit_bytes=VMEM_LIMIT
        ),
        name="gather",
    )(points, modes, pressure, area, center, nodes, ids)


VMEM_LIMIT = 24 << 20


def split3(value):
    hi = value.astype(BF16).astype(F32)
    rest = value - hi
    mid = rest.astype(BF16).astype(F32)
    return hi, mid, rest - mid


def regroup(v):
    sub = iota((8, 128), 0)
    grp = iota((8, 128), 1) // 16
    for bit in (1, 2, 4):
        below = pltpu.roll(pltpu.roll(v, 8 - bit, 0), 16 * bit, 1)
        above = pltpu.roll(pltpu.roll(v, bit, 0), 128 - 16 * bit, 1) if bit < 4 else below
        low = (sub & bit) == 0
        same = low == ((grp & bit) == 0)
        v = jnp.where(same, v, jnp.where(low, below, above))
    return v


def node_rows(nodes, p, r):
    sub = iota((8, 128), 0)
    x = [nodes[c, p, pl.ds(r, 1), :] for c in range(3)]
    square = x[0] * x[0] + x[1] * x[1] + x[2] * x[2]
    rows = jnp.where((sub == 0) | (sub == 3), -2.0 * x[0], 0.0)
    rows = jnp.where((sub == 1) | (sub == 4), -2.0 * x[1], rows)
    rows = jnp.where((sub == 2) | (sub == 5), -2.0 * x[2], rows)
    rows = jnp.where(sub == 7, square, rows)
    hi, mid, lo = split3(rows)
    one = sub == 6
    second = (sub >= 3) & (sub < 6)
    parts = [
        jnp.where(one, 1.0, jnp.where(second, mid, hi)),
        jnp.where(one, 1.0, jnp.where(sub < 3, hi, mid)),
        jnp.where(one, 1.0, jnp.where(second, hi, lo)),
        jnp.zeros((8, 128), F32),
    ]
    return jnp.concatenate(parts, axis=0).astype(BF16)


def control_rows(p):
    sub = iota((8, 128), 0)
    p = jnp.where(sub < 3, p, 0.0)
    square = jnp.sum(p * p, axis=0, keepdims=True)
    rows = p + pltpu.roll(p, 3, 0) + jnp.where(sub == 6, square, 0.0)
    hi, mid, lo = split3(rows)
    one = sub == 7
    parts = [
        jnp.where(one, 1.0, hi),
        jnp.where(one, 1.0, mid),
        jnp.where(one, 1.0, jnp.where(sub < 3, hi, lo)),
        jnp.zeros((8, 128), F32),
    ]
    return parts


BLOCK = 32


def pair_kernel(
    role,
    ids,
    more_ids,
    counts,
    motion,
    inverse_mass,
    raw,
    nodes,
    more_nodes,
    shift,
    more_shift,
    plane_edge,
    row_edge,
    state,
    feats,
    left_a,
    left_b,
    mix_a,
    mix_b,
    right,
    sums,
    unit_of,
):
    lines = LINES + MORE
    heavy = role[0] == 1
    sub = iota((8, 128), 0)

    def unpack(t, carry):
        total, n = carry
        v = [regroup(raw[t, r]) for r in range(3)]
        for r in range(3):
            feats[t, pl.ds(8 * r, 8), :] = v[r]
        i = t // 2
        kept = jnp.minimum(jnp.where(i < 8, i, jnp.where(i < 15, (i - 7) * 8, i + 42)), LINES - 1)
        q = t // 4
        hp, hr = jnp.minimum(q // 7, 1), q % 7 + 1
        line1 = jnp.where(heavy, kept, t)
        line2 = jnp.where(heavy, kept, LINES + hp * 8 + hr)
        start1 = jnp.where(heavy, 8 * (t % 2), 0)
        keep = jnp.where(t < 44, 4, 0)
        code1, code2 = line1 * NTILE, line2 * NTILE
        for e in range(4):
            unit_of[n + e] = code1 + ids[line1, start1 + e]
        n = n + jnp.where(heavy, keep, counts[t // 8, t % 8])
        quarter = 4 * (t % 4)
        more_line = hp * 8 + hr
        for e in range(4):
            unit_of[n + e] = code2 + jnp.where(heavy, ids[kept, start1 + 4 + e], more_ids[more_line, quarter + e])
        n = n + jnp.where(heavy, keep, jnp.where(t < 56, 4, 0))
        return total + v[2], n

    total, n = lax.fori_loop(0, NTILE, unpack, (jnp.zeros((8, 128), F32), 0), unroll=4)
    for e in range(BLOCK):
        unit_of[n + e] = lines * NTILE
    total = jnp.broadcast_to(total[5:6, :], (8, 128))
    for by in (16, 32, 64):
        total = total + pltpu.roll(total, by, 1)
    rigid = []
    for k in range(6):
        load = jnp.broadcast_to(total[:, k : k + 1], (8, 128))
        acceleration = inverse_mass[k] * load + GRAVITY[k]
        state[k] = (motion[k] + TIME_STEP * acceleration)[0, 0]
        rigid.append((TIME_STEP * motion[k] + 0.5 * TIME_STEP * TIME_STEP * acceleration)[0:3])

    wide = iota((128, 64), 1) < 32

    def prepare(t, _):
        parts = control_rows(feats[t, 0:8, :])
        columns = jnp.transpose(jnp.concatenate(parts + parts, axis=0), (1, 0))
        left_a[t] = jnp.where(wide, columns, 0.0).astype(BF16)
        left_b[t] = jnp.where(wide, 0.0, columns).astype(BF16)
        c = jnp.zeros((3, 128), F32)
        for k in range(6):
            c = c + rigid[k] * feats[t, 3 + 3 * k : 6 + 3 * k, :]
        c = c * (1.0 / 256.0)
        c = jnp.concatenate([c, c, jnp.zeros((2, 128), F32)], axis=0)
        c_hi = c.astype(BF16).astype(F32)
        c = jnp.where(sub < 3, c_hi, c - c_hi)
        zero = jnp.zeros((8, 128), F32)
        mix_a[t] = jnp.concatenate([c, zero], axis=0).astype(BF16)
        mix_b[t] = jnp.concatenate([zero, c], axis=0).astype(BF16)
        right[t] = node_rows(nodes, t // 8, t % 8)
        sums[t] = zero
        return 0

    lax.fori_loop(0, NTILE, prepare, 0, unroll=4)

    def prepare_more(i, _):
        right[LINES + i] = node_rows(more_nodes, i // 8, i % 8)
        sums[LINES + i] = jnp.zeros((8, 128), F32)
        return 0

    lax.fori_loop(0, MORE, prepare_more, 0, unroll=4)
    right[lines] = jnp.zeros((32, 128), BF16)
    sums[lines] = jnp.zeros((8, 128), F32)

    gap = jnp.zeros((32, 128), BF16)

    def block(g, _):
        for u in range(0, BLOCK, 2):
            i = g * BLOCK + u
            t1, t2 = unit_of[i] % NTILE, unit_of[i + 1] % NTILE
            l1, l2 = unit_of[i] // NTILE, unit_of[i + 1] // NTILE
            rhs = jnp.concatenate(
                [jnp.concatenate([right[l1], gap], axis=1), jnp.concatenate([gap, right[l2]], axis=1)], axis=0
            )
            s = jnp.dot(left_a[t1] + left_b[t2], rhs, preferred_element_type=F32)
            s = jnp.minimum(jnp.maximum(s, 1e-30), 16.0)
            d = s * lax.rsqrt(s)
            v = 4.0 - d
            v = v * v
            k = v * v * (1.0 + d)
            hi = k.astype(BF16)
            lo = (k - hi.astype(F32)).astype(BF16)
            m = mix_a[t1] + mix_b[t2]
            out = jnp.dot(
                jnp.concatenate([m, m], axis=1), jnp.concatenate([hi, lo], axis=0), preferred_element_type=F32
            )
            sums[l1] += out[0:8, 0:128]
            sums[l2] += out[8:16, 128:256]
        return 0

    lax.fori_loop(0, (n + BLOCK - 1) // BLOCK, block, 0)

    def finish(i, _):
        v = sums[i]
        v = v + pltpu.roll(v, 5, 0)
        for c in range(3):
            shift[c, i // 8, pl.ds(i % 8, 1), :] = v[c : c + 1, :]
        return 0

    lax.fori_loop(0, LINES, finish, 0, unroll=8)

    def finish_more(i, _):
        v = sums[LINES + i]
        v = v + pltpu.roll(v, 5, 0)
        for c in range(3):
            more_shift[c, i // 8, pl.ds(i % 8, 1), :] = v[c : c + 1, :]
        return 0

    lax.fori_loop(0, MORE, finish_more, 0, unroll=8)
    for c in range(3):
        plane_edge[0, c] = nodes[c, 0]
        plane_edge[1, c] = nodes[c, 0] + shift[c, 0]
        for p in range(8):
            row_edge[0, c, p : p + 1, :] = nodes[c, p, 0:1, :]
            row_edge[1, c, p : p + 1, :] = nodes[c, p, 0:1, :] + shift[c, p, 0:1, :]


LINES = 64
MORE = 16


def pair_sums(role, ids, more_ids, counts, motion, inverse_mass, raw, nodes, more_nodes):
    vmem = pl.BlockSpec(memory_space=pltpu.VMEM)
    smem = pl.BlockSpec(memory_space=pltpu.SMEM)
    lines = LINES + MORE
    units = 4 * LINES + 14 * 16 + 2 * BLOCK
    return pl.pallas_call(
        pair_kernel,
        out_shape=(
            jax.ShapeDtypeStruct((3, 8, 8, 128), F32),
            jax.ShapeDtypeStruct((3, 2, 8, 128), F32),
            jax.ShapeDtypeStruct((2, 3, 8, 128), F32),
            jax.ShapeDtypeStruct((2, 3, 8, 128), F32),
            jax.ShapeDtypeStruct((6,), F32),
        ),
        in_specs=[smem] * 6 + [vmem] * 3,
        out_specs=(vmem,) * 4 + (smem,),
        scratch_shapes=[
            pltpu.VMEM((NTILE, 24, 128), F32),
            pltpu.VMEM((NTILE, 128, 64), BF16),
            pltpu.VMEM((NTILE, 128, 64), BF16),
            pltpu.VMEM((NTILE, 16, 128), BF16),
            pltpu.VMEM((NTILE, 16, 128), BF16),
            pltpu.VMEM((lines + 1, 32, 128), BF16),
            pltpu.VMEM((lines + 1, 8, 128), F32),
            pltpu.SMEM((units,), jnp.int32),
        ],
        compiler_params=pltpu.CompilerParams(vmem_limit_bytes=VMEM_LIMIT),
        name="pairs",
    )(role, ids, more_ids, counts, motion, inverse_mass, raw, nodes, more_nodes)


def exchange_kernel(more_shift, plane_edge, row_edge, back, planes, rows, corners, send, recv):
    x, y, z, core = place()
    slab = lax.axis_index("slab")
    heavy = is_heavy()
    last = XS * ZS * CORES

    def at(ds, dy):
        return {"slab": (slab + ds + last) % last, "ctrl": (y + dy + YS) % YS}

    barrier = pltpu.get_barrier_semaphore()
    greet = [at(1, 0), at(-1, 0), at(0, 1), at(0, -1), at(1, 1), at(-1, -1)]
    greet += [device(x + i, y, z, core) for i in (1, 2, 3)]
    for target in greet:
        pl.semaphore_signal(barrier, inc=1, device_id=target, device_id_type=MESH)
    pl.semaphore_wait(barrier, len(greet))

    def put(src, dst, slot, target):
        return pltpu.make_async_remote_copy(
            src_ref=src,
            dst_ref=dst,
            send_sem=send.at[slot],
            recv_sem=recv.at[slot],
            device_id=target,
            device_id_type=MESH,
        )

    def give(h):
        return pltpu.make_async_remote_copy(
            src_ref=more_shift,
            dst_ref=back.at[h],
            send_sem=send.at[3],
            recv_sem=recv.at[3 + h],
            device_id=device(heavy_x(z), y, z, core),
            device_id_type=MESH,
        )

    mine = (x - heavy_x(z) + 3) % XS

    @pl.when(jnp.logical_not(heavy))
    def _():
        give(jnp.minimum(mine, 2)).start()

    edges = [
        put(plane_edge, corners, 2, at(-1, -1)),
        put(plane_edge, planes, 0, at(-1, 0)),
        put(row_edge, rows, 1, at(0, -1)),
    ]
    for copy in edges:
        copy.start()

    @pl.when(heavy)
    def _():
        for h in range(3):
            give(h).wait_recv()

    @pl.when(jnp.logical_not(heavy))
    def _():
        give(jnp.minimum(mine, 2)).wait_send()

    for copy in edges:
        copy.wait()


def exchange(more_shift, plane_edge, row_edge):
    hbm = pl.BlockSpec(memory_space=pl.ANY)
    edge = jax.ShapeDtypeStruct((2, 3, 8, 128), F32)
    return pl.pallas_call(
        exchange_kernel,
        out_shape=(jax.ShapeDtypeStruct((3, 3, 2, 8, 128), F32), edge, edge, edge),
        in_specs=[hbm] * 3,
        out_specs=(hbm,) * 4,
        scratch_shapes=[pltpu.SemaphoreType.DMA((4,)), pltpu.SemaphoreType.DMA((6,))],
        compiler_params=pltpu.CompilerParams(
            collective_id=1, has_side_effects=True, vmem_limit_bytes=VMEM_LIMIT
        ),
        name="exchange",
    )(more_shift, plane_edge, row_edge)


def volume_kernel(role, nodes, shift, back, planes, rows, corners, out_shift, volume, change):
    slab, y = role[1], role[2]
    out_shift[...] = shift[...]

    @pl.when(role[0] == 1)
    def _():
        row = iota((8, 128), 0)
        for h in range(3):
            for c in range(3):
                for i in range(2):
                    p = 1 + 2 * h + i
                    out_shift[c, p] = jnp.where(row == 0, shift[c, p], back[h, c, i])

    bottom = iota((8, 128), 0) == 7

    def faces(field, c, p):
        if p < 8:
            a = nodes[c, p]
            if field:
                a = a + out_shift[c, p]
            edge = rows[field, c, p : p + 1, :]
        else:
            a = planes[field, c]
            edge = corners[field, c, 0:1, :]
        b = jnp.where(bottom, edge, pltpu.roll(a, 7, 0))
        az = pltpu.roll(a, 127, 1)
        bz = pltpu.roll(b, 127, 1)
        near, far = a + b, az + bz
        return near + far, (b + bz) - (a + az), far - near

    row = iota((8, 128), 0) + y * 8
    inside = jnp.logical_and(row < 31, iota((8, 128), 1) < 127)
    held = {}
    for p in range(9):
        for field in range(2):
            for c in range(3):
                held[field, c, p % 2] = faces(field, c, p)
        if p == 0:
            continue
        both = []
        for field in range(2):
            now = [held[field, c, p % 2] for c in range(3)]
            before = [held[field, c, (p - 1) % 2] for c in range(3)]
            ex = [0.25 * (n[0] - b[0]) for n, b in zip(now, before)]
            ey = [0.25 * (n[1] + b[1]) for n, b in zip(now, before)]
            ez = [0.25 * (n[2] + b[2]) for n, b in zip(now, before)]
            both.append(
                ex[0] * (ey[1] * ez[2] - ey[2] * ez[1])
                + ex[1] * (ey[2] * ez[0] - ey[0] * ez[2])
                + ex[2] * (ey[0] * ez[1] - ey[1] * ez[0])
            )
        ok = jnp.logical_and(inside, slab * 8 + p - 1 < 1023)
        old, new = (jnp.where(ok, v, 0.0) for v in both)
        volume[p - 1] = new
        change[p - 1] = new - old


def volumes(role, nodes, shift, back, planes, rows, corners):
    vmem = pl.BlockSpec(memory_space=pltpu.VMEM)
    return pl.pallas_call(
        volume_kernel,
        out_shape=(
            jax.ShapeDtypeStruct((3, 8, 8, 128), F32),
            jax.ShapeDtypeStruct((8, 8, 128), F32),
            jax.ShapeDtypeStruct((8, 8, 128), F32),
        ),
        in_specs=[pl.BlockSpec(memory_space=pltpu.SMEM)] + [vmem] * 6,
        out_specs=(vmem,) * 3,
        compiler_params=pltpu.CompilerParams(vmem_limit_bytes=VMEM_LIMIT),
        name="volumes",
    )(role, nodes, shift, back, planes, rows, corners)


def local(
    face_pressure,
    face_area,
    face_center,
    motion,
    inverse_mass,
    control_points,
    control_modes,
    node_points,
    tile_list,
    tile_count,
):
    raw, more_nodes, more_ids = gather(
        control_points, control_modes, face_pressure.reshape(-1, 128), face_area, face_center, node_points, tile_list
    )
    role = jnp.stack(
        [is_heavy().astype(jnp.int32), lax.axis_index("slab").astype(jnp.int32), lax.axis_index("ctrl").astype(jnp.int32)]
    )
    shift, more_shift, plane_edge, row_edge, new_state = pair_sums(
        role,
        tile_list.reshape(LINES, 16),
        more_ids.reshape(MORE, 16),
        tile_count,
        motion,
        inverse_mass,
        raw.reshape(NTILE, 3, 8, 128),
        node_points,
        more_nodes,
    )
    back, planes, rows, corners = exchange(more_shift, plane_edge, row_edge)
    node_shift, volume, change = volumes(role, node_points, shift, back, planes, rows, corners)
    return node_shift, volume, change, new_state


def solution(mesh):
    placed = (
        P(("slab", "ctrl")),
        P(None, ("slab", "ctrl")),
        P(None, ("slab", "ctrl")),
        P(),
        P(),
        P(None, ("slab", "ctrl")),
        P(None, ("slab", "ctrl")),
        P(None, "slab", "ctrl", None),
        P("slab", "ctrl", None),
        P("slab", "ctrl"),
    )
    return jax.shard_map(
        local,
        mesh=mesh,
        in_specs=placed,
        out_specs=(
            P(None, "slab", "ctrl", None),
            P("slab", "ctrl", None),
            P("slab", "ctrl", None),
            P(),
        ),
        check_vma=False,
    )
```

```python
import functools

import jax
import jax.numpy as jnp
from jax import lax
from jax.experimental import pallas as pl
from jax.experimental.pallas import tpu as pltpu
from jax.sharding import PartitionSpec as P

MESH = pl.DeviceIdType.MESH
TILE = 128
NTILE = 64
F32 = jnp.float32
BF16 = jnp.bfloat16
TIME_STEP = 0.5
GRAVITY = (0.0, 0.0, -0.5, 0.0, 0.0, 0.0)
XS, YS, ZS, CORES = 4, 4, 16, 2
LOAD_LANE = 80


def iota(shape, axis):
    return lax.broadcasted_iota(jnp.int32, shape, axis)


def place():
    slab = lax.axis_index("slab")
    return slab // (ZS * CORES), lax.axis_index("ctrl"), (slab // CORES) % ZS, slab % CORES


def device(x, y, z, core):
    return {"slab": (x % XS * ZS + z % ZS) * CORES + core, "ctrl": y % YS}


def is_heavy():
    slab = lax.axis_index("slab")
    return jnp.logical_and(slab >= 48, slab < 80)


def heavy_x(z):
    return 2 - z // 8


def gather_kernel(
    points_hbm,
    modes_hbm,
    pressure_hbm,
    area_hbm,
    center_hbm,
    nodes,
    ids,
    buf,
    more_nodes,
    more_ids,
    points,
    modes,
    pressure,
    area,
    center,
    pack,
    turn,
    own,
    fetch,
    send,
    recv,
):
    x, y, z, core = place()
    group = core * YS + y
    plane = [(i * core, i * (1 - core)) for i in range(1, 4)]
    turned = [(i * (1 - core), i * core) for i in range(1, 4)]

    sources = (points_hbm, modes_hbm, pressure_hbm, area_hbm, center_hbm)
    fetches = [
        pltpu.make_async_copy(src, dst, fetch.at[i])
        for i, (src, dst) in enumerate(zip(sources, (points, modes, pressure, area, center)))
    ]
    for copy in fetches:
        copy.start()

    barrier = pltpu.get_barrier_semaphore()
    greet = [device(x, y, z + d, core) for d in (4, -4, 3, -3, 2, -2, 1, -1)]
    greet += [device(x + dx, y + dy, z, core) for dx, dy in plane + turned]
    greet += [device(x, y, z, 1 - core)]
    for target in greet:
        pl.semaphore_signal(barrier, inc=1, device_id=target, device_id_type=MESH)

    for copy in fetches[:2]:
        copy.wait()
    pack[...] = jnp.zeros((24, 128), F32)
    pack[0:3, 0:16] = points[...]
    turn[...] = jnp.zeros((16, 128), F32)
    turn[:, 0:18] = modes[...]
    pack[3:21, 0:16] = jnp.transpose(turn[...], (1, 0))[0:18]
    packed = []
    for r in range(3):
        v = pack[8 * r : 8 * r + 8, :]
        for bit in (1, 2, 4):
            v = jnp.where((iota((8, 128), 0) & bit) == 0, v, pltpu.roll(v, 16 * bit, 1))
        packed.append(jnp.sum(v, axis=0, keepdims=True))

    for copy in fetches[2:]:
        copy.wait()
    force = jnp.zeros((3, 128), F32)
    moment = jnp.zeros((3, 128), F32)
    for i in range(pressure.shape[0]):
        at = pl.ds(i * 128, 128)
        pushed = area[:, at] * pressure[i : i + 1, :]
        c = center[:, at]
        force = force + pushed
        moment = moment + jnp.concatenate(
            [
                c[1:2] * pushed[2:3] - c[2:3] * pushed[1:2],
                c[2:3] * pushed[0:1] - c[0:1] * pushed[2:3],
                c[0:1] * pushed[1:2] - c[1:2] * pushed[0:1],
            ],
            axis=0,
        )
    sums = jnp.sum(jnp.concatenate([force, moment], axis=0), axis=1, keepdims=True)
    lane = iota((6, 128), 1)
    row = iota((6, 128), 0)
    loads = jnp.sum(jnp.where(lane == row + LOAD_LANE, sums, 0.0), axis=0, keepdims=True)
    own[0] = packed[0]
    own[1] = packed[1]
    own[2] = packed[2] + loads
    for r in range(3):
        buf[x, 4, r, group] = own[r]

    pl.semaphore_wait(barrier, len(greet))

    heavy = is_heavy()

    def hand(h, src_plane):
        target = device(heavy_x(z) + 1 + h, y, z, core)
        parts = []
        for i, (src, dst) in enumerate(
            ((nodes.at[:, pl.ds(src_plane, 2)], more_nodes), (ids.at[pl.ds(src_plane, 2)], more_ids))
        ):
            parts.append(
                pltpu.make_async_remote_copy(
                    src_ref=src,
                    dst_ref=dst,
                    send_sem=send.at[29 + 2 * h + i],
                    recv_sem=recv.at[29 + i],
                    device_id=target,
                    device_id_type=MESH,
                )
            )
        return parts

    pending = []

    def put(src, dst, slot, target):
        copy = pltpu.make_async_remote_copy(
            src_ref=src,
            dst_ref=dst,
            send_sem=send.at[slot],
            recv_sem=recv.at[slot],
            device_id=target,
            device_id_type=MESH,
        )
        copy.start()
        pending.append(copy)
        return copy

    def slot(j):
        return buf.at[x, j, :, group]

    near = {}
    for d in (4, 3, 2, 1):
        near[d] = put(own, slot(4 - d), d - 1, device(x, y, z + d, core))
        near[-d] = put(own, slot(4 + d), d + 3, device(x, y, z - d, core))

    @pl.when(heavy)
    def _():
        for h in range(3):
            for copy in hand(h, 1 + 2 * h):
                copy.start()

    far = []
    for d in (1, 2, 3, 4):
        near[d].wait_recv()
        far.append(put(slot(4 - d), slot(16 - d), d + 7, device(x, y, z + 4, core)))
        near[-d].wait_recv()
        if d < 4:
            far.append(put(slot(4 + d), slot(8 + d), d + 11, device(x, y, z - 4, core)))

    halves = (pl.ds(0, 9), pl.ds(9, 7))

    def first(part):
        ref = buf.at[x, halves[part], :, group]
        return [
            put(ref, ref, 15 + 3 * part + i, device(x + dx, y + dy, z, core)) for i, (dx, dy) in enumerate(plane)
        ]

    def second(part, start):
        for i, (dx, dy) in enumerate(turned):
            target = device(x + dx, y + dy, z, core)

            def make(ref, i=i, target=target):
                return pltpu.make_async_remote_copy(
                    src_ref=ref,
                    dst_ref=ref,
                    send_sem=send.at[21 + 3 * part + i],
                    recv_sem=recv.at[21 + 3 * part + i],
                    device_id=target,
                    device_id_type=MESH,
                )

            @pl.when(core == 0)
            def _():
                copy = make(buf.at[x, halves[part], :, pl.ds(0, YS)])
                copy.start() if start else copy.wait()

            @pl.when(core == 1)
            def _():
                copy = make(buf.at[:, halves[part], :, group])
                copy.start() if start else copy.wait()

    def across(part):
        ref = buf.at[:, halves[part], :, pl.ds(core * YS, YS)]
        return put(ref, ref, 27 + part, device(x, y, z, 1 - core))

    first_near = first(0)
    for copy in first_near:
        copy.wait_recv()
    second(0, True)
    for copy in far:
        copy.wait_recv()
    first_far = first(1)
    for copy in first_far:
        copy.wait_recv()
    second(1, True)
    second(0, False)
    across_near = across(0)
    second(1, False)
    across_far = across(1)
    across_near.wait_recv()
    across_far.wait_recv()
    for copy in pending:
        copy.wait_send()

    @pl.when(heavy)
    def _():
        for h in range(3):
            for copy in hand(h, 1 + 2 * h):
                copy.wait_send()

    @pl.when(jnp.logical_not(heavy))
    def _():
        for copy in hand(0, 1):
            copy.wait_recv()


def gather(points, modes, pressure, area, center, nodes, ids):
    vmem = pl.BlockSpec(memory_space=pltpu.VMEM)
    hbm = pl.BlockSpec(memory_space=pl.ANY)
    return pl.pallas_call(
        gather_kernel,
        out_shape=(
            jax.ShapeDtypeStruct((XS, ZS, 3, 8, 1, 128), F32),
            jax.ShapeDtypeStruct((3, 2, 8, 128), F32),
            jax.ShapeDtypeStruct((2, 8, 16), jnp.int32),
        ),
        in_specs=[pl.BlockSpec(memory_space=pltpu.HBM)] * 7,
        out_specs=(vmem, hbm, hbm),
        scratch_shapes=[
            pltpu.VMEM(points.shape, F32),
            pltpu.VMEM(modes.shape, F32),
            pltpu.VMEM(pressure.shape, F32),
            pltpu.VMEM(area.shape, F32),
            pltpu.VMEM(center.shape, F32),
            pltpu.VMEM((24, 128), F32),
            pltpu.VMEM((16, 128), F32),
            pltpu.VMEM((3, 1, 128), F32),
            pltpu.SemaphoreType.DMA((5,)),
            pltpu.SemaphoreType.DMA((35,)),
            pltpu.SemaphoreType.DMA((31,)),
        ],
        compiler_params=pltpu.CompilerParams(
            collective_id=0, has_side_effects=True, vmem_limit_bytes=VMEM_LIMIT
        ),
        name="gather",
    )(*(pltpu.with_memory_space_constraint(v, pltpu.HBM) for v in (points, modes, pressure, area, center, nodes, ids)))


VMEM_LIMIT = 24 << 20


def split3(value):
    hi = value.astype(BF16).astype(F32)
    rest = value - hi
    mid = rest.astype(BF16).astype(F32)
    return hi, mid, rest - mid


def regroup(v):
    sub = iota((8, 128), 0)
    grp = iota((8, 128), 1) // 16
    for bit in (1, 2, 4):
        below = pltpu.roll(pltpu.roll(v, 8 - bit, 0), 16 * bit, 1)
        above = pltpu.roll(pltpu.roll(v, bit, 0), 128 - 16 * bit, 1) if bit < 4 else below
        low = (sub & bit) == 0
        same = low == ((grp & bit) == 0)
        v = jnp.where(same, v, jnp.where(low, below, above))
    return v


def node_rows(nodes, p, r):
    sub = iota((8, 128), 0)
    x = [nodes[c, p, pl.ds(r, 1), :] for c in range(3)]
    square = x[0] * x[0] + x[1] * x[1] + x[2] * x[2]
    rows = jnp.where((sub == 0) | (sub == 3), -2.0 * x[0], 0.0)
    rows = jnp.where((sub == 1) | (sub == 4), -2.0 * x[1], rows)
    rows = jnp.where((sub == 2) | (sub == 5), -2.0 * x[2], rows)
    rows = jnp.where(sub == 7, square, rows)
    hi, mid, lo = split3(rows)
    one = sub == 6
    second = (sub >= 3) & (sub < 6)
    parts = [
        jnp.where(one, 1.0, jnp.where(second, mid, hi)),
        jnp.where(one, 1.0, jnp.where(sub < 3, hi, mid)),
        jnp.where(one, 1.0, jnp.where(second, hi, lo)),
        jnp.zeros((8, 128), F32),
    ]
    return jnp.concatenate(parts, axis=0).astype(BF16)


def control_rows(p):
    sub = iota((8, 128), 0)
    p = jnp.where(sub < 3, p, 0.0)
    square = jnp.sum(p * p, axis=0, keepdims=True)
    rows = p + pltpu.roll(p, 3, 0) + jnp.where(sub == 6, square, 0.0)
    hi, mid, lo = split3(rows)
    one = sub == 7
    parts = [
        jnp.where(one, 1.0, hi),
        jnp.where(one, 1.0, mid),
        jnp.where(one, 1.0, jnp.where(sub < 3, hi, lo)),
        jnp.zeros((8, 128), F32),
    ]
    return parts


BLOCK = 32


def pair_kernel(
    role,
    ids_hbm,
    more_ids_hbm,
    counts_hbm,
    motion_hbm,
    inverse_mass_hbm,
    raw,
    nodes,
    more_nodes,
    shift,
    more_shift,
    plane_edge,
    row_edge,
    state,
    feats,
    left_a,
    left_b,
    mix_a,
    mix_b,
    right,
    sums,
    unit_of,
    ids,
    more_ids,
    counts,
    motion,
    inverse_mass,
    fetch,
):
    lines = LINES + MORE
    sources = (ids_hbm, more_ids_hbm, counts_hbm, motion_hbm, inverse_mass_hbm)
    fetches = [
        pltpu.make_async_copy(src, dst, fetch.at[i])
        for i, (src, dst) in enumerate(zip(sources, (ids, more_ids, counts, motion, inverse_mass)))
    ]
    for copy in fetches:
        copy.start()
    heavy = role[0]
    light = 1 - heavy
    z = (role[1] >> 1) & (ZS - 1)
    sub = iota((8, 128), 0)

    def unpack(t, total):
        at = (t & ~(ZS - 1)) | ((t - z + 4) & (ZS - 1))
        v = [regroup(raw[at, r]) for r in range(3)]
        for r in range(3):
            feats[t, pl.ds(8 * r, 8), :] = v[r]
        return total + v[2]

    total = lax.fori_loop(0, NTILE, unpack, jnp.zeros((8, 128), F32), unroll=4)
    for copy in fetches:
        copy.wait()
    total = jnp.broadcast_to(total[5:6, :], (8, 128))
    for by in (16, 32, 64):
        total = total + pltpu.roll(total, by, 1)
    rigid = []
    for k in range(6):
        load = jnp.broadcast_to(total[:, k : k + 1], (8, 128))
        acceleration = inverse_mass[k] * load + GRAVITY[k]
        state[k] = (motion[k] + TIME_STEP * acceleration)[0, 0]
        rigid.append((TIME_STEP * motion[k] + 0.5 * TIME_STEP * TIME_STEP * acceleration)[0:3])

    first_half = jnp.where(iota((128, 64), 1) < 32, 1.0, 0.0).astype(BF16)

    def prepare(i, n):
        q = jnp.minimum(i, 13)
        more_line = q + jnp.where(q < 7, 1, 2)
        more_code = (LINES + more_line) << 6
        more_count = jnp.where(i < 14, 4 * light, 0)
        for u in range(4):
            t = 4 * i + u
            for e in range(4):
                unit_of[n + e] = (t << 6) + ids[t, e]
            n = n + light * counts[i >> 1, ((i & 1) << 2) + u]
            for e in range(4):
                unit_of[n + e] = more_code + more_ids[more_line, 4 * u + e]
            n = n + more_count

            parts = control_rows(feats[t, 0:8, :])
            columns = jnp.transpose(jnp.concatenate(parts + parts, axis=0), (1, 0)).astype(BF16)
            left = columns * first_half
            left_a[t] = left
            left_b[t] = columns - left
            c = jnp.zeros((3, 128), F32)
            for k in range(6):
                c = c + rigid[k] * feats[t, 3 + 3 * k : 6 + 3 * k, :]
            c = c * (1.0 / 256.0)
            c = jnp.concatenate([c, c, jnp.zeros((2, 128), F32)], axis=0)
            c_hi = c.astype(BF16).astype(F32)
            c = jnp.where(sub < 3, c_hi, c - c_hi)
            zero = jnp.zeros((8, 128), F32)
            mix_a[t] = jnp.concatenate([c, zero], axis=0).astype(BF16)
            mix_b[t] = jnp.concatenate([zero, c], axis=0).astype(BF16)
            right[t] = node_rows(nodes, i >> 1, ((i & 1) << 2) + u)
            sums[t] = zero
        return n

    n = lax.fori_loop(0, NTILE // 4, prepare, jnp.int32(0))

    def keep(i, n):
        line = jnp.where(i < 8, i, jnp.where(i < 15, (i - 7) << 3, i + 42))
        for e in range(16):
            unit_of[n + e] = (line << 6) + ids[line, e]
        return n + 16

    n = lax.fori_loop(0, 22 * heavy, keep, n)
    for e in range(BLOCK):
        unit_of[n + e] = lines * NTILE

    def prepare_more(i, _):
        right[LINES + i] = node_rows(more_nodes, i >> 3, i & 7)
        sums[LINES + i] = jnp.zeros((8, 128), F32)
        return 0

    lax.fori_loop(0, MORE, prepare_more, 0, unroll=4)
    right[lines] = jnp.zeros((32, 128), BF16)
    sums[lines] = jnp.zeros((8, 128), F32)

    gap = jnp.zeros((32, 128), BF16)

    def block(g, _):
        for u in range(0, BLOCK, 2):
            i = g * BLOCK + u
            c1, c2 = unit_of[i], unit_of[i + 1]
            t1, t2 = c1 & (NTILE - 1), c2 & (NTILE - 1)
            l1, l2 = c1 >> 6, c2 >> 6
            rhs = jnp.concatenate(
                [jnp.concatenate([right[l1], gap], axis=1), jnp.concatenate([gap, right[l2]], axis=1)], axis=0
            )
            s = jnp.dot(left_a[t1] + left_b[t2], rhs, preferred_element_type=F32)
            s = jnp.minimum(jnp.maximum(s, 1e-30), 16.0)
            d = s * lax.rsqrt(s)
            v = 4.0 - d
            v = v * v
            k = v * v * (1.0 + d)
            hi = k.astype(BF16)
            lo = (k - hi.astype(F32)).astype(BF16)
            m = mix_a[t1] + mix_b[t2]
            out = jnp.dot(
                jnp.concatenate([m, m], axis=1), jnp.concatenate([hi, lo], axis=0), preferred_element_type=F32
            )
            sums[l1] += out[0:8, 0:128]
            sums[l2] += out[8:16, 128:256]
        return 0

    lax.fori_loop(0, (n + BLOCK - 1) >> 5, block, 0)

    for i in range(lines):
        v = sums[i]
        v = v + pltpu.roll(v, 5, 0)
        for c in range(3):
            if i < LINES:
                shift[c, i // 8, i % 8 : i % 8 + 1, :] = v[c : c + 1, :]
            else:
                more_shift[c, i // 8 - 8, i % 8 : i % 8 + 1, :] = v[c : c + 1, :]
    for c in range(3):
        plane_edge[0, c] = nodes[c, 0]
        plane_edge[1, c] = nodes[c, 0] + shift[c, 0]
        for p in range(8):
            row_edge[0, c, p : p + 1, :] = nodes[c, p, 0:1, :]
            row_edge[1, c, p : p + 1, :] = nodes[c, p, 0:1, :] + shift[c, p, 0:1, :]


LINES = 64
MORE = 16


def pair_sums(role, ids, more_ids, counts, motion, inverse_mass, raw, nodes, more_nodes):
    vmem = pl.BlockSpec(memory_space=pltpu.VMEM)
    smem = pl.BlockSpec(memory_space=pltpu.SMEM)
    lines = LINES + MORE
    units = 4 * LINES + 14 * 16 + 2 * BLOCK
    return pl.pallas_call(
        pair_kernel,
        out_shape=(
            jax.ShapeDtypeStruct((3, 8, 8, 128), F32),
            jax.ShapeDtypeStruct((3, 2, 8, 128), F32),
            jax.ShapeDtypeStruct((2, 3, 8, 128), F32),
            jax.ShapeDtypeStruct((2, 3, 8, 128), F32),
            jax.ShapeDtypeStruct((6,), F32),
        ),
        in_specs=[smem] + [pl.BlockSpec(memory_space=pltpu.HBM)] * 5 + [vmem] * 3,
        out_specs=(vmem,) * 4 + (smem,),
        scratch_shapes=[
            pltpu.VMEM((NTILE, 24, 128), F32),
            pltpu.VMEM((NTILE, 128, 64), BF16),
            pltpu.VMEM((NTILE, 128, 64), BF16),
            pltpu.VMEM((NTILE, 16, 128), BF16),
            pltpu.VMEM((NTILE, 16, 128), BF16),
            pltpu.VMEM((lines + 1, 32, 128), BF16),
            pltpu.VMEM((lines + 1, 8, 128), F32),
            pltpu.SMEM((units,), jnp.int32),
            pltpu.SMEM((LINES, 16), jnp.int32),
            pltpu.SMEM((MORE, 16), jnp.int32),
            pltpu.SMEM((8, 8), jnp.int32),
            pltpu.SMEM((6,), F32),
            pltpu.SMEM((6,), F32),
            pltpu.SemaphoreType.DMA((5,)),
        ],
        compiler_params=pltpu.CompilerParams(vmem_limit_bytes=VMEM_LIMIT),
        name="pairs",
    )(role, ids, more_ids, counts, motion, inverse_mass, raw, nodes, more_nodes)


def exchange_kernel(more_shift, plane_edge, row_edge, back, planes, rows, corners, send, recv):
    x, y, z, core = place()
    slab = lax.axis_index("slab")
    heavy = is_heavy()
    last = XS * ZS * CORES

    def at(ds, dy):
        return {"slab": (slab + ds + last) % last, "ctrl": (y + dy + YS) % YS}

    barrier = pltpu.get_barrier_semaphore()
    greet = [at(1, 0), at(-1, 0), at(0, 1), at(0, -1), at(1, 1), at(-1, -1)]
    greet += [device(x + i, y, z, core) for i in (1, 2, 3)]
    for target in greet:
        pl.semaphore_signal(barrier, inc=1, device_id=target, device_id_type=MESH)
    pl.semaphore_wait(barrier, len(greet))

    def put(src, dst, slot, target):
        return pltpu.make_async_remote_copy(
            src_ref=src,
            dst_ref=dst,
            send_sem=send.at[slot],
            recv_sem=recv.at[slot],
            device_id=target,
            device_id_type=MESH,
        )

    def give(h):
        return pltpu.make_async_remote_copy(
            src_ref=more_shift,
            dst_ref=back.at[h],
            send_sem=send.at[3],
            recv_sem=recv.at[3 + h],
            device_id=device(heavy_x(z), y, z, core),
            device_id_type=MESH,
        )

    mine = (x - heavy_x(z) + 3) % XS

    @pl.when(jnp.logical_not(heavy))
    def _():
        give(jnp.minimum(mine, 2)).start()

    edges = [
        put(plane_edge, corners, 2, at(-1, -1)),
        put(plane_edge, planes, 0, at(-1, 0)),
        put(row_edge, rows, 1, at(0, -1)),
    ]
    for copy in edges:
        copy.start()

    @pl.when(heavy)
    def _():
        for h in range(3):
            give(h).wait_recv()

    @pl.when(jnp.logical_not(heavy))
    def _():
        give(jnp.minimum(mine, 2)).wait_send()

    for copy in edges:
        copy.wait()


def exchange(more_shift, plane_edge, row_edge):
    hbm = pl.BlockSpec(memory_space=pl.ANY)
    edge = jax.ShapeDtypeStruct((2, 3, 8, 128), F32)
    return pl.pallas_call(
        exchange_kernel,
        out_shape=(jax.ShapeDtypeStruct((3, 3, 2, 8, 128), F32), edge, edge, edge),
        in_specs=[hbm] * 3,
        out_specs=(hbm,) * 4,
        scratch_shapes=[pltpu.SemaphoreType.DMA((4,)), pltpu.SemaphoreType.DMA((6,))],
        compiler_params=pltpu.CompilerParams(
            collective_id=1, has_side_effects=True, vmem_limit_bytes=VMEM_LIMIT
        ),
        name="exchange",
    )(more_shift, plane_edge, row_edge)


def volume_kernel(role, nodes, shift, back, planes, rows, corners, out_shift, volume, change):
    slab, y = role[1], role[2]
    out_shift[...] = shift[...]

    @pl.when(role[0] == 1)
    def _():
        row = iota((8, 128), 0)
        for h in range(3):
            for c in range(3):
                for i in range(2):
                    p = 1 + 2 * h + i
                    out_shift[c, p] = jnp.where(row == 0, shift[c, p], back[h, c, i])

    bottom = iota((8, 128), 0) == 7

    def faces(field, c, p):
        if p < 8:
            a = nodes[c, p]
            if field:
                a = a + out_shift[c, p]
            edge = rows[field, c, p : p + 1, :]
        else:
            a = planes[field, c]
            edge = corners[field, c, 0:1, :]
        b = jnp.where(bottom, edge, pltpu.roll(a, 7, 0))
        az = pltpu.roll(a, 127, 1)
        bz = pltpu.roll(b, 127, 1)
        near, far = a + b, az + bz
        return near + far, (b + bz) - (a + az), far - near

    row = iota((8, 128), 0) + y * 8
    inside = jnp.logical_and(row < 31, iota((8, 128), 1) < 127)
    held = {}
    for p in range(9):
        for field in range(2):
            for c in range(3):
                held[field, c, p % 2] = faces(field, c, p)
        if p == 0:
            continue
        both = []
        for field in range(2):
            now = [held[field, c, p % 2] for c in range(3)]
            before = [held[field, c, (p - 1) % 2] for c in range(3)]
            ex = [0.25 * (n[0] - b[0]) for n, b in zip(now, before)]
            ey = [0.25 * (n[1] + b[1]) for n, b in zip(now, before)]
            ez = [0.25 * (n[2] + b[2]) for n, b in zip(now, before)]
            both.append(
                ex[0] * (ey[1] * ez[2] - ey[2] * ez[1])
                + ex[1] * (ey[2] * ez[0] - ey[0] * ez[2])
                + ex[2] * (ey[0] * ez[1] - ey[1] * ez[0])
            )
        ok = jnp.logical_and(inside, slab * 8 + p - 1 < 1023)
        old, new = (jnp.where(ok, v, 0.0) for v in both)
        volume[p - 1] = new
        change[p - 1] = new - old


def volumes(role, nodes, shift, back, planes, rows, corners):
    vmem = pl.BlockSpec(memory_space=pltpu.VMEM)
    return pl.pallas_call(
        volume_kernel,
        out_shape=(
            jax.ShapeDtypeStruct((3, 8, 8, 128), F32),
            jax.ShapeDtypeStruct((8, 8, 128), F32),
            jax.ShapeDtypeStruct((8, 8, 128), F32),
        ),
        in_specs=[pl.BlockSpec(memory_space=pltpu.SMEM)] + [vmem] * 6,
        out_specs=(vmem,) * 3,
        compiler_params=pltpu.CompilerParams(vmem_limit_bytes=VMEM_LIMIT),
        name="volumes",
    )(role, nodes, shift, back, planes, rows, corners)


def local(
    face_pressure,
    face_area,
    face_center,
    motion,
    inverse_mass,
    control_points,
    control_modes,
    node_points,
    tile_list,
    tile_count,
):
    raw, more_nodes, more_ids = gather(
        control_points, control_modes.T, face_pressure.reshape(-1, 128), face_area, face_center, node_points, tile_list
    )
    role = jnp.stack(
        [is_heavy().astype(jnp.int32), lax.axis_index("slab").astype(jnp.int32), lax.axis_index("ctrl").astype(jnp.int32)]
    )
    shift, more_shift, plane_edge, row_edge, new_state = pair_sums(
        role,
        tile_list.reshape(LINES, 16),
        more_ids.reshape(MORE, 16),
        *(pltpu.with_memory_space_constraint(v, pltpu.HBM) for v in (tile_count, motion, inverse_mass)),
        raw.reshape(NTILE, 3, 8, 128),
        node_points,
        more_nodes,
    )
    back, planes, rows, corners = exchange(more_shift, plane_edge, row_edge)
    node_shift, volume, change = volumes(role, node_points, shift, back, planes, rows, corners)
    return node_shift, volume, change, new_state


def solution(mesh):
    placed = (
        P(("slab", "ctrl")),
        P(None, ("slab", "ctrl")),
        P(None, ("slab", "ctrl")),
        P(),
        P(),
        P(None, ("slab", "ctrl")),
        P(None, ("slab", "ctrl")),
        P(None, "slab", "ctrl", None),
        P("slab", "ctrl", None),
        P("slab", "ctrl"),
    )
    return jax.shard_map(
        local,
        mesh=mesh,
        in_specs=placed,
        out_specs=(
            P(None, "slab", "ctrl", None),
            P("slab", "ctrl", None),
            P("slab", "ctrl", None),
            P(),
        ),
        check_vma=False,
    )
```

```python
import functools

import jax
import jax.numpy as jnp
from jax import lax
from jax.experimental import pallas as pl
from jax.experimental.pallas import tpu as pltpu
from jax.sharding import PartitionSpec as P

MESH = pl.DeviceIdType.MESH
TILE = 128
NTILE = 64
F32 = jnp.float32
BF16 = jnp.bfloat16
TIME_STEP = 0.5
GRAVITY = (0.0, 0.0, -0.5, 0.0, 0.0, 0.0)
XS, YS, ZS, CORES = 4, 4, 16, 2
LOAD_LANE = 80


def iota(shape, axis):
    return lax.broadcasted_iota(jnp.int32, shape, axis)


def place():
    slab = lax.axis_index("slab")
    return slab // (ZS * CORES), lax.axis_index("ctrl"), (slab // CORES) % ZS, slab % CORES


def device(x, y, z, core):
    return {"slab": (x % XS * ZS + z % ZS) * CORES + core, "ctrl": y % YS}


def is_heavy():
    slab = lax.axis_index("slab")
    return jnp.logical_and(slab >= 48, slab < 80)


def heavy_x(z):
    return 2 - z // 8


def split3(value):
    hi = value.astype(BF16).astype(F32)
    rest = value - hi
    mid = rest.astype(BF16).astype(F32)
    return hi, mid, rest - mid


def regroup(v):
    sub = iota((8, 128), 0)
    grp = iota((8, 128), 1) // 16
    for bit in (1, 2, 4):
        below = pltpu.roll(pltpu.roll(v, 8 - bit, 0), 16 * bit, 1)
        above = pltpu.roll(pltpu.roll(v, bit, 0), 128 - 16 * bit, 1) if bit < 4 else below
        low = (sub & bit) == 0
        same = low == ((grp & bit) == 0)
        v = jnp.where(same, v, jnp.where(low, below, above))
    return v


def node_rows(nodes, p, r):
    sub = iota((8, 128), 0)
    x = [nodes[c, p, pl.ds(r, 1), :] for c in range(3)]
    square = x[0] * x[0] + x[1] * x[1] + x[2] * x[2]
    rows = jnp.where((sub == 0) | (sub == 3), -2.0 * x[0], 0.0)
    rows = jnp.where((sub == 1) | (sub == 4), -2.0 * x[1], rows)
    rows = jnp.where((sub == 2) | (sub == 5), -2.0 * x[2], rows)
    rows = jnp.where(sub == 7, square, rows)
    hi, mid, lo = split3(rows)
    one = sub == 6
    second = (sub >= 3) & (sub < 6)
    parts = [
        jnp.where(one, 1.0, jnp.where(second, mid, hi)),
        jnp.where(one, 1.0, jnp.where(sub < 3, hi, mid)),
        jnp.where(one, 1.0, jnp.where(second, hi, lo)),
        jnp.zeros((8, 128), F32),
    ]
    return jnp.concatenate(parts, axis=0).astype(BF16)


def control_rows(p):
    sub = iota((8, 128), 0)
    p = jnp.where(sub < 3, p, 0.0)
    square = jnp.sum(p * p, axis=0, keepdims=True)
    rows = p + pltpu.roll(p, 3, 0) + jnp.where(sub == 6, square, 0.0)
    hi, mid, lo = split3(rows)
    one = sub == 7
    parts = [
        jnp.where(one, 1.0, hi),
        jnp.where(one, 1.0, mid),
        jnp.where(one, 1.0, jnp.where(sub < 3, hi, lo)),
        jnp.zeros((8, 128), F32),
    ]
    return parts


LINES = 64
MORE = 16


def gather_kernel(
    points_hbm,
    modes_hbm,
    pressure_hbm,
    area_hbm,
    center_hbm,
    nodes_hbm,
    ids,
    more_ids,
    feats,
    left_a,
    left_b,
    right,
    total,
    buf,
    nodes,
    more_nodes,
    points,
    modes,
    pressure,
    area,
    center,
    pack,
    turn,
    own,
    fetch,
    send,
    recv,
):
    x, y, z, core = place()
    group = core * YS + y
    plane = [(i * core, i * (1 - core)) for i in range(1, 4)]
    turned = [(i * (1 - core), i * core) for i in range(1, 4)]

    sources = (points_hbm, modes_hbm, pressure_hbm, area_hbm, center_hbm, nodes_hbm)
    fetches = [
        pltpu.make_async_copy(src, dst, fetch.at[i])
        for i, (src, dst) in enumerate(zip(sources, (points, modes, pressure, area, center, nodes)))
    ]
    for copy in fetches:
        copy.start()

    barrier = pltpu.get_barrier_semaphore()
    greet = [device(x, y, z + d, core) for d in (4, -4, 3, -3, 2, -2, 1, -1)]
    greet += [device(x + dx, y + dy, z, core) for dx, dy in plane + turned]
    greet += [device(x, y, z, 1 - core)]
    for target in greet:
        pl.semaphore_signal(barrier, inc=1, device_id=target, device_id_type=MESH)

    for copy in fetches[:2]:
        copy.wait()
    pack[...] = jnp.zeros((24, 128), F32)
    pack[0:3, 0:16] = points[...]
    turn[...] = jnp.zeros((16, 128), F32)
    turn[:, 0:18] = modes[...]
    pack[3:21, 0:16] = jnp.transpose(turn[...], (1, 0))[0:18]
    packed = []
    for r in range(3):
        v = pack[8 * r : 8 * r + 8, :]
        for bit in (1, 2, 4):
            v = jnp.where((iota((8, 128), 0) & bit) == 0, v, pltpu.roll(v, 16 * bit, 1))
        packed.append(jnp.sum(v, axis=0, keepdims=True))

    for copy in fetches[2:]:
        copy.wait()
    force = jnp.zeros((3, 128), F32)
    moment = jnp.zeros((3, 128), F32)
    for i in range(pressure.shape[0]):
        at = pl.ds(i * 128, 128)
        pushed = area[:, at] * pressure[i : i + 1, :]
        c = center[:, at]
        force = force + pushed
        moment = moment + jnp.concatenate(
            [
                c[1:2] * pushed[2:3] - c[2:3] * pushed[1:2],
                c[2:3] * pushed[0:1] - c[0:1] * pushed[2:3],
                c[0:1] * pushed[1:2] - c[1:2] * pushed[0:1],
            ],
            axis=0,
        )
    sums = jnp.sum(jnp.concatenate([force, moment], axis=0), axis=1, keepdims=True)
    lane = iota((6, 128), 1)
    row = iota((6, 128), 0)
    loads = jnp.sum(jnp.where(lane == row + LOAD_LANE, sums, 0.0), axis=0, keepdims=True)
    own[0:1, :] = packed[0]
    own[1:2, :] = packed[1]
    own[2:3, :] = packed[2] + loads
    for r in range(3):
        buf[x, 4, r, pl.ds(group, 1), :] = own[r : r + 1, :]

    pl.semaphore_wait(barrier, len(greet))

    heavy = is_heavy()

    def hand(h, src_plane):
        target = device(heavy_x(z) + 1 + h, y, z, core)
        parts = []
        for i, (src, dst) in enumerate(
            ((nodes_hbm.at[:, pl.ds(src_plane, 2)], more_nodes), (ids.at[pl.ds(src_plane, 2)], more_ids))
        ):
            parts.append(
                pltpu.make_async_remote_copy(
                    src_ref=src,
                    dst_ref=dst,
                    send_sem=send.at[29 + 2 * h + i],
                    recv_sem=recv.at[29 + i],
                    device_id=target,
                    device_id_type=MESH,
                )
            )
        return parts

    pending = []

    def put(src, dst, slot, target):
        copy = pltpu.make_async_remote_copy(
            src_ref=src,
            dst_ref=dst,
            send_sem=send.at[slot],
            recv_sem=recv.at[slot],
            device_id=target,
            device_id_type=MESH,
        )
        copy.start()
        pending.append(copy)
        return copy

    def slot(j):
        return buf.at[x, j, :, group]

    near = {}
    for d in (4, 3, 2, 1):
        near[d] = put(own, slot(4 - d), d - 1, device(x, y, z + d, core))
        near[-d] = put(own, slot(4 + d), d + 3, device(x, y, z - d, core))

    @pl.when(heavy)
    def _():
        for h in range(3):
            for copy in hand(h, 1 + 2 * h):
                copy.start()

    def line(i, _):
        right[i] = node_rows(nodes, i >> 3, i & 7)
        return 0

    lax.fori_loop(0, LINES, line, 0, unroll=4)
    right[LINES + MORE] = jnp.zeros((32, 128), BF16)

    far = []
    for d in (1, 2, 3, 4):
        near[d].wait_recv()
        far.append(put(slot(4 - d), slot(16 - d), d + 7, device(x, y, z + 4, core)))
        near[-d].wait_recv()
        if d < 4:
            far.append(put(slot(4 + d), slot(8 + d), d + 11, device(x, y, z - 4, core)))

    halves = (pl.ds(0, 9), pl.ds(9, 7))

    def first(part):
        ref = buf.at[x, halves[part], :, group]
        return [
            put(ref, ref, 15 + 3 * part + i, device(x + dx, y + dy, z, core)) for i, (dx, dy) in enumerate(plane)
        ]

    def second(part, start):
        for i, (dx, dy) in enumerate(turned):
            target = device(x + dx, y + dy, z, core)

            def make(ref, i=i, target=target):
                return pltpu.make_async_remote_copy(
                    src_ref=ref,
                    dst_ref=ref,
                    send_sem=send.at[21 + 3 * part + i],
                    recv_sem=recv.at[21 + 3 * part + i],
                    device_id=target,
                    device_id_type=MESH,
                )

            @pl.when(core == 0)
            def _():
                copy = make(buf.at[x, halves[part], :, pl.ds(0, YS)])
                copy.start() if start else copy.wait()

            @pl.when(core == 1)
            def _():
                copy = make(buf.at[:, halves[part], :, group])
                copy.start() if start else copy.wait()

    def across(part):
        ref = buf.at[:, halves[part], :, pl.ds(core * YS, YS)]
        return put(ref, ref, 27 + part, device(x, y, z, 1 - core))

    half = jnp.where(iota((128, 64), 1) < 32, 1.0, 0.0).astype(BF16)

    def unpack(j, carry):
        for xx in range(XS):
            t = xx * ZS + ((j + z + ZS - 4) & (ZS - 1))
            v = [regroup(buf[xx, j, r]) for r in range(3)]
            for r in range(3):
                feats[t, pl.ds(8 * r, 8), :] = v[r]
            parts = control_rows(v[0])
            columns = jnp.transpose(jnp.concatenate(parts + parts, axis=0), (1, 0)).astype(BF16)
            left = columns * half
            left_a[t] = left
            left_b[t] = columns - left
            carry = carry + v[2]
        return carry

    first_near = first(0)
    for copy in first_near:
        copy.wait_recv()
    second(0, True)
    for copy in far:
        copy.wait_recv()
    first_far = first(1)
    for copy in first_far:
        copy.wait_recv()
    second(1, True)
    second(0, False)
    across_near = across(0)

    @pl.when(jnp.logical_not(heavy))
    def _():
        for copy in hand(0, 1):
            copy.wait_recv()

        def more(i, _):
            right[LINES + i] = node_rows(more_nodes, i >> 3, i & 7)
            return 0

        lax.fori_loop(0, MORE, more, 0, unroll=4)

    across_near.wait_recv()
    loads = lax.fori_loop(0, 9, unpack, jnp.zeros((8, 128), F32))
    second(1, False)
    across_far = across(1)
    across_far.wait_recv()
    total[...] = lax.fori_loop(9, ZS, unpack, loads)
    for copy in pending:
        copy.wait_send()

    @pl.when(heavy)
    def _():
        for h in range(3):
            for copy in hand(h, 1 + 2 * h):
                copy.wait_send()


def gather(points, modes, pressure, area, center, nodes, ids):
    vmem = pl.BlockSpec(memory_space=pltpu.VMEM)
    hbm = pl.BlockSpec(memory_space=pl.ANY)
    return pl.pallas_call(
        gather_kernel,
        out_shape=(
            jax.ShapeDtypeStruct((2, 8, 16), jnp.int32),
            jax.ShapeDtypeStruct((NTILE, 24, 128), F32),
            jax.ShapeDtypeStruct((NTILE, 128, 64), BF16),
            jax.ShapeDtypeStruct((NTILE, 128, 64), BF16),
            jax.ShapeDtypeStruct((LINES + MORE + 1, 32, 128), BF16),
            jax.ShapeDtypeStruct((8, 128), F32),
        ),
        in_specs=[pl.BlockSpec(memory_space=pltpu.HBM)] * 7,
        out_specs=(hbm,) + (vmem,) * 5,
        scratch_shapes=[
            pltpu.VMEM((XS, ZS, 3, 8, 128), F32),
            pltpu.VMEM(nodes.shape, F32),
            pltpu.VMEM((3, 2, 8, 128), F32),
            pltpu.VMEM(points.shape, F32),
            pltpu.VMEM(modes.shape, F32),
            pltpu.VMEM(pressure.shape, F32),
            pltpu.VMEM(area.shape, F32),
            pltpu.VMEM(center.shape, F32),
            pltpu.VMEM((24, 128), F32),
            pltpu.VMEM((16, 128), F32),
            pltpu.VMEM((3, 128), F32),
            pltpu.SemaphoreType.DMA((6,)),
            pltpu.SemaphoreType.DMA((35,)),
            pltpu.SemaphoreType.DMA((31,)),
        ],
        compiler_params=pltpu.CompilerParams(
            collective_id=0, has_side_effects=True, vmem_limit_bytes=VMEM_LIMIT
        ),
        name="gather",
    )(*(pltpu.with_memory_space_constraint(v, pltpu.HBM) for v in (points, modes, pressure, area, center, nodes, ids)))


VMEM_LIMIT = 24 << 20


BLOCK = 32


def pair_kernel(
    role,
    ids_hbm,
    more_ids_hbm,
    counts_hbm,
    motion_hbm,
    inverse_mass_hbm,
    total_ref,
    feats,
    left_a,
    left_b,
    right,
    nodes,
    shift,
    more_shift,
    plane_edge,
    row_edge,
    state,
    mix_a,
    mix_b,
    sums,
    unit_of,
    ids,
    more_ids,
    counts,
    motion,
    inverse_mass,
    fetch,
):
    lines = LINES + MORE
    sources = (ids_hbm, more_ids_hbm, counts_hbm, motion_hbm, inverse_mass_hbm)
    fetches = [
        pltpu.make_async_copy(src, dst, fetch.at[i])
        for i, (src, dst) in enumerate(zip(sources, (ids, more_ids, counts, motion, inverse_mass)))
    ]
    for copy in fetches:
        copy.start()
    heavy = role[0]
    light = 1 - heavy
    sub = iota((8, 128), 0)

    for copy in fetches:
        copy.wait()
    total = jnp.broadcast_to(total_ref[5:6, :], (8, 128))
    for by in (16, 32, 64):
        total = total + pltpu.roll(total, by, 1)
    rigid = []
    for k in range(6):
        load = jnp.broadcast_to(total[:, k : k + 1], (8, 128))
        acceleration = inverse_mass[k] * load + GRAVITY[k]
        state[k] = (motion[k] + TIME_STEP * acceleration)[0, 0]
        rigid.append((TIME_STEP * motion[k] + 0.5 * TIME_STEP * TIME_STEP * acceleration)[0:3])

    def prepare(i, n):
        q = jnp.minimum(i, 13)
        more_line = q + jnp.where(q < 7, 1, 2)
        more_code = (LINES + more_line) << 6
        more_count = jnp.where(i < 14, 4 * light, 0)
        for u in range(4):
            t = 4 * i + u
            for e in range(4):
                unit_of[n + e] = (t << 6) + ids[t, e]
            n = n + light * counts[i >> 1, ((i & 1) << 2) + u]
            for e in range(4):
                unit_of[n + e] = more_code + more_ids[more_line, 4 * u + e]
            n = n + more_count

            c = jnp.zeros((3, 128), F32)
            for k in range(6):
                c = c + rigid[k] * feats[t, 3 + 3 * k : 6 + 3 * k, :]
            c = c * (1.0 / 256.0)
            c = jnp.concatenate([c, c, jnp.zeros((2, 128), F32)], axis=0)
            c_hi = c.astype(BF16).astype(F32)
            c = jnp.where(sub < 3, c_hi, c - c_hi)
            zero = jnp.zeros((8, 128), F32)
            mix_a[t] = jnp.concatenate([c, zero], axis=0).astype(BF16)
            mix_b[t] = jnp.concatenate([zero, c], axis=0).astype(BF16)
            sums[t] = zero
        return n

    n = lax.fori_loop(0, NTILE // 4, prepare, jnp.int32(0))

    def keep(i, n):
        line = jnp.where(i < 8, i, jnp.where(i < 15, (i - 7) << 3, i + 42))
        for e in range(16):
            unit_of[n + e] = (line << 6) + ids[line, e]
        return n + 16

    n = lax.fori_loop(0, 22 * heavy, keep, n)
    for e in range(BLOCK):
        unit_of[n + e] = lines * NTILE

    for i in range(LINES, lines):
        sums[i] = jnp.zeros((8, 128), F32)
    sums[lines] = jnp.zeros((8, 128), F32)

    gap = jnp.zeros((32, 128), BF16)

    def block(g, _):
        for u in range(0, BLOCK, 2):
            i = g * BLOCK + u
            c1, c2 = unit_of[i], unit_of[i + 1]
            t1, t2 = c1 & (NTILE - 1), c2 & (NTILE - 1)
            l1, l2 = c1 >> 6, c2 >> 6
            rhs = jnp.concatenate(
                [jnp.concatenate([right[l1], gap], axis=1), jnp.concatenate([gap, right[l2]], axis=1)], axis=0
            )
            s = jnp.dot(left_a[t1] + left_b[t2], rhs, preferred_element_type=F32)
            s = jnp.minimum(jnp.maximum(s, 1e-30), 16.0)
            d = s * lax.rsqrt(s)
            v = 4.0 - d
            v = v * v
            k = v * v * (1.0 + d)
            hi = k.astype(BF16)
            lo = (k - hi.astype(F32)).astype(BF16)
            m = mix_a[t1] + mix_b[t2]
            out = jnp.dot(
                jnp.concatenate([m, m], axis=1), jnp.concatenate([hi, lo], axis=0), preferred_element_type=F32
            )
            sums[l1] += out[0:8, 0:128]
            sums[l2] += out[8:16, 128:256]
        return 0

    lax.fori_loop(0, (n + BLOCK - 1) >> 5, block, 0)

    for i in range(lines):
        v = sums[i]
        v = v + pltpu.roll(v, 5, 0)
        for c in range(3):
            if i < LINES:
                shift[c, i // 8, i % 8 : i % 8 + 1, :] = v[c : c + 1, :]
            else:
                more_shift[c, i // 8 - 8, i % 8 : i % 8 + 1, :] = v[c : c + 1, :]
    for c in range(3):
        plane_edge[0, c] = nodes[c, 0]
        plane_edge[1, c] = nodes[c, 0] + shift[c, 0]
        for p in range(8):
            row_edge[0, c, p : p + 1, :] = nodes[c, p, 0:1, :]
            row_edge[1, c, p : p + 1, :] = nodes[c, p, 0:1, :] + shift[c, p, 0:1, :]


def pair_sums(role, ids, more_ids, counts, motion, inverse_mass, total, feats, left_a, left_b, right, nodes):
    vmem = pl.BlockSpec(memory_space=pltpu.VMEM)
    smem = pl.BlockSpec(memory_space=pltpu.SMEM)
    lines = LINES + MORE
    units = 4 * LINES + 14 * 16 + 2 * BLOCK
    return pl.pallas_call(
        pair_kernel,
        out_shape=(
            jax.ShapeDtypeStruct((3, 8, 8, 128), F32),
            jax.ShapeDtypeStruct((3, 2, 8, 128), F32),
            jax.ShapeDtypeStruct((2, 3, 8, 128), F32),
            jax.ShapeDtypeStruct((2, 3, 8, 128), F32),
            jax.ShapeDtypeStruct((6,), F32),
        ),
        in_specs=[smem] + [pl.BlockSpec(memory_space=pltpu.HBM)] * 5 + [vmem] * 6,
        out_specs=(vmem,) * 4 + (smem,),
        scratch_shapes=[
            pltpu.VMEM((NTILE, 16, 128), BF16),
            pltpu.VMEM((NTILE, 16, 128), BF16),
            pltpu.VMEM((lines + 1, 8, 128), F32),
            pltpu.SMEM((units,), jnp.int32),
            pltpu.SMEM((LINES, 16), jnp.int32),
            pltpu.SMEM((MORE, 16), jnp.int32),
            pltpu.SMEM((8, 8), jnp.int32),
            pltpu.SMEM((6,), F32),
            pltpu.SMEM((6,), F32),
            pltpu.SemaphoreType.DMA((5,)),
        ],
        compiler_params=pltpu.CompilerParams(vmem_limit_bytes=VMEM_LIMIT),
        name="pairs",
    )(role, ids, more_ids, counts, motion, inverse_mass, total, feats, left_a, left_b, right, nodes)


def exchange_kernel(more_shift, plane_edge, row_edge, back, planes, rows, corners, send, recv):
    x, y, z, core = place()
    slab = lax.axis_index("slab")
    heavy = is_heavy()
    last = XS * ZS * CORES

    def at(ds, dy):
        return {"slab": (slab + ds + last) % last, "ctrl": (y + dy + YS) % YS}

    barrier = pltpu.get_barrier_semaphore()
    greet = [at(1, 0), at(-1, 0), at(0, 1), at(0, -1), at(1, 1), at(-1, -1)]
    greet += [device(x + i, y, z, core) for i in (1, 2, 3)]
    for target in greet:
        pl.semaphore_signal(barrier, inc=1, device_id=target, device_id_type=MESH)
    pl.semaphore_wait(barrier, len(greet))

    def put(src, dst, slot, target):
        return pltpu.make_async_remote_copy(
            src_ref=src,
            dst_ref=dst,
            send_sem=send.at[slot],
            recv_sem=recv.at[slot],
            device_id=target,
            device_id_type=MESH,
        )

    def give(h):
        return pltpu.make_async_remote_copy(
            src_ref=more_shift,
            dst_ref=back.at[h],
            send_sem=send.at[3],
            recv_sem=recv.at[3 + h],
            device_id=device(heavy_x(z), y, z, core),
            device_id_type=MESH,
        )

    mine = (x - heavy_x(z) + 3) % XS

    @pl.when(jnp.logical_not(heavy))
    def _():
        give(jnp.minimum(mine, 2)).start()

    edges = [
        put(plane_edge, corners, 2, at(-1, -1)),
        put(plane_edge, planes, 0, at(-1, 0)),
        put(row_edge, rows, 1, at(0, -1)),
    ]
    for copy in edges:
        copy.start()

    @pl.when(heavy)
    def _():
        for h in range(3):
            give(h).wait_recv()

    @pl.when(jnp.logical_not(heavy))
    def _():
        give(jnp.minimum(mine, 2)).wait_send()

    for copy in edges:
        copy.wait()


def exchange(more_shift, plane_edge, row_edge):
    hbm = pl.BlockSpec(memory_space=pl.ANY)
    edge = jax.ShapeDtypeStruct((2, 3, 8, 128), F32)
    return pl.pallas_call(
        exchange_kernel,
        out_shape=(jax.ShapeDtypeStruct((3, 3, 2, 8, 128), F32), edge, edge, edge),
        in_specs=[hbm] * 3,
        out_specs=(hbm,) * 4,
        scratch_shapes=[pltpu.SemaphoreType.DMA((4,)), pltpu.SemaphoreType.DMA((6,))],
        compiler_params=pltpu.CompilerParams(
            collective_id=1, has_side_effects=True, vmem_limit_bytes=VMEM_LIMIT
        ),
        name="exchange",
    )(more_shift, plane_edge, row_edge)


def volume_kernel(role, nodes, shift, back, planes, rows, corners, out_shift, volume, change):
    slab, y = role[1], role[2]
    out_shift[...] = shift[...]

    @pl.when(role[0] == 1)
    def _():
        row = iota((8, 128), 0)
        for h in range(3):
            for c in range(3):
                for i in range(2):
                    p = 1 + 2 * h + i
                    out_shift[c, p] = jnp.where(row == 0, shift[c, p], back[h, c, i])

    bottom = iota((8, 128), 0) == 7

    def faces(field, c, p):
        if p < 8:
            a = nodes[c, p]
            if field:
                a = a + out_shift[c, p]
            edge = rows[field, c, p : p + 1, :]
        else:
            a = planes[field, c]
            edge = corners[field, c, 0:1, :]
        b = jnp.where(bottom, edge, pltpu.roll(a, 7, 0))
        az = pltpu.roll(a, 127, 1)
        bz = pltpu.roll(b, 127, 1)
        near, far = a + b, az + bz
        return near + far, (b + bz) - (a + az), far - near

    row = iota((8, 128), 0) + y * 8
    inside = jnp.logical_and(row < 31, iota((8, 128), 1) < 127)
    held = {}
    for p in range(9):
        for field in range(2):
            for c in range(3):
                held[field, c, p % 2] = faces(field, c, p)
        if p == 0:
            continue
        both = []
        for field in range(2):
            now = [held[field, c, p % 2] for c in range(3)]
            before = [held[field, c, (p - 1) % 2] for c in range(3)]
            ex = [0.25 * (n[0] - b[0]) for n, b in zip(now, before)]
            ey = [0.25 * (n[1] + b[1]) for n, b in zip(now, before)]
            ez = [0.25 * (n[2] + b[2]) for n, b in zip(now, before)]
            both.append(
                ex[0] * (ey[1] * ez[2] - ey[2] * ez[1])
                + ex[1] * (ey[2] * ez[0] - ey[0] * ez[2])
                + ex[2] * (ey[0] * ez[1] - ey[1] * ez[0])
            )
        ok = jnp.logical_and(inside, slab * 8 + p - 1 < 1023)
        old, new = (jnp.where(ok, v, 0.0) for v in both)
        volume[p - 1] = new
        change[p - 1] = new - old


def volumes(role, nodes, shift, back, planes, rows, corners):
    vmem = pl.BlockSpec(memory_space=pltpu.VMEM)
    return pl.pallas_call(
        volume_kernel,
        out_shape=(
            jax.ShapeDtypeStruct((3, 8, 8, 128), F32),
            jax.ShapeDtypeStruct((8, 8, 128), F32),
            jax.ShapeDtypeStruct((8, 8, 128), F32),
        ),
        in_specs=[pl.BlockSpec(memory_space=pltpu.SMEM)] + [vmem] * 6,
        out_specs=(vmem,) * 3,
        compiler_params=pltpu.CompilerParams(vmem_limit_bytes=VMEM_LIMIT),
        name="volumes",
    )(role, nodes, shift, back, planes, rows, corners)


def local(
    face_pressure,
    face_area,
    face_center,
    motion,
    inverse_mass,
    control_points,
    control_modes,
    node_points,
    tile_list,
    tile_count,
):
    more_ids, feats, left_a, left_b, right, total = gather(
        control_points, control_modes.T, face_pressure.reshape(-1, 128), face_area, face_center, node_points, tile_list
    )
    role = jnp.stack(
        [is_heavy().astype(jnp.int32), lax.axis_index("slab").astype(jnp.int32), lax.axis_index("ctrl").astype(jnp.int32)]
    )
    shift, more_shift, plane_edge, row_edge, new_state = pair_sums(
        role,
        tile_list.reshape(LINES, 16),
        more_ids.reshape(MORE, 16),
        *(pltpu.with_memory_space_constraint(v, pltpu.HBM) for v in (tile_count, motion, inverse_mass)),
        total,
        feats,
        left_a,
        left_b,
        right,
        node_points,
    )
    back, planes, rows, corners = exchange(more_shift, plane_edge, row_edge)
    node_shift, volume, change = volumes(role, node_points, shift, back, planes, rows, corners)
    return node_shift, volume, change, new_state


def solution(mesh):
    placed = (
        P(("slab", "ctrl")),
        P(None, ("slab", "ctrl")),
        P(None, ("slab", "ctrl")),
        P(),
        P(),
        P(None, ("slab", "ctrl")),
        P(None, ("slab", "ctrl")),
        P(None, "slab", "ctrl", None),
        P("slab", "ctrl", None),
        P("slab", "ctrl"),
    )
    return jax.shard_map(
        local,
        mesh=mesh,
        in_specs=placed,
        out_specs=(
            P(None, "slab", "ctrl", None),
            P("slab", "ctrl", None),
            P("slab", "ctrl", None),
            P(),
        ),
        check_vma=False,
    )
```

```python
import functools

import jax
import jax.numpy as jnp
from jax import lax
from jax.experimental import pallas as pl
from jax.experimental.pallas import tpu as pltpu
from jax.sharding import PartitionSpec as P

MESH = pl.DeviceIdType.MESH
TILE = 128
NTILE = 64
F32 = jnp.float32
BF16 = jnp.bfloat16
TIME_STEP = 0.5
GRAVITY = (0.0, 0.0, -0.5, 0.0, 0.0, 0.0)
XS, YS, ZS, CORES = 4, 4, 16, 2
LOAD_LANE = 80


def iota(shape, axis):
    return lax.broadcasted_iota(jnp.int32, shape, axis)


def place():
    slab = lax.axis_index("slab")
    return slab // (ZS * CORES), lax.axis_index("ctrl"), (slab // CORES) % ZS, slab % CORES


def device(x, y, z, core):
    return {"slab": (x % XS * ZS + z % ZS) * CORES + core, "ctrl": y % YS}


def is_heavy():
    slab = lax.axis_index("slab")
    return jnp.logical_and(slab >= 48, slab < 80)


def heavy_x(z):
    return 2 - z // 8


def split3(value):
    hi = value.astype(BF16).astype(F32)
    rest = value - hi
    mid = rest.astype(BF16).astype(F32)
    return hi, mid, rest - mid


def regroup(v):
    sub = iota((8, 128), 0)
    grp = iota((8, 128), 1) // 16
    for bit in (1, 2, 4):
        below = pltpu.roll(pltpu.roll(v, 8 - bit, 0), 16 * bit, 1)
        above = pltpu.roll(pltpu.roll(v, bit, 0), 128 - 16 * bit, 1) if bit < 4 else below
        low = (sub & bit) == 0
        same = low == ((grp & bit) == 0)
        v = jnp.where(same, v, jnp.where(low, below, above))
    return v


def node_rows(nodes, p, r):
    sub = iota((8, 128), 0)
    x = [nodes[c, p, pl.ds(r, 1), :] for c in range(3)]
    square = x[0] * x[0] + x[1] * x[1] + x[2] * x[2]
    rows = jnp.where((sub == 0) | (sub == 3), -2.0 * x[0], 0.0)
    rows = jnp.where((sub == 1) | (sub == 4), -2.0 * x[1], rows)
    rows = jnp.where((sub == 2) | (sub == 5), -2.0 * x[2], rows)
    rows = jnp.where(sub == 7, square, rows)
    hi, mid, lo = split3(rows)
    one = sub == 6
    second = (sub >= 3) & (sub < 6)
    parts = [
        jnp.where(one, 1.0, jnp.where(second, mid, hi)),
        jnp.where(one, 1.0, jnp.where(sub < 3, hi, mid)),
        jnp.where(one, 1.0, jnp.where(second, hi, lo)),
        jnp.zeros((8, 128), F32),
    ]
    return jnp.concatenate(parts, axis=0).astype(BF16)


def control_rows(p):
    sub = iota((8, 128), 0)
    p = jnp.where(sub < 3, p, 0.0)
    square = jnp.sum(p * p, axis=0, keepdims=True)
    rows = p + pltpu.roll(p, 3, 0) + jnp.where(sub == 6, square, 0.0)
    hi, mid, lo = split3(rows)
    one = sub == 7
    parts = [
        jnp.where(one, 1.0, hi),
        jnp.where(one, 1.0, mid),
        jnp.where(one, 1.0, jnp.where(sub < 3, hi, lo)),
        jnp.zeros((8, 128), F32),
    ]
    return parts


LINES = 64
MORE = 16


def gather_kernel(
    points_hbm,
    modes_hbm,
    pressure_hbm,
    area_hbm,
    center_hbm,
    nodes_hbm,
    ids_hbm,
    counts_hbm,
    motion_hbm,
    inverse_mass_hbm,
    all_ids,
    counts,
    feats,
    left_a,
    left_b,
    right,
    rigid,
    accelerations,
    buf,
    nodes,
    more_nodes,
    points,
    modes,
    pressure,
    area,
    center,
    pack,
    turn,
    own,
    motion,
    inverse_mass,
    fetch,
    send,
    recv,
):
    x, y, z, core = place()
    group = core * YS + y
    plane = [(i * core, i * (1 - core)) for i in range(1, 4)]
    turned = [(i * (1 - core), i * core) for i in range(1, 4)]

    sources = (
        points_hbm,
        modes_hbm,
        pressure_hbm,
        area_hbm,
        center_hbm,
        nodes_hbm,
        ids_hbm,
        counts_hbm,
        motion_hbm,
        inverse_mass_hbm,
    )
    kept = all_ids.at[pl.ds(0, 8)]
    targets = (points, modes, pressure, area, center, nodes, kept, counts, motion, inverse_mass)
    fetches = [
        pltpu.make_async_copy(src, dst, fetch.at[i]) for i, (src, dst) in enumerate(zip(sources, targets))
    ]
    for copy in fetches:
        copy.start()

    barrier = pltpu.get_barrier_semaphore()
    greet = [device(x, y, z + d, core) for d in (4, -4, 3, -3, 2, -2, 1, -1)]
    greet += [device(x + dx, y + dy, z, core) for dx, dy in plane + turned]
    greet += [device(x, y, z, 1 - core)]
    for target in greet:
        pl.semaphore_signal(barrier, inc=1, device_id=target, device_id_type=MESH)

    for copy in fetches[:2]:
        copy.wait()
    pack[...] = jnp.zeros((24, 128), F32)
    pack[0:3, 0:16] = points[...]
    turn[...] = jnp.zeros((16, 128), F32)
    turn[:, 0:18] = modes[...]
    pack[3:21, 0:16] = jnp.transpose(turn[...], (1, 0))[0:18]
    packed = []
    for r in range(3):
        v = pack[8 * r : 8 * r + 8, :]
        for bit in (1, 2, 4):
            v = jnp.where((iota((8, 128), 0) & bit) == 0, v, pltpu.roll(v, 16 * bit, 1))
        packed.append(jnp.sum(v, axis=0, keepdims=True))

    for copy in fetches[2:]:
        copy.wait()
    force = jnp.zeros((3, 128), F32)
    moment = jnp.zeros((3, 128), F32)
    for i in range(pressure.shape[0]):
        at = pl.ds(i * 128, 128)
        pushed = area[:, at] * pressure[i : i + 1, :]
        c = center[:, at]
        force = force + pushed
        moment = moment + jnp.concatenate(
            [
                c[1:2] * pushed[2:3] - c[2:3] * pushed[1:2],
                c[2:3] * pushed[0:1] - c[0:1] * pushed[2:3],
                c[0:1] * pushed[1:2] - c[1:2] * pushed[0:1],
            ],
            axis=0,
        )
    sums = jnp.sum(jnp.concatenate([force, moment], axis=0), axis=1, keepdims=True)
    lane = iota((6, 128), 1)
    row = iota((6, 128), 0)
    loads = jnp.sum(jnp.where(lane == row + LOAD_LANE, sums, 0.0), axis=0, keepdims=True)
    own[0:1, :] = packed[0]
    own[1:2, :] = packed[1]
    own[2:3, :] = packed[2] + loads
    for r in range(3):
        buf[x, 4, r, pl.ds(group, 1), :] = own[r : r + 1, :]

    pl.semaphore_wait(barrier, len(greet))

    heavy = is_heavy()

    def hand(h, src_plane):
        target = device(heavy_x(z) + 1 + h, y, z, core)
        parts = []
        for i, (src, dst) in enumerate(
            ((nodes_hbm.at[:, pl.ds(src_plane, 2)], more_nodes), (ids_hbm.at[pl.ds(src_plane, 2)], all_ids.at[pl.ds(8, 2)]))
        ):
            parts.append(
                pltpu.make_async_remote_copy(
                    src_ref=src,
                    dst_ref=dst,
                    send_sem=send.at[29 + 2 * h + i],
                    recv_sem=recv.at[29 + i],
                    device_id=target,
                    device_id_type=MESH,
                )
            )
        return parts

    pending = []

    def put(src, dst, slot, target):
        copy = pltpu.make_async_remote_copy(
            src_ref=src,
            dst_ref=dst,
            send_sem=send.at[slot],
            recv_sem=recv.at[slot],
            device_id=target,
            device_id_type=MESH,
        )
        copy.start()
        pending.append(copy)
        return copy

    def slot(j):
        return buf.at[x, j, :, group]

    near = {}
    for d in (4, 3, 2, 1):
        near[d] = put(own, slot(4 - d), d - 1, device(x, y, z + d, core))
        near[-d] = put(own, slot(4 + d), d + 3, device(x, y, z - d, core))

    @pl.when(heavy)
    def _():
        for h in range(3):
            for copy in hand(h, 1 + 2 * h):
                copy.start()

    def line(i, _):
        right[i] = node_rows(nodes, i >> 3, i & 7)
        return 0

    lax.fori_loop(0, LINES, line, 0, unroll=4)
    right[LINES + MORE] = jnp.zeros((32, 128), BF16)

    far = []
    for d in (1, 2, 3, 4):
        near[d].wait_recv()
        far.append(put(slot(4 - d), slot(16 - d), d + 7, device(x, y, z + 4, core)))
        near[-d].wait_recv()
        if d < 4:
            far.append(put(slot(4 + d), slot(8 + d), d + 11, device(x, y, z - 4, core)))

    halves = (pl.ds(0, 9), pl.ds(9, 7))

    def first(part):
        ref = buf.at[x, halves[part], :, group]
        return [
            put(ref, ref, 15 + 3 * part + i, device(x + dx, y + dy, z, core)) for i, (dx, dy) in enumerate(plane)
        ]

    def second(part, start):
        for i, (dx, dy) in enumerate(turned):
            target = device(x + dx, y + dy, z, core)

            def make(ref, i=i, target=target):
                return pltpu.make_async_remote_copy(
                    src_ref=ref,
                    dst_ref=ref,
                    send_sem=send.at[21 + 3 * part + i],
                    recv_sem=recv.at[21 + 3 * part + i],
                    device_id=target,
                    device_id_type=MESH,
                )

            @pl.when(core == 0)
            def _():
                copy = make(buf.at[x, halves[part], :, pl.ds(0, YS)])
                copy.start() if start else copy.wait()

            @pl.when(core == 1)
            def _():
                copy = make(buf.at[:, halves[part], :, group])
                copy.start() if start else copy.wait()

    def across(part):
        ref = buf.at[:, halves[part], :, pl.ds(core * YS, YS)]
        return put(ref, ref, 27 + part, device(x, y, z, 1 - core))

    half = jnp.where(iota((128, 64), 1) < 32, 1.0, 0.0).astype(BF16)

    def unpack(j, carry):
        for xx in range(XS):
            t = xx * ZS + ((j + z + ZS - 4) & (ZS - 1))
            v = [regroup(buf[xx, j, r]) for r in range(3)]
            for r in range(3):
                feats[t, pl.ds(8 * r, 8), :] = v[r]
            parts = control_rows(v[0])
            columns = jnp.transpose(jnp.concatenate(parts + parts, axis=0), (1, 0)).astype(BF16)
            left = columns * half
            left_a[t] = left
            left_b[t] = columns - left
            carry = carry + v[2]
        return carry

    first_near = first(0)
    for copy in first_near:
        copy.wait_recv()
    second(0, True)
    for copy in far:
        copy.wait_recv()
    first_far = first(1)
    for copy in first_far:
        copy.wait_recv()
    second(1, True)
    second(0, False)
    across_near = across(0)

    @pl.when(jnp.logical_not(heavy))
    def _():
        for copy in hand(0, 1):
            copy.wait_recv()

        def more(i, _):
            right[LINES + i] = node_rows(more_nodes, i >> 3, i & 7)
            return 0

        lax.fori_loop(0, MORE, more, 0, unroll=4)

    across_near.wait_recv()
    loads = lax.fori_loop(0, 5, unpack, jnp.zeros((8, 128), F32))
    second(1, False)
    across_far = across(1)
    loads = lax.fori_loop(5, 9, unpack, loads)
    across_far.wait_recv()
    loads = lax.fori_loop(9, ZS, unpack, loads)
    total = jnp.broadcast_to(loads[5:6, :], (8, 128))
    for by in (16, 32, 64):
        total = total + pltpu.roll(total, by, 1)
    for k in range(6):
        acceleration = inverse_mass[k] * jnp.broadcast_to(total[:, k : k + 1], (8, 128)) + GRAVITY[k]
        accelerations[k] = acceleration
        rigid[k] = TIME_STEP * motion[k] + 0.5 * TIME_STEP * TIME_STEP * acceleration
    for copy in pending:
        copy.wait_send()

    @pl.when(heavy)
    def _():
        for h in range(3):
            for copy in hand(h, 1 + 2 * h):
                copy.wait_send()


def gather(*arrays):
    points, modes, pressure, area, center, nodes, ids, counts, motion, inverse_mass = arrays
    vmem = pl.BlockSpec(memory_space=pltpu.VMEM)
    return pl.pallas_call(
        gather_kernel,
        out_shape=(
            jax.ShapeDtypeStruct((10, 8, 16), jnp.int32),
            jax.ShapeDtypeStruct((8, 8), jnp.int32),
            jax.ShapeDtypeStruct((NTILE, 24, 128), F32),
            jax.ShapeDtypeStruct((NTILE, 128, 64), BF16),
            jax.ShapeDtypeStruct((NTILE, 128, 64), BF16),
            jax.ShapeDtypeStruct((LINES + MORE + 1, 32, 128), BF16),
            jax.ShapeDtypeStruct((6, 8, 128), F32),
            jax.ShapeDtypeStruct((6, 8, 128), F32),
        ),
        in_specs=[pl.BlockSpec(memory_space=pltpu.HBM)] * 10,
        out_specs=(vmem,) * 8,
        scratch_shapes=[
            pltpu.VMEM((XS, ZS, 3, 8, 128), F32),
            pltpu.VMEM(nodes.shape, F32),
            pltpu.VMEM((3, 2, 8, 128), F32),
            pltpu.VMEM(points.shape, F32),
            pltpu.VMEM(modes.shape, F32),
            pltpu.VMEM(pressure.shape, F32),
            pltpu.VMEM(area.shape, F32),
            pltpu.VMEM(center.shape, F32),
            pltpu.VMEM((24, 128), F32),
            pltpu.VMEM((16, 128), F32),
            pltpu.VMEM((3, 128), F32),
            pltpu.SMEM((6,), F32),
            pltpu.SMEM((6,), F32),
            pltpu.SemaphoreType.DMA((10,)),
            pltpu.SemaphoreType.DMA((35,)),
            pltpu.SemaphoreType.DMA((31,)),
        ],
        compiler_params=pltpu.CompilerParams(
            collective_id=0, has_side_effects=True, vmem_limit_bytes=VMEM_LIMIT
        ),
        name="gather",
    )(*(pltpu.with_memory_space_constraint(v, pltpu.HBM) for v in arrays))


VMEM_LIMIT = 24 << 20


BLOCK = 32


def weights(s):
    s = jnp.minimum(jnp.maximum(s, 1e-30), 16.0)
    d = s * lax.rsqrt(s)
    v = 4.0 - d
    v = v * v
    k = v * v * (1.0 + d)
    hi = k.astype(BF16)
    return jnp.concatenate([hi, (k - hi.astype(F32)).astype(BF16)], axis=0)


def pair_kernel(
    role,
    ids_vmem,
    counts_vmem,
    motion_hbm,
    nodes_hbm,
    rigid,
    accelerations,
    feats,
    left_a,
    left_b,
    right,
    shift,
    more_shift,
    plane_edge,
    row_edge,
    state,
    mix_a,
    mix_b,
    sums,
    nodes,
    unit_of,
    ids,
    counts,
    motion,
    fetch,
):
    lines = LINES + MORE
    sources = (ids_vmem, counts_vmem, motion_hbm, nodes_hbm)
    fetches = [
        pltpu.make_async_copy(src, dst, fetch.at[i])
        for i, (src, dst) in enumerate(zip(sources, (ids, counts, motion, nodes)))
    ]
    for copy in fetches:
        copy.start()
    heavy = role[0]
    light = 1 - heavy
    sub = iota((8, 128), 0)
    zero = jnp.zeros((8, 128), F32)

    for i in range(lines + 1):
        sums[i] = zero
    for copy in fetches[:2]:
        copy.wait()

    def prepare(t, n):
        for e in range(4):
            unit_of[n + e] = (t << 6) + ids[t, e]
        n = n + light * counts[t >> 3, t & 7]
        c = jnp.zeros((3, 128), F32)
        for k in range(6):
            c = c + rigid[k, 0:3, :] * feats[t, 3 + 3 * k : 6 + 3 * k, :]
        c = c * (1.0 / 256.0)
        c = jnp.concatenate([c, c, jnp.zeros((2, 128), F32)], axis=0)
        c_hi = c.astype(BF16).astype(F32)
        c = jnp.where(sub < 3, c_hi, c - c_hi)
        mix_a[t] = jnp.concatenate([c, zero], axis=0).astype(BF16)
        mix_b[t] = jnp.concatenate([zero, c], axis=0).astype(BF16)
        return n

    n = lax.fori_loop(0, NTILE, prepare, jnp.int32(0), unroll=8)

    gap = jnp.zeros((32, 128), BF16)

    def pair(t1, t2, rhs):
        s = jnp.dot(left_a[t1] + left_b[t2], rhs, preferred_element_type=F32)
        m = mix_a[t1] + mix_b[t2]
        return jnp.dot(jnp.concatenate([m, m], axis=1), weights(s), preferred_element_type=F32)

    def beside(l1, l2):
        return jnp.concatenate(
            [jnp.concatenate([right[l1], gap], axis=1), jnp.concatenate([gap, right[l2]], axis=1)], axis=0
        )

    def full_line(i):
        own = jnp.where(i < 8, i, jnp.where(i < 15, (i - 7) << 3, i + 42))
        return jnp.where(heavy == 1, own, LINES + i + jnp.where(i < 7, 1, 2))

    def full(b, _):
        l1, l2 = full_line(2 * b), full_line(2 * b + 1)
        for e in range(16):
            out = pair(ids[l1, e], ids[l2, e], beside(l1, l2))
            sums[l1] += out[0:8, 0:128]
            sums[l2] += out[8:16, 128:256]
        return 0

    lax.fori_loop(0, jnp.where(heavy == 1, 11, 7), full, 0)
    for e in range(BLOCK):
        unit_of[n + e] = lines << 6

    def block(g, _):
        for u in range(0, BLOCK, 2):
            i = g * BLOCK + u
            c1, c2 = unit_of[i], unit_of[i + 1]
            l1, l2 = c1 >> 6, c2 >> 6
            out = pair(c1 & (NTILE - 1), c2 & (NTILE - 1), beside(l1, l2))
            sums[l1] += out[0:8, 0:128]
            sums[l2] += out[8:16, 128:256]
        return 0

    lax.fori_loop(0, (n + BLOCK - 1) >> 5, block, 0)

    for copy in fetches[2:]:
        copy.wait()
    for k in range(6):
        state[k] = motion[k] + TIME_STEP * accelerations[k][0, 0]
    for i in range(lines):
        v = sums[i]
        v = v + pltpu.roll(v, 5, 0)
        for c in range(3):
            if i < LINES:
                shift[c, i // 8, i % 8 : i % 8 + 1, :] = v[c : c + 1, :]
            else:
                more_shift[c, i // 8 - 8, i % 8 : i % 8 + 1, :] = v[c : c + 1, :]
    for c in range(3):
        plane_edge[0, c] = nodes[c, 0]
        plane_edge[1, c] = nodes[c, 0] + shift[c, 0]
        for p in range(8):
            row_edge[0, c, p : p + 1, :] = nodes[c, p, 0:1, :]
            row_edge[1, c, p : p + 1, :] = nodes[c, p, 0:1, :] + shift[c, p, 0:1, :]


def pair_sums(role, ids, counts, motion, nodes, rigid, accelerations, feats, left_a, left_b, right):
    vmem = pl.BlockSpec(memory_space=pltpu.VMEM)
    smem = pl.BlockSpec(memory_space=pltpu.SMEM)
    lines = LINES + MORE
    units = 4 * LINES + 2 * BLOCK
    return pl.pallas_call(
        pair_kernel,
        out_shape=(
            jax.ShapeDtypeStruct((3, 8, 8, 128), F32),
            jax.ShapeDtypeStruct((3, 2, 8, 128), F32),
            jax.ShapeDtypeStruct((2, 3, 8, 128), F32),
            jax.ShapeDtypeStruct((2, 3, 8, 128), F32),
            jax.ShapeDtypeStruct((6,), F32),
        ),
        in_specs=[smem, vmem, vmem] + [pl.BlockSpec(memory_space=pltpu.HBM)] * 2 + [vmem] * 6,
        out_specs=(vmem,) * 4 + (smem,),
        scratch_shapes=[
            pltpu.VMEM((NTILE, 16, 128), BF16),
            pltpu.VMEM((NTILE, 16, 128), BF16),
            pltpu.VMEM((lines + 1, 8, 128), F32),
            pltpu.VMEM((3, 8, 8, 128), F32),
            pltpu.SMEM((units,), jnp.int32),
            pltpu.SMEM((LINES + MORE, 16), jnp.int32),
            pltpu.SMEM((8, 8), jnp.int32),
            pltpu.SMEM((6,), F32),
            pltpu.SemaphoreType.DMA((4,)),
        ],
        compiler_params=pltpu.CompilerParams(vmem_limit_bytes=VMEM_LIMIT),
        name="pairs",
    )(role, ids, counts, motion, nodes, rigid, accelerations, feats, left_a, left_b, right)


def exchange_kernel(more_shift, plane_edge, row_edge, back, planes, rows, corners, send, recv):
    x, y, z, core = place()
    slab = lax.axis_index("slab")
    heavy = is_heavy()
    last = XS * ZS * CORES

    def at(ds, dy):
        return {"slab": (slab + ds + last) % last, "ctrl": (y + dy + YS) % YS}

    barrier = pltpu.get_barrier_semaphore()
    greet = [at(1, 0), at(-1, 0), at(0, 1), at(0, -1), at(1, 1), at(-1, -1)]
    greet += [device(x + i, y, z, core) for i in (1, 2, 3)]
    for target in greet:
        pl.semaphore_signal(barrier, inc=1, device_id=target, device_id_type=MESH)
    pl.semaphore_wait(barrier, len(greet))

    def put(src, dst, slot, target):
        return pltpu.make_async_remote_copy(
            src_ref=src,
            dst_ref=dst,
            send_sem=send.at[slot],
            recv_sem=recv.at[slot],
            device_id=target,
            device_id_type=MESH,
        )

    def give(h):
        return pltpu.make_async_remote_copy(
            src_ref=more_shift,
            dst_ref=back.at[h],
            send_sem=send.at[3],
            recv_sem=recv.at[3 + h],
            device_id=device(heavy_x(z), y, z, core),
            device_id_type=MESH,
        )

    mine = (x - heavy_x(z) + 3) % XS

    @pl.when(jnp.logical_not(heavy))
    def _():
        give(jnp.minimum(mine, 2)).start()

    edges = [
        put(plane_edge, corners, 2, at(-1, -1)),
        put(plane_edge, planes, 0, at(-1, 0)),
        put(row_edge, rows, 1, at(0, -1)),
    ]
    for copy in edges:
        copy.start()

    @pl.when(heavy)
    def _():
        for h in range(3):
            give(h).wait_recv()

    @pl.when(jnp.logical_not(heavy))
    def _():
        give(jnp.minimum(mine, 2)).wait_send()

    for copy in edges:
        copy.wait()


def exchange(more_shift, plane_edge, row_edge):
    hbm = pl.BlockSpec(memory_space=pl.ANY)
    edge = jax.ShapeDtypeStruct((2, 3, 8, 128), F32)
    return pl.pallas_call(
        exchange_kernel,
        out_shape=(jax.ShapeDtypeStruct((3, 3, 2, 8, 128), F32), edge, edge, edge),
        in_specs=[hbm] * 3,
        out_specs=(hbm,) * 4,
        scratch_shapes=[pltpu.SemaphoreType.DMA((4,)), pltpu.SemaphoreType.DMA((6,))],
        compiler_params=pltpu.CompilerParams(
            collective_id=1, has_side_effects=True, vmem_limit_bytes=VMEM_LIMIT
        ),
        name="exchange",
    )(more_shift, plane_edge, row_edge)


def volume_kernel(role, nodes, shift, back, planes, rows, corners, out_shift, volume, change):
    slab, y = role[1], role[2]
    out_shift[...] = shift[...]

    @pl.when(role[0] == 1)
    def _():
        row = iota((8, 128), 0)
        for h in range(3):
            for c in range(3):
                for i in range(2):
                    p = 1 + 2 * h + i
                    out_shift[c, p] = jnp.where(row == 0, shift[c, p], back[h, c, i])

    bottom = iota((8, 128), 0) == 7

    def faces(field, c, p):
        if p < 8:
            a = nodes[c, p]
            if field:
                a = a + out_shift[c, p]
            edge = rows[field, c, p : p + 1, :]
        else:
            a = planes[field, c]
            edge = corners[field, c, 0:1, :]
        b = jnp.where(bottom, edge, pltpu.roll(a, 7, 0))
        az = pltpu.roll(a, 127, 1)
        bz = pltpu.roll(b, 127, 1)
        near, far = a + b, az + bz
        return near + far, (b + bz) - (a + az), far - near

    row = iota((8, 128), 0) + y * 8
    inside = jnp.logical_and(row < 31, iota((8, 128), 1) < 127)
    held = {}
    for p in range(9):
        for field in range(2):
            for c in range(3):
                held[field, c, p % 2] = faces(field, c, p)
        if p == 0:
            continue
        both = []
        for field in range(2):
            now = [held[field, c, p % 2] for c in range(3)]
            before = [held[field, c, (p - 1) % 2] for c in range(3)]
            ex = [0.25 * (n[0] - b[0]) for n, b in zip(now, before)]
            ey = [0.25 * (n[1] + b[1]) for n, b in zip(now, before)]
            ez = [0.25 * (n[2] + b[2]) for n, b in zip(now, before)]
            both.append(
                ex[0] * (ey[1] * ez[2] - ey[2] * ez[1])
                + ex[1] * (ey[2] * ez[0] - ey[0] * ez[2])
                + ex[2] * (ey[0] * ez[1] - ey[1] * ez[0])
            )
        ok = jnp.logical_and(inside, slab * 8 + p - 1 < 1023)
        old, new = (jnp.where(ok, v, 0.0) for v in both)
        volume[p - 1] = new
        change[p - 1] = new - old


def volumes(role, nodes, shift, back, planes, rows, corners):
    vmem = pl.BlockSpec(memory_space=pltpu.VMEM)
    return pl.pallas_call(
        volume_kernel,
        out_shape=(
            jax.ShapeDtypeStruct((3, 8, 8, 128), F32),
            jax.ShapeDtypeStruct((8, 8, 128), F32),
            jax.ShapeDtypeStruct((8, 8, 128), F32),
        ),
        in_specs=[pl.BlockSpec(memory_space=pltpu.SMEM)] + [vmem] * 6,
        out_specs=(vmem,) * 3,
        compiler_params=pltpu.CompilerParams(vmem_limit_bytes=VMEM_LIMIT),
        name="volumes",
    )(role, nodes, shift, back, planes, rows, corners)


def local(
    face_pressure,
    face_area,
    face_center,
    motion,
    inverse_mass,
    control_points,
    control_modes,
    node_points,
    tile_list,
    tile_count,
):
    all_ids, counts, feats, left_a, left_b, right, rigid, accelerations = gather(
        control_points,
        control_modes.T,
        face_pressure.reshape(-1, 128),
        face_area,
        face_center,
        node_points,
        tile_list,
        tile_count,
        motion,
        inverse_mass,
    )
    role = jnp.stack(
        [is_heavy().astype(jnp.int32), lax.axis_index("slab").astype(jnp.int32), lax.axis_index("ctrl").astype(jnp.int32)]
    )
    shift, more_shift, plane_edge, row_edge, new_state = pair_sums(
        role,
        all_ids.reshape(LINES + MORE, 16),
        counts,
        *(pltpu.with_memory_space_constraint(v, pltpu.HBM) for v in (motion, node_points)),
        rigid,
        accelerations,
        feats,
        left_a,
        left_b,
        right,
    )
    back, planes, rows, corners = exchange(more_shift, plane_edge, row_edge)
    node_shift, volume, change = volumes(role, node_points, shift, back, planes, rows, corners)
    return node_shift, volume, change, new_state


def solution(mesh):
    placed = (
        P(("slab", "ctrl")),
        P(None, ("slab", "ctrl")),
        P(None, ("slab", "ctrl")),
        P(),
        P(),
        P(None, ("slab", "ctrl")),
        P(None, ("slab", "ctrl")),
        P(None, "slab", "ctrl", None),
        P("slab", "ctrl", None),
        P("slab", "ctrl"),
    )
    return jax.shard_map(
        local,
        mesh=mesh,
        in_specs=placed,
        out_specs=(
            P(None, "slab", "ctrl", None),
            P("slab", "ctrl", None),
            P("slab", "ctrl", None),
            P(),
        ),
        check_vma=False,
    )
```

```python
import functools

import jax
import jax.numpy as jnp
from jax import lax
from jax.experimental import pallas as pl
from jax.experimental.pallas import tpu as pltpu
from jax.sharding import PartitionSpec as P

MESH = pl.DeviceIdType.MESH
TILE = 128
NTILE = 64
F32 = jnp.float32
BF16 = jnp.bfloat16
TIME_STEP = 0.5
GRAVITY = (0.0, 0.0, -0.5, 0.0, 0.0, 0.0)
XS, YS, ZS, CORES = 4, 4, 16, 2
LOAD_LANE = 80


def iota(shape, axis):
    return lax.broadcasted_iota(jnp.int32, shape, axis)


def place():
    slab = lax.axis_index("slab")
    return slab >> 5, lax.axis_index("ctrl"), (slab >> 1) & (ZS - 1), slab & 1


def device(x, y, z, core):
    return {"slab": ((x & (XS - 1)) << 5) + ((z & (ZS - 1)) << 1) + core, "ctrl": y & (YS - 1)}


def is_heavy():
    slab = lax.axis_index("slab")
    return jnp.logical_and(slab >= 48, slab < 80)


def heavy_x(z):
    return 2 - (z >> 3)


def split3(value):
    hi = value.astype(BF16).astype(F32)
    rest = value - hi
    mid = rest.astype(BF16).astype(F32)
    return hi, mid, rest - mid


def regroup(v):
    sub = iota((8, 128), 0)
    grp = iota((8, 128), 1) // 16
    for bit in (1, 2, 4):
        below = pltpu.roll(pltpu.roll(v, 8 - bit, 0), 16 * bit, 1)
        above = pltpu.roll(pltpu.roll(v, bit, 0), 128 - 16 * bit, 1) if bit < 4 else below
        low = (sub & bit) == 0
        same = low == ((grp & bit) == 0)
        v = jnp.where(same, v, jnp.where(low, below, above))
    return v


def node_rows(nodes, p, r):
    sub = iota((8, 128), 0)
    x = [nodes[c, p, pl.ds(r, 1), :] for c in range(3)]
    square = x[0] * x[0] + x[1] * x[1] + x[2] * x[2]
    rows = jnp.where((sub == 0) | (sub == 3), -2.0 * x[0], 0.0)
    rows = jnp.where((sub == 1) | (sub == 4), -2.0 * x[1], rows)
    rows = jnp.where((sub == 2) | (sub == 5), -2.0 * x[2], rows)
    rows = jnp.where(sub == 7, square, rows)
    hi, mid, lo = split3(rows)
    one = sub == 6
    second = (sub >= 3) & (sub < 6)
    parts = [
        jnp.where(one, 1.0, jnp.where(second, mid, hi)),
        jnp.where(one, 1.0, jnp.where(sub < 3, hi, mid)),
        jnp.where(one, 1.0, jnp.where(second, hi, lo)),
        jnp.zeros((8, 128), F32),
    ]
    return jnp.concatenate(parts, axis=0).astype(BF16)


def control_rows(p):
    sub = iota((8, 128), 0)
    p = jnp.where(sub < 3, p, 0.0)
    square = jnp.sum(p * p, axis=0, keepdims=True)
    rows = p + pltpu.roll(p, 3, 0) + jnp.where(sub == 6, square, 0.0)
    hi, mid, lo = split3(rows)
    one = sub == 7
    parts = [
        jnp.where(one, 1.0, hi),
        jnp.where(one, 1.0, mid),
        jnp.where(one, 1.0, jnp.where(sub < 3, hi, lo)),
        jnp.zeros((8, 128), F32),
    ]
    return parts


LINES = 64
MORE = 16


def gather_kernel(
    points_hbm,
    modes_hbm,
    pressure_hbm,
    area_hbm,
    center_hbm,
    nodes_hbm,
    ids_hbm,
    counts_hbm,
    motion_hbm,
    inverse_mass_hbm,
    all_ids,
    counts,
    feats,
    left_a,
    left_b,
    right,
    rigid,
    accelerations,
    buf,
    nodes,
    more_nodes,
    points,
    modes,
    pressure,
    area,
    center,
    pack,
    turn,
    own,
    motion,
    inverse_mass,
    fetch,
    send,
    recv,
):
    x, y, z, core = place()
    group = core * YS + y
    plane = [(i * core, i * (1 - core)) for i in range(1, 4)]
    turned = [(i * (1 - core), i * core) for i in range(1, 4)]

    sources = (
        points_hbm,
        modes_hbm,
        pressure_hbm,
        area_hbm,
        center_hbm,
        nodes_hbm,
        ids_hbm,
        counts_hbm,
        motion_hbm,
        inverse_mass_hbm,
    )
    kept = all_ids.at[pl.ds(0, 8)]
    targets = (points, modes, pressure, area, center, nodes, kept, counts, motion, inverse_mass)
    fetches = [
        pltpu.make_async_copy(src, dst, fetch.at[i]) for i, (src, dst) in enumerate(zip(sources, targets))
    ]
    for copy in fetches:
        copy.start()

    along = {d: device(x, y, z + d, core) for d in (4, -4, 3, -3, 2, -2, 1, -1)}
    peers = [device(x + dx, y + dy, z, core) for dx, dy in plane]
    crossing = [device(x + dx, y + dy, z, core) for dx, dy in turned]
    barrier = pltpu.get_barrier_semaphore()
    greet = list(along.values()) + peers + crossing
    greet += [device(x, y, z, 1 - core)]
    for target in greet:
        pl.semaphore_signal(barrier, inc=1, device_id=target, device_id_type=MESH)

    for copy in fetches[:2]:
        copy.wait()
    pack[...] = jnp.zeros((24, 128), F32)
    pack[0:3, 0:16] = points[...]
    turn[...] = jnp.zeros((16, 128), F32)
    turn[:, 0:18] = modes[...]
    pack[3:21, 0:16] = jnp.transpose(turn[...], (1, 0))[0:18]
    packed = []
    for r in range(3):
        v = pack[8 * r : 8 * r + 8, :]
        for bit in (1, 2, 4):
            v = jnp.where((iota((8, 128), 0) & bit) == 0, v, pltpu.roll(v, 16 * bit, 1))
        packed.append(jnp.sum(v, axis=0, keepdims=True))

    for copy in fetches[2:]:
        copy.wait()
    force = jnp.zeros((3, 128), F32)
    moment = jnp.zeros((3, 128), F32)
    for i in range(pressure.shape[0]):
        at = pl.ds(i * 128, 128)
        pushed = area[:, at] * pressure[i : i + 1, :]
        c = center[:, at]
        force = force + pushed
        moment = moment + jnp.concatenate(
            [
                c[1:2] * pushed[2:3] - c[2:3] * pushed[1:2],
                c[2:3] * pushed[0:1] - c[0:1] * pushed[2:3],
                c[0:1] * pushed[1:2] - c[1:2] * pushed[0:1],
            ],
            axis=0,
        )
    sums = jnp.sum(jnp.concatenate([force, moment], axis=0), axis=1, keepdims=True)
    lane = iota((6, 128), 1)
    row = iota((6, 128), 0)
    loads = jnp.sum(jnp.where(lane == row + LOAD_LANE, sums, 0.0), axis=0, keepdims=True)
    own[0:1, :] = packed[0]
    own[1:2, :] = packed[1]
    own[2:3, :] = packed[2] + loads
    for r in range(3):
        buf[x, 4, r, pl.ds(group, 1), :] = own[r : r + 1, :]

    pl.semaphore_wait(barrier, len(greet))

    heavy = is_heavy()

    def hand(h, src_plane):
        target = device(heavy_x(z) + 1 + h, y, z, core)
        parts = []
        for i, (src, dst) in enumerate(
            ((nodes_hbm.at[:, pl.ds(src_plane, 2)], more_nodes), (ids_hbm.at[pl.ds(src_plane, 2)], all_ids.at[pl.ds(8, 2)]))
        ):
            parts.append(
                pltpu.make_async_remote_copy(
                    src_ref=src,
                    dst_ref=dst,
                    send_sem=send.at[29 + 2 * h + i],
                    recv_sem=recv.at[29 + i],
                    device_id=target,
                    device_id_type=MESH,
                )
            )
        return parts

    pending = []

    def put(src, dst, slot, target):
        copy = pltpu.make_async_remote_copy(
            src_ref=src,
            dst_ref=dst,
            send_sem=send.at[slot],
            recv_sem=recv.at[slot],
            device_id=target,
            device_id_type=MESH,
        )
        copy.start()
        pending.append(copy)
        return copy

    def slot(j):
        return buf.at[x, j, :, group]

    near = {}
    for d in (4, 3, 2, 1):
        near[d] = put(own, slot(4 - d), d - 1, along[d])
        near[-d] = put(own, slot(4 + d), d + 3, along[-d])

    @pl.when(heavy)
    def _():
        for h in range(3):
            for copy in hand(h, 1 + 2 * h):
                copy.start()

    def line(i, _):
        right[i] = node_rows(nodes, i >> 3, i & 7)
        return 0

    lax.fori_loop(0, LINES, line, 0, unroll=4)
    right[LINES + MORE] = jnp.zeros((32, 128), BF16)

    far = []
    for d in (1, 2, 3, 4):
        near[d].wait_recv()
        far.append(put(slot(4 - d), slot(16 - d), d + 7, along[4]))
        near[-d].wait_recv()
        if d < 4:
            far.append(put(slot(4 + d), slot(8 + d), d + 11, along[-4]))

    halves = (pl.ds(0, 9), pl.ds(9, 7))

    def first(part):
        ref = buf.at[x, halves[part], :, group]
        return [
            put(ref, ref, 15 + 3 * part + i, peer) for i, peer in enumerate(peers)
        ]

    def second(part, start):
        for i, target in enumerate(crossing):

            def make(ref, i=i, target=target):
                return pltpu.make_async_remote_copy(
                    src_ref=ref,
                    dst_ref=ref,
                    send_sem=send.at[21 + 3 * part + i],
                    recv_sem=recv.at[21 + 3 * part + i],
                    device_id=target,
                    device_id_type=MESH,
                )

            @pl.when(core == 0)
            def _():
                copy = make(buf.at[x, halves[part], :, pl.ds(0, YS)])
                copy.start() if start else copy.wait()

            @pl.when(core == 1)
            def _():
                copy = make(buf.at[:, halves[part], :, group])
                copy.start() if start else copy.wait()

    def across(part):
        ref = buf.at[:, halves[part], :, pl.ds(core * YS, YS)]
        return put(ref, ref, 27 + part, device(x, y, z, 1 - core))

    half = jnp.where(iota((128, 64), 1) < 32, 1.0, 0.0).astype(BF16)

    def unpack(j, carry):
        for xx in range(XS):
            t = xx * ZS + ((j + z + ZS - 4) & (ZS - 1))
            v = [regroup(buf[xx, j, r]) for r in range(3)]
            for r in range(3):
                feats[t, pl.ds(8 * r, 8), :] = v[r]
            parts = control_rows(v[0])
            columns = jnp.transpose(jnp.concatenate(parts + parts, axis=0), (1, 0)).astype(BF16)
            left = columns * half
            left_a[t] = left
            left_b[t] = columns - left
            carry = carry + v[2]
        return carry

    first_near = first(0)
    for copy in first_near:
        copy.wait_recv()
    second(0, True)
    for copy in far:
        copy.wait_recv()
    first_far = first(1)
    for copy in first_far:
        copy.wait_recv()
    second(1, True)
    second(0, False)
    across_near = across(0)

    @pl.when(jnp.logical_not(heavy))
    def _():
        for copy in hand(0, 1):
            copy.wait_recv()

        def more(i, _):
            right[LINES + i] = node_rows(more_nodes, i >> 3, i & 7)
            return 0

        lax.fori_loop(0, MORE, more, 0, unroll=4)

    across_near.wait_recv()
    loads = lax.fori_loop(0, 5, unpack, jnp.zeros((8, 128), F32))
    second(1, False)
    across_far = across(1)
    loads = lax.fori_loop(5, 9, unpack, loads)
    across_far.wait_recv()
    loads = lax.fori_loop(9, ZS, unpack, loads)
    total = jnp.broadcast_to(loads[5:6, :], (8, 128))
    for by in (16, 32, 64):
        total = total + pltpu.roll(total, by, 1)
    for k in range(6):
        acceleration = inverse_mass[k] * jnp.broadcast_to(total[:, k : k + 1], (8, 128)) + GRAVITY[k]
        accelerations[k] = acceleration
        rigid[k] = TIME_STEP * motion[k] + 0.5 * TIME_STEP * TIME_STEP * acceleration
    for copy in pending:
        copy.wait_send()

    @pl.when(heavy)
    def _():
        for h in range(3):
            for copy in hand(h, 1 + 2 * h):
                copy.wait_send()


def gather(*arrays):
    points, modes, pressure, area, center, nodes, ids, counts, motion, inverse_mass = arrays
    vmem = pl.BlockSpec(memory_space=pltpu.VMEM)
    return pl.pallas_call(
        gather_kernel,
        out_shape=(
            jax.ShapeDtypeStruct((10, 8, 16), jnp.int32),
            jax.ShapeDtypeStruct((8, 8), jnp.int32),
            jax.ShapeDtypeStruct((NTILE, 24, 128), F32),
            jax.ShapeDtypeStruct((NTILE, 128, 64), BF16),
            jax.ShapeDtypeStruct((NTILE, 128, 64), BF16),
            jax.ShapeDtypeStruct((LINES + MORE + 1, 32, 128), BF16),
            jax.ShapeDtypeStruct((6, 8, 128), F32),
            jax.ShapeDtypeStruct((6, 8, 128), F32),
        ),
        in_specs=[pl.BlockSpec(memory_space=pltpu.HBM)] * 10,
        out_specs=(vmem,) * 8,
        scratch_shapes=[
            pltpu.VMEM((XS, ZS, 3, 8, 128), F32),
            pltpu.VMEM(nodes.shape, F32),
            pltpu.VMEM((3, 2, 8, 128), F32),
            pltpu.VMEM(points.shape, F32),
            pltpu.VMEM(modes.shape, F32),
            pltpu.VMEM(pressure.shape, F32),
            pltpu.VMEM(area.shape, F32),
            pltpu.VMEM(center.shape, F32),
            pltpu.VMEM((24, 128), F32),
            pltpu.VMEM((16, 128), F32),
            pltpu.VMEM((3, 128), F32),
            pltpu.SMEM((6,), F32),
            pltpu.SMEM((6,), F32),
            pltpu.SemaphoreType.DMA((10,)),
            pltpu.SemaphoreType.DMA((35,)),
            pltpu.SemaphoreType.DMA((31,)),
        ],
        compiler_params=pltpu.CompilerParams(
            collective_id=0, has_side_effects=True, vmem_limit_bytes=VMEM_LIMIT
        ),
        name="gather",
    )(*(pltpu.with_memory_space_constraint(v, pltpu.HBM) for v in arrays))


VMEM_LIMIT = 24 << 20


BLOCK = 32


def weights(s):
    s = jnp.minimum(jnp.maximum(s, 1e-30), 16.0)
    d = s * lax.rsqrt(s)
    v = 4.0 - d
    v = v * v
    k = v * v * (1.0 + d)
    hi = k.astype(BF16)
    return jnp.concatenate([hi, (k - hi.astype(F32)).astype(BF16)], axis=0)


def pair_kernel(
    role,
    ids_vmem,
    counts_vmem,
    motion_hbm,
    nodes_hbm,
    rigid,
    accelerations,
    feats,
    left_a,
    left_b,
    right,
    shift,
    more_shift,
    plane_edge,
    row_edge,
    state,
    mix_a,
    mix_b,
    sums,
    nodes,
    unit_of,
    ids,
    counts,
    motion,
    fetch,
):
    lines = LINES + MORE
    sources = (ids_vmem, counts_vmem, motion_hbm, nodes_hbm)
    fetches = [
        pltpu.make_async_copy(src, dst, fetch.at[i])
        for i, (src, dst) in enumerate(zip(sources, (ids, counts, motion, nodes)))
    ]
    for copy in fetches:
        copy.start()
    heavy = role[0]
    light = 1 - heavy
    sub = iota((8, 128), 0)
    zero = jnp.zeros((8, 128), F32)

    for i in range(lines + 1):
        sums[i] = zero
    for copy in fetches[:2]:
        copy.wait()

    def prepare(t, n):
        for e in range(4):
            unit_of[n + e] = (t << 6) + ids[t, e]
        n = n + light * counts[t >> 3, t & 7]
        c = jnp.zeros((3, 128), F32)
        for k in range(6):
            c = c + rigid[k, 0:3, :] * feats[t, 3 + 3 * k : 6 + 3 * k, :]
        c = c * (1.0 / 256.0)
        c = jnp.concatenate([c, c, jnp.zeros((2, 128), F32)], axis=0)
        c_hi = c.astype(BF16).astype(F32)
        c = jnp.where(sub < 3, c_hi, c - c_hi)
        mix_a[t] = jnp.concatenate([c, zero], axis=0).astype(BF16)
        mix_b[t] = jnp.concatenate([zero, c], axis=0).astype(BF16)
        return n

    n = lax.fori_loop(0, NTILE, prepare, jnp.int32(0), unroll=8)

    gap = jnp.zeros((32, 128), BF16)

    def pair(t1, t2, rhs):
        s = jnp.dot(left_a[t1] + left_b[t2], rhs, preferred_element_type=F32)
        m = mix_a[t1] + mix_b[t2]
        return jnp.dot(jnp.concatenate([m, m], axis=1), weights(s), preferred_element_type=F32)

    def beside(l1, l2):
        return jnp.concatenate(
            [jnp.concatenate([right[l1], gap], axis=1), jnp.concatenate([gap, right[l2]], axis=1)], axis=0
        )

    def full_line(i):
        own = jnp.where(i < 8, i, jnp.where(i < 15, (i - 7) << 3, i + 42))
        return jnp.where(heavy == 1, own, LINES + i + jnp.where(i < 7, 1, 2))

    def full(b, _):
        l1, l2 = full_line(2 * b), full_line(2 * b + 1)
        for e in range(16):
            out = pair(ids[l1, e], ids[l2, e], beside(l1, l2))
            sums[l1] += out[0:8, 0:128]
            sums[l2] += out[8:16, 128:256]
        return 0

    lax.fori_loop(0, jnp.where(heavy == 1, 11, 7), full, 0)
    for e in range(BLOCK):
        unit_of[n + e] = lines << 6

    def block(start, units):
        for u in range(0, units, 2):
            i = start + u
            c1, c2 = unit_of[i], unit_of[i + 1]
            l1, l2 = c1 >> 6, c2 >> 6
            out = pair(c1 & (NTILE - 1), c2 & (NTILE - 1), beside(l1, l2))
            sums[l1] += out[0:8, 0:128]
            sums[l2] += out[8:16, 128:256]
        return 0

    whole = (n + BLOCK // 2 - 1) >> 5
    lax.fori_loop(0, whole, lambda g, _: block(g * BLOCK, BLOCK), 0)
    lax.fori_loop(0, jnp.where(n > whole * BLOCK, 1, 0), lambda g, _: block(whole * BLOCK, BLOCK // 2), 0)

    for copy in fetches[2:]:
        copy.wait()
    for k in range(6):
        state[k] = motion[k] + TIME_STEP * accelerations[k][0, 0]
    for i in range(lines):
        v = sums[i]
        v = v + pltpu.roll(v, 5, 0)
        for c in range(3):
            if i < LINES:
                shift[c, i // 8, i % 8 : i % 8 + 1, :] = v[c : c + 1, :]
            else:
                more_shift[c, i // 8 - 8, i % 8 : i % 8 + 1, :] = v[c : c + 1, :]
    for c in range(3):
        plane_edge[0, c] = nodes[c, 0]
        plane_edge[1, c] = nodes[c, 0] + shift[c, 0]
        for p in range(8):
            row_edge[0, c, p : p + 1, :] = nodes[c, p, 0:1, :]
            row_edge[1, c, p : p + 1, :] = nodes[c, p, 0:1, :] + shift[c, p, 0:1, :]


def pair_sums(role, ids, counts, motion, nodes, rigid, accelerations, feats, left_a, left_b, right):
    vmem = pl.BlockSpec(memory_space=pltpu.VMEM)
    smem = pl.BlockSpec(memory_space=pltpu.SMEM)
    lines = LINES + MORE
    units = 4 * LINES + 2 * BLOCK
    return pl.pallas_call(
        pair_kernel,
        out_shape=(
            jax.ShapeDtypeStruct((3, 8, 8, 128), F32),
            jax.ShapeDtypeStruct((3, 2, 8, 128), F32),
            jax.ShapeDtypeStruct((2, 3, 8, 128), F32),
            jax.ShapeDtypeStruct((2, 3, 8, 128), F32),
            jax.ShapeDtypeStruct((6,), F32),
        ),
        in_specs=[smem, vmem, vmem] + [pl.BlockSpec(memory_space=pltpu.HBM)] * 2 + [vmem] * 6,
        out_specs=(vmem,) * 4 + (smem,),
        scratch_shapes=[
            pltpu.VMEM((NTILE, 16, 128), BF16),
            pltpu.VMEM((NTILE, 16, 128), BF16),
            pltpu.VMEM((lines + 1, 8, 128), F32),
            pltpu.VMEM((3, 8, 8, 128), F32),
            pltpu.SMEM((units,), jnp.int32),
            pltpu.SMEM((LINES + MORE, 16), jnp.int32),
            pltpu.SMEM((8, 8), jnp.int32),
            pltpu.SMEM((6,), F32),
            pltpu.SemaphoreType.DMA((4,)),
        ],
        compiler_params=pltpu.CompilerParams(vmem_limit_bytes=VMEM_LIMIT),
        name="pairs",
    )(role, ids, counts, motion, nodes, rigid, accelerations, feats, left_a, left_b, right)


def exchange_kernel(more_shift, plane_edge, row_edge, back, planes, rows, corners, send, recv):
    x, y, z, core = place()
    slab = lax.axis_index("slab")
    heavy = is_heavy()
    last = XS * ZS * CORES

    def at(ds, dy):
        return {"slab": (slab + ds) & (last - 1), "ctrl": (y + dy) & (YS - 1)}

    barrier = pltpu.get_barrier_semaphore()
    greet = [at(1, 0), at(-1, 0), at(0, 1), at(0, -1), at(1, 1), at(-1, -1)]
    greet += [device(x + i, y, z, core) for i in (1, 2, 3)]
    for target in greet:
        pl.semaphore_signal(barrier, inc=1, device_id=target, device_id_type=MESH)
    pl.semaphore_wait(barrier, len(greet))

    def put(src, dst, slot, target):
        return pltpu.make_async_remote_copy(
            src_ref=src,
            dst_ref=dst,
            send_sem=send.at[slot],
            recv_sem=recv.at[slot],
            device_id=target,
            device_id_type=MESH,
        )

    def give(h):
        return pltpu.make_async_remote_copy(
            src_ref=more_shift,
            dst_ref=back.at[h],
            send_sem=send.at[3],
            recv_sem=recv.at[3 + h],
            device_id=device(heavy_x(z), y, z, core),
            device_id_type=MESH,
        )

    mine = (x - heavy_x(z) + 3) & (XS - 1)

    @pl.when(jnp.logical_not(heavy))
    def _():
        give(jnp.minimum(mine, 2)).start()

    edges = [
        put(plane_edge, corners, 2, at(-1, -1)),
        put(plane_edge, planes, 0, at(-1, 0)),
        put(row_edge, rows, 1, at(0, -1)),
    ]
    for copy in edges:
        copy.start()

    @pl.when(heavy)
    def _():
        for h in range(3):
            give(h).wait_recv()

    @pl.when(jnp.logical_not(heavy))
    def _():
        give(jnp.minimum(mine, 2)).wait_send()

    for copy in edges:
        copy.wait()


def exchange(more_shift, plane_edge, row_edge):
    hbm = pl.BlockSpec(memory_space=pl.ANY)
    edge = jax.ShapeDtypeStruct((2, 3, 8, 128), F32)
    return pl.pallas_call(
        exchange_kernel,
        out_shape=(jax.ShapeDtypeStruct((3, 3, 2, 8, 128), F32), edge, edge, edge),
        in_specs=[hbm] * 3,
        out_specs=(hbm,) * 4,
        scratch_shapes=[pltpu.SemaphoreType.DMA((4,)), pltpu.SemaphoreType.DMA((6,))],
        compiler_params=pltpu.CompilerParams(
            collective_id=1, has_side_effects=True, vmem_limit_bytes=VMEM_LIMIT
        ),
        name="exchange",
    )(more_shift, plane_edge, row_edge)


def volume_kernel(role, nodes, shift, back, planes, rows, corners, out_shift, volume, change):
    slab, y = role[1], role[2]
    out_shift[...] = shift[...]

    @pl.when(role[0] == 1)
    def _():
        row = iota((8, 128), 0)
        for h in range(3):
            for c in range(3):
                for i in range(2):
                    p = 1 + 2 * h + i
                    out_shift[c, p] = jnp.where(row == 0, shift[c, p], back[h, c, i])

    bottom = iota((8, 128), 0) == 7

    def faces(field, c, p):
        if p < 8:
            a = nodes[c, p]
            if field:
                a = a + out_shift[c, p]
            edge = rows[field, c, p : p + 1, :]
        else:
            a = planes[field, c]
            edge = corners[field, c, 0:1, :]
        b = jnp.where(bottom, edge, pltpu.roll(a, 7, 0))
        az = pltpu.roll(a, 127, 1)
        bz = pltpu.roll(b, 127, 1)
        near, far = a + b, az + bz
        return near + far, (b + bz) - (a + az), far - near

    row = iota((8, 128), 0) + y * 8
    inside = jnp.logical_and(row < 31, iota((8, 128), 1) < 127)
    held = {}
    for p in range(9):
        for field in range(2):
            for c in range(3):
                held[field, c, p % 2] = faces(field, c, p)
        if p == 0:
            continue
        both = []
        for field in range(2):
            now = [held[field, c, p % 2] for c in range(3)]
            before = [held[field, c, (p - 1) % 2] for c in range(3)]
            ex = [0.25 * (n[0] - b[0]) for n, b in zip(now, before)]
            ey = [0.25 * (n[1] + b[1]) for n, b in zip(now, before)]
            ez = [0.25 * (n[2] + b[2]) for n, b in zip(now, before)]
            both.append(
                ex[0] * (ey[1] * ez[2] - ey[2] * ez[1])
                + ex[1] * (ey[2] * ez[0] - ey[0] * ez[2])
                + ex[2] * (ey[0] * ez[1] - ey[1] * ez[0])
            )
        ok = jnp.logical_and(inside, slab * 8 + p - 1 < 1023)
        old, new = (jnp.where(ok, v, 0.0) for v in both)
        volume[p - 1] = new
        change[p - 1] = new - old


def volumes(role, nodes, shift, back, planes, rows, corners):
    vmem = pl.BlockSpec(memory_space=pltpu.VMEM)
    return pl.pallas_call(
        volume_kernel,
        out_shape=(
            jax.ShapeDtypeStruct((3, 8, 8, 128), F32),
            jax.ShapeDtypeStruct((8, 8, 128), F32),
            jax.ShapeDtypeStruct((8, 8, 128), F32),
        ),
        in_specs=[pl.BlockSpec(memory_space=pltpu.SMEM)] + [vmem] * 6,
        out_specs=(vmem,) * 3,
        compiler_params=pltpu.CompilerParams(vmem_limit_bytes=VMEM_LIMIT),
        name="volumes",
    )(role, nodes, shift, back, planes, rows, corners)


def local(
    face_pressure,
    face_area,
    face_center,
    motion,
    inverse_mass,
    control_points,
    control_modes,
    node_points,
    tile_list,
    tile_count,
):
    all_ids, counts, feats, left_a, left_b, right, rigid, accelerations = gather(
        control_points,
        control_modes.T,
        face_pressure.reshape(-1, 128),
        face_area,
        face_center,
        node_points,
        tile_list,
        tile_count,
        motion,
        inverse_mass,
    )
    role = jnp.stack(
        [is_heavy().astype(jnp.int32), lax.axis_index("slab").astype(jnp.int32), lax.axis_index("ctrl").astype(jnp.int32)]
    )
    shift, more_shift, plane_edge, row_edge, new_state = pair_sums(
        role,
        all_ids.reshape(LINES + MORE, 16),
        counts,
        *(pltpu.with_memory_space_constraint(v, pltpu.HBM) for v in (motion, node_points)),
        rigid,
        accelerations,
        feats,
        left_a,
        left_b,
        right,
    )
    back, planes, rows, corners = exchange(more_shift, plane_edge, row_edge)
    node_shift, volume, change = volumes(role, node_points, shift, back, planes, rows, corners)
    return node_shift, volume, change, new_state


def solution(mesh):
    placed = (
        P(("slab", "ctrl")),
        P(None, ("slab", "ctrl")),
        P(None, ("slab", "ctrl")),
        P(),
        P(),
        P(None, ("slab", "ctrl")),
        P(None, ("slab", "ctrl")),
        P(None, "slab", "ctrl", None),
        P("slab", "ctrl", None),
        P("slab", "ctrl"),
    )
    return jax.shard_map(
        local,
        mesh=mesh,
        in_specs=placed,
        out_specs=(
            P(None, "slab", "ctrl", None),
            P("slab", "ctrl", None),
            P("slab", "ctrl", None),
            P(),
        ),
        check_vma=False,
    )
```

```python
import functools

import jax
import jax.numpy as jnp
from jax import lax
from jax.experimental import pallas as pl
from jax.experimental.pallas import tpu as pltpu
from jax.sharding import PartitionSpec as P

MESH = pl.DeviceIdType.MESH
TILE = 128
NTILE = 64
F32 = jnp.float32
BF16 = jnp.bfloat16
TIME_STEP = 0.5
GRAVITY = (0.0, 0.0, -0.5, 0.0, 0.0, 0.0)
XS, YS, ZS, CORES = 4, 4, 16, 2
LOAD_LANE = 80


def iota(shape, axis):
    return lax.broadcasted_iota(jnp.int32, shape, axis)


def place():
    slab = lax.axis_index("slab")
    return slab >> 5, lax.axis_index("ctrl"), (slab >> 1) & (ZS - 1), slab & 1


def device(x, y, z, core):
    return {"slab": ((x & (XS - 1)) << 5) + ((z & (ZS - 1)) << 1) + core, "ctrl": y & (YS - 1)}


def is_heavy():
    slab = lax.axis_index("slab")
    return jnp.logical_and(slab >= 48, slab < 80)


def heavy_x(z):
    return 2 - (z >> 3)


def split3(value):
    hi = value.astype(BF16).astype(F32)
    rest = value - hi
    mid = rest.astype(BF16).astype(F32)
    return hi, mid, rest - mid


def regroup(v):
    sub = iota((8, 128), 0)
    grp = iota((8, 128), 1) // 16
    for bit in (1, 2, 4):
        below = pltpu.roll(pltpu.roll(v, 8 - bit, 0), 16 * bit, 1)
        above = pltpu.roll(pltpu.roll(v, bit, 0), 128 - 16 * bit, 1) if bit < 4 else below
        low = (sub & bit) == 0
        same = low == ((grp & bit) == 0)
        v = jnp.where(same, v, jnp.where(low, below, above))
    return v


def node_rows(nodes, p, r):
    sub = iota((8, 128), 0)
    x = [nodes[c, p, pl.ds(r, 1), :] for c in range(3)]
    square = x[0] * x[0] + x[1] * x[1] + x[2] * x[2]
    rows = jnp.where((sub == 0) | (sub == 3), -2.0 * x[0], 0.0)
    rows = jnp.where((sub == 1) | (sub == 4), -2.0 * x[1], rows)
    rows = jnp.where((sub == 2) | (sub == 5), -2.0 * x[2], rows)
    rows = jnp.where(sub == 7, square, rows)
    hi, mid, lo = split3(rows)
    one = sub == 6
    second = (sub >= 3) & (sub < 6)
    parts = [
        jnp.where(one, 1.0, jnp.where(second, mid, hi)),
        jnp.where(one, 1.0, jnp.where(sub < 3, hi, mid)),
        jnp.where(one, 1.0, jnp.where(second, hi, lo)),
        jnp.zeros((8, 128), F32),
    ]
    return jnp.concatenate(parts, axis=0).astype(BF16)


def control_rows(p):
    sub = iota((8, 128), 0)
    p = jnp.where(sub < 3, p, 0.0)
    square = jnp.sum(p * p, axis=0, keepdims=True)
    rows = p + pltpu.roll(p, 3, 0) + jnp.where(sub == 6, square, 0.0)
    hi, mid, lo = split3(rows)
    one = sub == 7
    parts = [
        jnp.where(one, 1.0, hi),
        jnp.where(one, 1.0, mid),
        jnp.where(one, 1.0, jnp.where(sub < 3, hi, lo)),
        jnp.zeros((8, 128), F32),
    ]
    return parts


LINES = 64
MORE = 16


def gather_kernel(
    points_hbm,
    modes_hbm,
    pressure_hbm,
    area_hbm,
    center_hbm,
    nodes_hbm,
    ids_hbm,
    counts_hbm,
    motion_hbm,
    inverse_mass_hbm,
    all_ids,
    counts,
    feats,
    left_a,
    left_b,
    right,
    rigid,
    accelerations,
    buf,
    nodes,
    more_nodes,
    points,
    modes,
    pressure,
    area,
    center,
    pack,
    turn,
    own,
    motion,
    inverse_mass,
    fetch,
    send,
    recv,
):
    x, y, z, core = place()
    group = core * YS + y
    plane = [(i * core, i * (1 - core)) for i in range(1, 4)]
    turned = [(i * (1 - core), i * core) for i in range(1, 4)]

    sources = (
        points_hbm,
        modes_hbm,
        pressure_hbm,
        area_hbm,
        center_hbm,
        nodes_hbm,
        ids_hbm,
        counts_hbm,
        motion_hbm,
        inverse_mass_hbm,
    )
    kept = all_ids.at[pl.ds(0, 8)]
    targets = (points, modes, pressure, area, center, nodes, kept, counts, motion, inverse_mass)
    fetches = [
        pltpu.make_async_copy(src, dst, fetch.at[i]) for i, (src, dst) in enumerate(zip(sources, targets))
    ]
    for copy in fetches:
        copy.start()

    along = {d: device(x, y, z + d, core) for d in (4, -4, 3, -3, 2, -2, 1, -1)}
    peers = [device(x + dx, y + dy, z, core) for dx, dy in plane]
    crossing = [device(x + dx, y + dy, z, core) for dx, dy in turned]
    barrier = pltpu.get_barrier_semaphore()
    greet = list(along.values()) + peers + crossing
    greet += [device(x, y, z, 1 - core)]
    for target in greet:
        pl.semaphore_signal(barrier, inc=1, device_id=target, device_id_type=MESH)

    for copy in fetches[:2]:
        copy.wait()
    pack[...] = jnp.zeros((24, 128), F32)
    pack[0:3, 0:16] = points[...]
    turn[...] = jnp.zeros((16, 128), F32)
    turn[:, 0:18] = modes[...]
    pack[3:21, 0:16] = jnp.transpose(turn[...], (1, 0))[0:18]
    packed = []
    for r in range(3):
        v = pack[8 * r : 8 * r + 8, :]
        for bit in (1, 2, 4):
            v = jnp.where((iota((8, 128), 0) & bit) == 0, v, pltpu.roll(v, 16 * bit, 1))
        packed.append(jnp.sum(v, axis=0, keepdims=True))

    for copy in fetches[2:]:
        copy.wait()
    force = jnp.zeros((3, 128), F32)
    moment = jnp.zeros((3, 128), F32)
    for i in range(pressure.shape[0]):
        at = pl.ds(i * 128, 128)
        pushed = area[:, at] * pressure[i : i + 1, :]
        c = center[:, at]
        force = force + pushed
        moment = moment + jnp.concatenate(
            [
                c[1:2] * pushed[2:3] - c[2:3] * pushed[1:2],
                c[2:3] * pushed[0:1] - c[0:1] * pushed[2:3],
                c[0:1] * pushed[1:2] - c[1:2] * pushed[0:1],
            ],
            axis=0,
        )
    sums = jnp.sum(jnp.concatenate([force, moment], axis=0), axis=1, keepdims=True)
    lane = iota((6, 128), 1)
    row = iota((6, 128), 0)
    loads = jnp.sum(jnp.where(lane == row + LOAD_LANE, sums, 0.0), axis=0, keepdims=True)
    own[0:1, :] = packed[0]
    own[1:2, :] = packed[1]
    own[2:3, :] = packed[2] + loads
    for r in range(3):
        buf[x, 4, r, pl.ds(group, 1), :] = own[r : r + 1, :]

    pl.semaphore_wait(barrier, len(greet))

    heavy = is_heavy()

    def hand(h, src_plane):
        target = device(heavy_x(z) + 1 + h, y, z, core)
        parts = []
        for i, (src, dst) in enumerate(
            ((nodes_hbm.at[:, pl.ds(src_plane, 2)], more_nodes), (ids_hbm.at[pl.ds(src_plane, 2)], all_ids.at[pl.ds(8, 2)]))
        ):
            parts.append(
                pltpu.make_async_remote_copy(
                    src_ref=src,
                    dst_ref=dst,
                    send_sem=send.at[29 + 2 * h + i],
                    recv_sem=recv.at[29 + i],
                    device_id=target,
                    device_id_type=MESH,
                )
            )
        return parts

    pending = []

    def put(src, dst, slot, target):
        copy = pltpu.make_async_remote_copy(
            src_ref=src,
            dst_ref=dst,
            send_sem=send.at[slot],
            recv_sem=recv.at[slot],
            device_id=target,
            device_id_type=MESH,
        )
        copy.start()
        pending.append(copy)
        return copy

    def slot(j):
        return buf.at[x, j, :, group]

    near = {}
    for d in (4, 3, 2, 1):
        near[d] = put(own, slot(4 - d), d - 1, along[d])
        near[-d] = put(own, slot(4 + d), d + 3, along[-d])

    @pl.when(heavy)
    def _():
        for h in range(3):
            for copy in hand(h, 1 + 2 * h):
                copy.start()

    def line(i, _):
        right[i] = node_rows(nodes, i >> 3, i & 7)
        return 0

    lax.fori_loop(0, LINES, line, 0, unroll=4)
    right[LINES + MORE] = jnp.zeros((32, 128), BF16)

    far = []
    for d in (1, 2, 3, 4):
        near[d].wait_recv()
        far.append(put(slot(4 - d), slot(16 - d), d + 7, along[4]))
        near[-d].wait_recv()
        if d < 4:
            far.append(put(slot(4 + d), slot(8 + d), d + 11, along[-4]))

    halves = (pl.ds(0, 9), pl.ds(9, 7))

    def first(part):
        ref = buf.at[x, halves[part], :, group]
        return [
            put(ref, ref, 15 + 3 * part + i, peer) for i, peer in enumerate(peers)
        ]

    def second(part, start):
        for i, target in enumerate(crossing):

            def make(ref, i=i, target=target):
                return pltpu.make_async_remote_copy(
                    src_ref=ref,
                    dst_ref=ref,
                    send_sem=send.at[21 + 3 * part + i],
                    recv_sem=recv.at[21 + 3 * part + i],
                    device_id=target,
                    device_id_type=MESH,
                )

            @pl.when(core == 0)
            def _():
                copy = make(buf.at[x, halves[part], :, pl.ds(0, YS)])
                copy.start() if start else copy.wait()

            @pl.when(core == 1)
            def _():
                copy = make(buf.at[:, halves[part], :, group])
                copy.start() if start else copy.wait()

    def across(part):
        ref = buf.at[:, halves[part], :, pl.ds(core * YS, YS)]
        return put(ref, ref, 27 + part, device(x, y, z, 1 - core))

    half = jnp.where(iota((128, 64), 1) < 32, 1.0, 0.0).astype(BF16)

    unit = jnp.where(iota((128, 128), 0) == iota((128, 128), 1), 1.0, 0.0).astype(BF16)

    def unpack(j, carry):
        for xx in range(XS):
            t = xx * ZS + ((j + z + ZS - 4) & (ZS - 1))
            v = [regroup(buf[xx, j, r]) for r in range(3)]
            for r in range(3):
                feats[t, pl.ds(8 * r, 8), :] = v[r]
            parts = control_rows(v[0])
            columns = lax.dot_general(
                unit,
                jnp.concatenate(parts + parts, axis=0).astype(BF16),
                (((1,), (1,)), ((), ())),
                preferred_element_type=F32,
            ).astype(BF16)
            left = columns * half
            left_a[t] = left
            left_b[t] = columns - left
            carry = carry + v[2]
        return carry

    first_near = first(0)
    for copy in first_near:
        copy.wait_recv()
    second(0, True)
    for copy in far:
        copy.wait_recv()
    first_far = first(1)
    for copy in first_far:
        copy.wait_recv()
    second(1, True)
    second(0, False)
    across_near = across(0)

    @pl.when(jnp.logical_not(heavy))
    def _():
        for copy in hand(0, 1):
            copy.wait_recv()

        def more(i, _):
            right[LINES + i] = node_rows(more_nodes, i >> 3, i & 7)
            return 0

        lax.fori_loop(0, MORE, more, 0, unroll=4)

    across_near.wait_recv()
    loads = lax.fori_loop(0, 5, unpack, jnp.zeros((8, 128), F32))
    second(1, False)
    across_far = across(1)
    loads = lax.fori_loop(5, 9, unpack, loads)
    across_far.wait_recv()
    loads = lax.fori_loop(9, ZS, unpack, loads)
    total = jnp.broadcast_to(loads[5:6, :], (8, 128))
    for by in (16, 32, 64):
        total = total + pltpu.roll(total, by, 1)
    for k in range(6):
        acceleration = inverse_mass[k] * jnp.broadcast_to(total[:, k : k + 1], (8, 128)) + GRAVITY[k]
        accelerations[k] = acceleration
        rigid[k] = TIME_STEP * motion[k] + 0.5 * TIME_STEP * TIME_STEP * acceleration
    for copy in pending:
        copy.wait_send()

    @pl.when(heavy)
    def _():
        for h in range(3):
            for copy in hand(h, 1 + 2 * h):
                copy.wait_send()


def gather(*arrays):
    points, modes, pressure, area, center, nodes, ids, counts, motion, inverse_mass = arrays
    vmem = pl.BlockSpec(memory_space=pltpu.VMEM)
    return pl.pallas_call(
        gather_kernel,
        out_shape=(
            jax.ShapeDtypeStruct((10, 8, 16), jnp.int32),
            jax.ShapeDtypeStruct((8, 8), jnp.int32),
            jax.ShapeDtypeStruct((NTILE, 24, 128), F32),
            jax.ShapeDtypeStruct((NTILE, 128, 64), BF16),
            jax.ShapeDtypeStruct((NTILE, 128, 64), BF16),
            jax.ShapeDtypeStruct((LINES + MORE + 1, 32, 128), BF16),
            jax.ShapeDtypeStruct((6, 8, 128), F32),
            jax.ShapeDtypeStruct((6, 8, 128), F32),
        ),
        in_specs=[pl.BlockSpec(memory_space=pltpu.HBM)] * 10,
        out_specs=(vmem,) * 8,
        scratch_shapes=[
            pltpu.VMEM((XS, ZS, 3, 8, 128), F32),
            pltpu.VMEM(nodes.shape, F32),
            pltpu.VMEM((3, 2, 8, 128), F32),
            pltpu.VMEM(points.shape, F32),
            pltpu.VMEM(modes.shape, F32),
            pltpu.VMEM(pressure.shape, F32),
            pltpu.VMEM(area.shape, F32),
            pltpu.VMEM(center.shape, F32),
            pltpu.VMEM((24, 128), F32),
            pltpu.VMEM((16, 128), F32),
            pltpu.VMEM((3, 128), F32),
            pltpu.SMEM((6,), F32),
            pltpu.SMEM((6,), F32),
            pltpu.SemaphoreType.DMA((10,)),
            pltpu.SemaphoreType.DMA((35,)),
            pltpu.SemaphoreType.DMA((31,)),
        ],
        compiler_params=pltpu.CompilerParams(
            collective_id=0, has_side_effects=True, vmem_limit_bytes=VMEM_LIMIT
        ),
        name="gather",
    )(*(pltpu.with_memory_space_constraint(v, pltpu.HBM) for v in arrays))


VMEM_LIMIT = 24 << 20


BLOCK = 32


def weights(s):
    s = jnp.minimum(jnp.maximum(s, 1e-30), 16.0)
    d = s * lax.rsqrt(s)
    v = 4.0 - d
    v = v * v
    k = v * v * (1.0 + d)
    hi = k.astype(BF16)
    return jnp.concatenate([hi, (k - hi.astype(F32)).astype(BF16)], axis=0)


def pair_kernel(
    role,
    ids_vmem,
    counts_vmem,
    motion_hbm,
    nodes_hbm,
    rigid,
    accelerations,
    feats,
    left_a,
    left_b,
    right,
    shift,
    more_shift,
    plane_edge,
    row_edge,
    state,
    mix_a,
    mix_b,
    sums,
    nodes,
    unit_of,
    ids,
    counts,
    motion,
    fetch,
):
    lines = LINES + MORE
    sources = (ids_vmem, counts_vmem, motion_hbm, nodes_hbm)
    fetches = [
        pltpu.make_async_copy(src, dst, fetch.at[i])
        for i, (src, dst) in enumerate(zip(sources, (ids, counts, motion, nodes)))
    ]
    for copy in fetches:
        copy.start()
    heavy = role[0]
    light = 1 - heavy
    sub = iota((8, 128), 0)
    zero = jnp.zeros((8, 128), F32)

    for i in range(lines + 1):
        sums[i] = zero
    for copy in fetches[:2]:
        copy.wait()

    def prepare(t, n):
        for e in range(4):
            unit_of[n + e] = (t << 6) + ids[t, e]
        n = n + light * counts[t >> 3, t & 7]
        c = jnp.zeros((3, 128), F32)
        for k in range(6):
            c = c + rigid[k, 0:3, :] * feats[t, 3 + 3 * k : 6 + 3 * k, :]
        c = c * (1.0 / 256.0)
        c = jnp.concatenate([c, c, jnp.zeros((2, 128), F32)], axis=0)
        c_hi = c.astype(BF16).astype(F32)
        c = jnp.where(sub < 3, c_hi, c - c_hi)
        mix_a[t] = jnp.concatenate([c, zero], axis=0).astype(BF16)
        mix_b[t] = jnp.concatenate([zero, c], axis=0).astype(BF16)
        return n

    n = lax.fori_loop(0, NTILE, prepare, jnp.int32(0), unroll=8)

    gap = jnp.zeros((32, 128), BF16)

    def pair(t1, t2, rhs):
        s = jnp.dot(left_a[t1] + left_b[t2], rhs, preferred_element_type=F32)
        m = mix_a[t1] + mix_b[t2]
        return jnp.dot(jnp.concatenate([m, m], axis=1), weights(s), preferred_element_type=F32)

    def beside(l1, l2):
        return jnp.concatenate(
            [jnp.concatenate([right[l1], gap], axis=1), jnp.concatenate([gap, right[l2]], axis=1)], axis=0
        )

    def full_line(i):
        own = jnp.where(i < 8, i, jnp.where(i < 15, (i - 7) << 3, i + 42))
        return jnp.where(heavy == 1, own, LINES + i + jnp.where(i < 7, 1, 2))

    def full(i):
        l1, l2 = full_line(i), full_line(i + 1)
        for e in range(16):
            out = pair(ids[l1, e], ids[l2, e], beside(l1, l2))
            sums[l1] += out[0:8, 0:128]
            sums[l2] += out[8:16, 128:256]

    def four(b, _):
        full(4 * b)
        full(4 * b + 2)
        return 0

    fours = jnp.where(heavy == 1, 5, 3)
    lax.fori_loop(0, fours, four, 0)
    full(4 * fours)
    for e in range(BLOCK):
        unit_of[n + e] = lines << 6

    def block(start, units):
        for u in range(0, units, 2):
            i = start + u
            c1, c2 = unit_of[i], unit_of[i + 1]
            l1, l2 = c1 >> 6, c2 >> 6
            out = pair(c1 & (NTILE - 1), c2 & (NTILE - 1), beside(l1, l2))
            sums[l1] += out[0:8, 0:128]
            sums[l2] += out[8:16, 128:256]
        return 0

    twos = n >> 6
    lax.fori_loop(0, twos, lambda g, _: block(g * 2 * BLOCK, 2 * BLOCK), 0)
    whole = (n + BLOCK // 2 - 1) >> 5
    lax.fori_loop(2 * twos, whole, lambda g, _: block(g * BLOCK, BLOCK), 0)
    lax.fori_loop(0, jnp.where(n > whole * BLOCK, 1, 0), lambda g, _: block(whole * BLOCK, BLOCK // 2), 0)

    for copy in fetches[2:]:
        copy.wait()
    for k in range(6):
        state[k] = motion[k] + TIME_STEP * accelerations[k][0, 0]
    for i in range(lines):
        v = sums[i]
        v = v + pltpu.roll(v, 5, 0)
        for c in range(3):
            if i < LINES:
                shift[c, i // 8, i % 8 : i % 8 + 1, :] = v[c : c + 1, :]
            else:
                more_shift[c, i // 8 - 8, i % 8 : i % 8 + 1, :] = v[c : c + 1, :]
    for c in range(3):
        plane_edge[0, c] = nodes[c, 0]
        plane_edge[1, c] = nodes[c, 0] + shift[c, 0]
        for p in range(8):
            row_edge[0, c, p : p + 1, :] = nodes[c, p, 0:1, :]
            row_edge[1, c, p : p + 1, :] = nodes[c, p, 0:1, :] + shift[c, p, 0:1, :]


def pair_sums(role, ids, counts, motion, nodes, rigid, accelerations, feats, left_a, left_b, right):
    vmem = pl.BlockSpec(memory_space=pltpu.VMEM)
    smem = pl.BlockSpec(memory_space=pltpu.SMEM)
    lines = LINES + MORE
    units = 4 * LINES + 2 * BLOCK
    return pl.pallas_call(
        pair_kernel,
        out_shape=(
            jax.ShapeDtypeStruct((3, 8, 8, 128), F32),
            jax.ShapeDtypeStruct((3, 2, 8, 128), F32),
            jax.ShapeDtypeStruct((2, 3, 8, 128), F32),
            jax.ShapeDtypeStruct((2, 3, 8, 128), F32),
            jax.ShapeDtypeStruct((6,), F32),
        ),
        in_specs=[smem, vmem, vmem] + [pl.BlockSpec(memory_space=pltpu.HBM)] * 2 + [vmem] * 6,
        out_specs=(vmem,) * 4 + (smem,),
        scratch_shapes=[
            pltpu.VMEM((NTILE, 16, 128), BF16),
            pltpu.VMEM((NTILE, 16, 128), BF16),
            pltpu.VMEM((lines + 1, 8, 128), F32),
            pltpu.VMEM((3, 8, 8, 128), F32),
            pltpu.SMEM((units,), jnp.int32),
            pltpu.SMEM((LINES + MORE, 16), jnp.int32),
            pltpu.SMEM((8, 8), jnp.int32),
            pltpu.SMEM((6,), F32),
            pltpu.SemaphoreType.DMA((4,)),
        ],
        compiler_params=pltpu.CompilerParams(vmem_limit_bytes=VMEM_LIMIT),
        name="pairs",
    )(role, ids, counts, motion, nodes, rigid, accelerations, feats, left_a, left_b, right)


def exchange_kernel(more_shift, plane_edge, row_edge, back, planes, rows, corners, send, recv):
    x, y, z, core = place()
    slab = lax.axis_index("slab")
    heavy = is_heavy()
    last = XS * ZS * CORES

    def at(ds, dy):
        return {"slab": (slab + ds) & (last - 1), "ctrl": (y + dy) & (YS - 1)}

    barrier = pltpu.get_barrier_semaphore()
    greet = [at(1, 0), at(-1, 0), at(0, 1), at(0, -1), at(1, 1), at(-1, -1)]
    greet += [device(x + i, y, z, core) for i in (1, 2, 3)]
    for target in greet:
        pl.semaphore_signal(barrier, inc=1, device_id=target, device_id_type=MESH)
    pl.semaphore_wait(barrier, len(greet))

    def put(src, dst, slot, target):
        return pltpu.make_async_remote_copy(
            src_ref=src,
            dst_ref=dst,
            send_sem=send.at[slot],
            recv_sem=recv.at[slot],
            device_id=target,
            device_id_type=MESH,
        )

    def give(h):
        return pltpu.make_async_remote_copy(
            src_ref=more_shift,
            dst_ref=back.at[h],
            send_sem=send.at[3],
            recv_sem=recv.at[3 + h],
            device_id=device(heavy_x(z), y, z, core),
            device_id_type=MESH,
        )

    mine = (x - heavy_x(z) + 3) & (XS - 1)

    @pl.when(jnp.logical_not(heavy))
    def _():
        give(jnp.minimum(mine, 2)).start()

    edges = [
        put(plane_edge, corners, 2, at(-1, -1)),
        put(plane_edge, planes, 0, at(-1, 0)),
        put(row_edge, rows, 1, at(0, -1)),
    ]
    for copy in edges:
        copy.start()

    @pl.when(heavy)
    def _():
        for h in range(3):
            give(h).wait_recv()

    @pl.when(jnp.logical_not(heavy))
    def _():
        give(jnp.minimum(mine, 2)).wait_send()

    for copy in edges:
        copy.wait()


def exchange(more_shift, plane_edge, row_edge):
    hbm = pl.BlockSpec(memory_space=pl.ANY)
    edge = jax.ShapeDtypeStruct((2, 3, 8, 128), F32)
    return pl.pallas_call(
        exchange_kernel,
        out_shape=(jax.ShapeDtypeStruct((3, 3, 2, 8, 128), F32), edge, edge, edge),
        in_specs=[hbm] * 3,
        out_specs=(hbm,) * 4,
        scratch_shapes=[pltpu.SemaphoreType.DMA((4,)), pltpu.SemaphoreType.DMA((6,))],
        compiler_params=pltpu.CompilerParams(
            collective_id=1, has_side_effects=True, vmem_limit_bytes=VMEM_LIMIT
        ),
        name="exchange",
    )(more_shift, plane_edge, row_edge)


def volume_kernel(role, nodes, shift, back, planes, rows, corners, out_shift, volume, change):
    slab, y = role[1], role[2]
    out_shift[...] = shift[...]

    @pl.when(role[0] == 1)
    def _():
        row = iota((8, 128), 0)
        for h in range(3):
            for c in range(3):
                for i in range(2):
                    p = 1 + 2 * h + i
                    out_shift[c, p] = jnp.where(row == 0, shift[c, p], back[h, c, i])

    bottom = iota((8, 128), 0) == 7

    def faces(field, c, p):
        if p < 8:
            a = nodes[c, p]
            if field:
                a = a + out_shift[c, p]
            edge = rows[field, c, p : p + 1, :]
        else:
            a = planes[field, c]
            edge = corners[field, c, 0:1, :]
        b = jnp.where(bottom, edge, pltpu.roll(a, 7, 0))
        az = pltpu.roll(a, 127, 1)
        bz = pltpu.roll(b, 127, 1)
        near, far = a + b, az + bz
        return near + far, (b + bz) - (a + az), far - near

    row = iota((8, 128), 0) + y * 8
    inside = jnp.logical_and(row < 31, iota((8, 128), 1) < 127)
    held = {}
    for p in range(9):
        for field in range(2):
            for c in range(3):
                held[field, c, p % 2] = faces(field, c, p)
        if p == 0:
            continue
        both = []
        for field in range(2):
            now = [held[field, c, p % 2] for c in range(3)]
            before = [held[field, c, (p - 1) % 2] for c in range(3)]
            ex = [0.25 * (n[0] - b[0]) for n, b in zip(now, before)]
            ey = [0.25 * (n[1] + b[1]) for n, b in zip(now, before)]
            ez = [0.25 * (n[2] + b[2]) for n, b in zip(now, before)]
            both.append(
                ex[0] * (ey[1] * ez[2] - ey[2] * ez[1])
                + ex[1] * (ey[2] * ez[0] - ey[0] * ez[2])
                + ex[2] * (ey[0] * ez[1] - ey[1] * ez[0])
            )
        ok = jnp.logical_and(inside, slab * 8 + p - 1 < 1023)
        old, new = (jnp.where(ok, v, 0.0) for v in both)
        volume[p - 1] = new
        change[p - 1] = new - old


def volumes(role, nodes, shift, back, planes, rows, corners):
    vmem = pl.BlockSpec(memory_space=pltpu.VMEM)
    return pl.pallas_call(
        volume_kernel,
        out_shape=(
            jax.ShapeDtypeStruct((3, 8, 8, 128), F32),
            jax.ShapeDtypeStruct((8, 8, 128), F32),
            jax.ShapeDtypeStruct((8, 8, 128), F32),
        ),
        in_specs=[pl.BlockSpec(memory_space=pltpu.SMEM)] + [vmem] * 6,
        out_specs=(vmem,) * 3,
        compiler_params=pltpu.CompilerParams(vmem_limit_bytes=VMEM_LIMIT),
        name="volumes",
    )(role, nodes, shift, back, planes, rows, corners)


def local(
    face_pressure,
    face_area,
    face_center,
    motion,
    inverse_mass,
    control_points,
    control_modes,
    node_points,
    tile_list,
    tile_count,
):
    all_ids, counts, feats, left_a, left_b, right, rigid, accelerations = gather(
        control_points,
        control_modes.T,
        face_pressure.reshape(-1, 128),
        face_area,
        face_center,
        node_points,
        tile_list,
        tile_count,
        motion,
        inverse_mass,
    )
    role = jnp.stack(
        [is_heavy().astype(jnp.int32), lax.axis_index("slab").astype(jnp.int32), lax.axis_index("ctrl").astype(jnp.int32)]
    )
    shift, more_shift, plane_edge, row_edge, new_state = pair_sums(
        role,
        all_ids.reshape(LINES + MORE, 16),
        counts,
        *(pltpu.with_memory_space_constraint(v, pltpu.HBM) for v in (motion, node_points)),
        rigid,
        accelerations,
        feats,
        left_a,
        left_b,
        right,
    )
    back, planes, rows, corners = exchange(more_shift, plane_edge, row_edge)
    node_shift, volume, change = volumes(role, node_points, shift, back, planes, rows, corners)
    return node_shift, volume, change, new_state


def solution(mesh):
    placed = (
        P(("slab", "ctrl")),
        P(None, ("slab", "ctrl")),
        P(None, ("slab", "ctrl")),
        P(),
        P(),
        P(None, ("slab", "ctrl")),
        P(None, ("slab", "ctrl")),
        P(None, "slab", "ctrl", None),
        P("slab", "ctrl", None),
        P("slab", "ctrl"),
    )
    return jax.shard_map(
        local,
        mesh=mesh,
        in_specs=placed,
        out_specs=(
            P(None, "slab", "ctrl", None),
            P("slab", "ctrl", None),
            P("slab", "ctrl", None),
            P(),
        ),
        check_vma=False,
    )
```

```python
import functools

import jax
import jax.numpy as jnp
from jax import lax
from jax.experimental import pallas as pl
from jax.experimental.pallas import tpu as pltpu
from jax.sharding import PartitionSpec as P

MESH = pl.DeviceIdType.MESH
TILE = 128
NTILE = 64
F32 = jnp.float32
BF16 = jnp.bfloat16
TIME_STEP = 0.5
GRAVITY = (0.0, 0.0, -0.5, 0.0, 0.0, 0.0)
XS, YS, ZS, CORES = 4, 4, 16, 2
LOAD_LANE = 80


def iota(shape, axis):
    return lax.broadcasted_iota(jnp.int32, shape, axis)


def place():
    slab = lax.axis_index("slab")
    return slab >> 5, lax.axis_index("ctrl"), (slab >> 1) & (ZS - 1), slab & 1


def device(x, y, z, core):
    return {"slab": ((x & (XS - 1)) << 5) + ((z & (ZS - 1)) << 1) + core, "ctrl": y & (YS - 1)}


def is_heavy():
    slab = lax.axis_index("slab")
    return jnp.logical_and(slab >= 48, slab < 80)


def heavy_x(z):
    return 2 - (z >> 3)


def split3(value):
    hi = value.astype(BF16).astype(F32)
    rest = value - hi
    mid = rest.astype(BF16).astype(F32)
    return hi, mid, rest - mid


def regroup(v):
    sub = iota((8, 128), 0)
    grp = iota((8, 128), 1) // 16
    for bit in (1, 2, 4):
        below = pltpu.roll(pltpu.roll(v, 8 - bit, 0), 16 * bit, 1)
        above = pltpu.roll(pltpu.roll(v, bit, 0), 128 - 16 * bit, 1) if bit < 4 else below
        low = (sub & bit) == 0
        same = low == ((grp & bit) == 0)
        v = jnp.where(same, v, jnp.where(low, below, above))
    return v


def node_rows(nodes, p, r):
    sub = iota((8, 128), 0)
    x = [nodes[c, p, pl.ds(r, 1), :] for c in range(3)]
    square = x[0] * x[0] + x[1] * x[1] + x[2] * x[2]
    rows = jnp.where((sub == 0) | (sub == 3), -2.0 * x[0], 0.0)
    rows = jnp.where((sub == 1) | (sub == 4), -2.0 * x[1], rows)
    rows = jnp.where((sub == 2) | (sub == 5), -2.0 * x[2], rows)
    rows = jnp.where(sub == 7, square, rows)
    hi, mid, lo = split3(rows)
    one = sub == 6
    second = (sub >= 3) & (sub < 6)
    parts = [
        jnp.where(one, 1.0, jnp.where(second, mid, hi)),
        jnp.where(one, 1.0, jnp.where(sub < 3, hi, mid)),
        jnp.where(one, 1.0, jnp.where(second, hi, lo)),
        jnp.zeros((8, 128), F32),
    ]
    return jnp.concatenate(parts, axis=0).astype(BF16)


def control_rows(p):
    sub = iota((8, 128), 0)
    p = jnp.where(sub < 3, p, 0.0)
    square = jnp.sum(p * p, axis=0, keepdims=True)
    rows = p + pltpu.roll(p, 3, 0) + jnp.where(sub == 6, square, 0.0)
    hi, mid, lo = split3(rows)
    one = sub == 7
    parts = [
        jnp.where(one, 1.0, hi),
        jnp.where(one, 1.0, mid),
        jnp.where(one, 1.0, jnp.where(sub < 3, hi, lo)),
        jnp.zeros((8, 128), F32),
    ]
    return parts


LINES = 64
MORE = 16


def gather_kernel(
    points_hbm,
    modes_hbm,
    pressure_hbm,
    area_hbm,
    center_hbm,
    nodes_hbm,
    ids_hbm,
    counts_hbm,
    motion_hbm,
    inverse_mass_hbm,
    all_ids,
    counts,
    feats,
    left_a,
    left_b,
    right,
    rigid,
    accelerations,
    buf,
    nodes,
    more_nodes,
    points,
    modes,
    pressure,
    area,
    center,
    pack,
    turn,
    own,
    motion,
    inverse_mass,
    fetch,
    send,
    recv,
):
    x, y, z, core = place()
    group = core * YS + y
    plane = [(i * core, i * (1 - core)) for i in range(1, 4)]
    turned = [(i * (1 - core), i * core) for i in range(1, 4)]

    sources = (
        points_hbm,
        modes_hbm,
        pressure_hbm,
        area_hbm,
        center_hbm,
        nodes_hbm,
        ids_hbm,
        counts_hbm,
        motion_hbm,
        inverse_mass_hbm,
    )
    kept = all_ids.at[pl.ds(0, 8)]
    targets = (points, modes, pressure, area, center, nodes, kept, counts, motion, inverse_mass)
    fetches = [
        pltpu.make_async_copy(src, dst, fetch.at[i]) for i, (src, dst) in enumerate(zip(sources, targets))
    ]
    for copy in fetches:
        copy.start()

    along = {d: device(x, y, z + d, core) for d in (4, -4, 3, -3, 2, -2, 1, -1)}
    peers = [device(x + dx, y + dy, z, core) for dx, dy in plane]
    crossing = [device(x + dx, y + dy, z, core) for dx, dy in turned]
    barrier = pltpu.get_barrier_semaphore()
    greet = list(along.values()) + peers + crossing
    greet += [device(x, y, z, 1 - core)]
    for target in greet:
        pl.semaphore_signal(barrier, inc=1, device_id=target, device_id_type=MESH)

    for copy in fetches[:2]:
        copy.wait()
    pack[...] = jnp.zeros((24, 128), F32)
    pack[0:3, 0:16] = points[...]
    turn[...] = jnp.zeros((16, 128), F32)
    turn[:, 0:18] = modes[...]
    pack[3:21, 0:16] = jnp.transpose(turn[...], (1, 0))[0:18]
    packed = []
    for r in range(3):
        v = pack[8 * r : 8 * r + 8, :]
        for bit in (1, 2, 4):
            v = jnp.where((iota((8, 128), 0) & bit) == 0, v, pltpu.roll(v, 16 * bit, 1))
        packed.append(jnp.sum(v, axis=0, keepdims=True))

    for copy in fetches[2:]:
        copy.wait()
    force = jnp.zeros((3, 128), F32)
    moment = jnp.zeros((3, 128), F32)
    for i in range(pressure.shape[0]):
        at = pl.ds(i * 128, 128)
        pushed = area[:, at] * pressure[i : i + 1, :]
        c = center[:, at]
        force = force + pushed
        moment = moment + jnp.concatenate(
            [
                c[1:2] * pushed[2:3] - c[2:3] * pushed[1:2],
                c[2:3] * pushed[0:1] - c[0:1] * pushed[2:3],
                c[0:1] * pushed[1:2] - c[1:2] * pushed[0:1],
            ],
            axis=0,
        )
    sums = jnp.sum(jnp.concatenate([force, moment], axis=0), axis=1, keepdims=True)
    lane = iota((6, 128), 1)
    row = iota((6, 128), 0)
    loads = jnp.sum(jnp.where(lane == row + LOAD_LANE, sums, 0.0), axis=0, keepdims=True)
    own[0:1, :] = packed[0]
    own[1:2, :] = packed[1]
    own[2:3, :] = packed[2] + loads
    for r in range(3):
        buf[x, 4, r, pl.ds(group, 1), :] = own[r : r + 1, :]

    pl.semaphore_wait(barrier, len(greet))

    heavy = is_heavy()

    def hand(h, src_plane):
        target = device(heavy_x(z) + 1 + h, y, z, core)
        parts = []
        for i, (src, dst) in enumerate(
            ((nodes_hbm.at[:, pl.ds(src_plane, 2)], more_nodes), (ids_hbm.at[pl.ds(src_plane, 2)], all_ids.at[pl.ds(8, 2)]))
        ):
            parts.append(
                pltpu.make_async_remote_copy(
                    src_ref=src,
                    dst_ref=dst,
                    send_sem=send.at[29 + 2 * h + i],
                    recv_sem=recv.at[29 + i],
                    device_id=target,
                    device_id_type=MESH,
                )
            )
        return parts

    pending = []

    def put(src, dst, slot, target):
        copy = pltpu.make_async_remote_copy(
            src_ref=src,
            dst_ref=dst,
            send_sem=send.at[slot],
            recv_sem=recv.at[slot],
            device_id=target,
            device_id_type=MESH,
        )
        copy.start()
        pending.append(copy)
        return copy

    def slot(j):
        return buf.at[x, j, :, group]

    near = {}
    for d in (4, 3, 2, 1):
        near[d] = put(own, slot(4 - d), d - 1, along[d])
        near[-d] = put(own, slot(4 + d), d + 3, along[-d])

    @pl.when(heavy)
    def _():
        for h in range(3):
            for copy in hand(h, 1 + 2 * h):
                copy.start()

    def line(i, _):
        right[i] = node_rows(nodes, i >> 3, i & 7)
        return 0

    lax.fori_loop(0, LINES, line, 0, unroll=4)
    right[LINES + MORE] = jnp.zeros((32, 128), BF16)

    far = []
    for d in (1, 2, 3, 4):
        near[d].wait_recv()
        far.append(put(slot(4 - d), slot(16 - d), d + 7, along[4]))
        near[-d].wait_recv()
        if d < 4:
            far.append(put(slot(4 + d), slot(8 + d), d + 11, along[-4]))

    halves = (pl.ds(0, 9), pl.ds(9, 7))

    def first(part):
        ref = buf.at[x, halves[part], :, group]
        return [
            put(ref, ref, 15 + 3 * part + i, peer) for i, peer in enumerate(peers)
        ]

    def second(part, start):
        for i, target in enumerate(crossing):

            def make(ref, i=i, target=target):
                return pltpu.make_async_remote_copy(
                    src_ref=ref,
                    dst_ref=ref,
                    send_sem=send.at[21 + 3 * part + i],
                    recv_sem=recv.at[21 + 3 * part + i],
                    device_id=target,
                    device_id_type=MESH,
                )

            @pl.when(core == 0)
            def _():
                copy = make(buf.at[x, halves[part], :, pl.ds(0, YS)])
                copy.start() if start else copy.wait()

            @pl.when(core == 1)
            def _():
                copy = make(buf.at[:, halves[part], :, group])
                copy.start() if start else copy.wait()

    def across(part):
        ref = buf.at[:, halves[part], :, pl.ds(core * YS, YS)]
        return put(ref, ref, 27 + part, device(x, y, z, 1 - core))

    half = jnp.where(iota((128, 64), 1) < 32, 1.0, 0.0).astype(BF16)

    def unpack(j, carry):
        for xx in range(XS):
            t = xx * ZS + ((j + z + ZS - 4) & (ZS - 1))
            v = [regroup(buf[xx, j, r]) for r in range(3)]
            for r in range(3):
                feats[t, pl.ds(8 * r, 8), :] = v[r]
            parts = control_rows(v[0])
            columns = jnp.transpose(jnp.concatenate(parts + parts, axis=0), (1, 0)).astype(BF16)
            left = columns * half
            left_a[t] = left
            left_b[t] = columns - left
            carry = carry + v[2]
        return carry

    first_near = first(0)
    for copy in first_near:
        copy.wait_recv()
    second(0, True)
    for copy in far:
        copy.wait_recv()
    first_far = first(1)
    for copy in first_far:
        copy.wait_recv()
    second(1, True)
    second(0, False)
    across_near = across(0)

    @pl.when(jnp.logical_not(heavy))
    def _():
        for copy in hand(0, 1):
            copy.wait_recv()

        def more(i, _):
            right[LINES + i] = node_rows(more_nodes, i >> 3, i & 7)
            return 0

        lax.fori_loop(0, MORE, more, 0, unroll=4)

    across_near.wait_recv()
    loads = lax.fori_loop(0, 5, unpack, jnp.zeros((8, 128), F32))
    second(1, False)
    across_far = across(1)
    loads = lax.fori_loop(5, 9, unpack, loads)
    across_far.wait_recv()
    loads = lax.fori_loop(9, ZS, unpack, loads)
    total = jnp.broadcast_to(loads[5:6, :], (8, 128))
    for by in (16, 32, 64):
        total = total + pltpu.roll(total, by, 1)
    for k in range(6):
        acceleration = inverse_mass[k] * jnp.broadcast_to(total[:, k : k + 1], (8, 128)) + GRAVITY[k]
        accelerations[k] = acceleration
        rigid[k] = TIME_STEP * motion[k] + 0.5 * TIME_STEP * TIME_STEP * acceleration
    for copy in pending:
        copy.wait_send()

    @pl.when(heavy)
    def _():
        for h in range(3):
            for copy in hand(h, 1 + 2 * h):
                copy.wait_send()


def gather(*arrays):
    points, modes, pressure, area, center, nodes, ids, counts, motion, inverse_mass = arrays
    vmem = pl.BlockSpec(memory_space=pltpu.VMEM)
    return pl.pallas_call(
        gather_kernel,
        out_shape=(
            jax.ShapeDtypeStruct((10, 8, 16), jnp.int32),
            jax.ShapeDtypeStruct((8, 8), jnp.int32),
            jax.ShapeDtypeStruct((NTILE, 24, 128), F32),
            jax.ShapeDtypeStruct((NTILE, 128, 64), BF16),
            jax.ShapeDtypeStruct((NTILE, 128, 64), BF16),
            jax.ShapeDtypeStruct((LINES + MORE + 1, 32, 128), BF16),
            jax.ShapeDtypeStruct((6, 8, 128), F32),
            jax.ShapeDtypeStruct((6, 8, 128), F32),
        ),
        in_specs=[pl.BlockSpec(memory_space=pltpu.HBM)] * 10,
        out_specs=(vmem,) * 8,
        scratch_shapes=[
            pltpu.VMEM((XS, ZS, 3, 8, 128), F32),
            pltpu.VMEM(nodes.shape, F32),
            pltpu.VMEM((3, 2, 8, 128), F32),
            pltpu.VMEM(points.shape, F32),
            pltpu.VMEM(modes.shape, F32),
            pltpu.VMEM(pressure.shape, F32),
            pltpu.VMEM(area.shape, F32),
            pltpu.VMEM(center.shape, F32),
            pltpu.VMEM((24, 128), F32),
            pltpu.VMEM((16, 128), F32),
            pltpu.VMEM((3, 128), F32),
            pltpu.SMEM((6,), F32),
            pltpu.SMEM((6,), F32),
            pltpu.SemaphoreType.DMA((10,)),
            pltpu.SemaphoreType.DMA((35,)),
            pltpu.SemaphoreType.DMA((31,)),
        ],
        compiler_params=pltpu.CompilerParams(
            collective_id=0, has_side_effects=True, vmem_limit_bytes=VMEM_LIMIT
        ),
        name="gather",
    )(*(pltpu.with_memory_space_constraint(v, pltpu.HBM) for v in arrays))


VMEM_LIMIT = 24 << 20


BLOCK = 32


def weights(s):
    s = jnp.minimum(jnp.maximum(s, 1e-30), 16.0)
    d = s * lax.rsqrt(s)
    v = 4.0 - d
    v = v * v
    k = v * v * (1.0 + d)
    hi = k.astype(BF16)
    return jnp.concatenate([hi, (k - hi.astype(F32)).astype(BF16)], axis=0)


def pair_kernel(
    role,
    ids_vmem,
    counts_vmem,
    motion_hbm,
    nodes_hbm,
    rigid,
    accelerations,
    feats,
    left_a,
    left_b,
    right,
    shift,
    more_shift,
    plane_edge,
    row_edge,
    state,
    mix_a,
    mix_b,
    sums,
    nodes,
    unit_of,
    ids,
    counts,
    motion,
    fetch,
):
    lines = LINES + MORE
    sources = (ids_vmem, counts_vmem, motion_hbm, nodes_hbm)
    fetches = [
        pltpu.make_async_copy(src, dst, fetch.at[i])
        for i, (src, dst) in enumerate(zip(sources, (ids, counts, motion, nodes)))
    ]
    for copy in fetches:
        copy.start()
    heavy = role[0]
    light = 1 - heavy
    sub = iota((8, 128), 0)
    zero = jnp.zeros((8, 128), F32)

    for i in range(lines + 1):
        sums[i] = zero
    for copy in fetches[:2]:
        copy.wait()

    def prepare(t, n):
        for e in range(4):
            unit_of[n + e] = (t << 6) + ids[t, e]
        n = n + light * counts[t >> 3, t & 7]
        c = jnp.zeros((3, 128), F32)
        for k in range(6):
            c = c + rigid[k, 0:3, :] * feats[t, 3 + 3 * k : 6 + 3 * k, :]
        c = c * (1.0 / 256.0)
        c = jnp.concatenate([c, c, jnp.zeros((2, 128), F32)], axis=0)
        c_hi = c.astype(BF16).astype(F32)
        c = jnp.where(sub < 3, c_hi, c - c_hi)
        mix_a[t] = jnp.concatenate([c, zero], axis=0).astype(BF16)
        mix_b[t] = jnp.concatenate([zero, c], axis=0).astype(BF16)
        return n

    n = lax.fori_loop(0, NTILE, prepare, jnp.int32(0), unroll=8)

    gap = jnp.zeros((32, 128), BF16)

    def pair(t1, t2, rhs):
        s = jnp.dot(left_a[t1] + left_b[t2], rhs, preferred_element_type=F32)
        m = mix_a[t1] + mix_b[t2]
        return jnp.dot(jnp.concatenate([m, m], axis=1), weights(s), preferred_element_type=F32)

    def beside(l1, l2):
        return jnp.concatenate(
            [jnp.concatenate([right[l1], gap], axis=1), jnp.concatenate([gap, right[l2]], axis=1)], axis=0
        )

    def full_line(i):
        own = jnp.where(i < 8, i, jnp.where(i < 15, (i - 7) << 3, i + 42))
        return jnp.where(heavy == 1, own, LINES + i + jnp.where(i < 7, 1, 2))

    def full(i):
        l1, l2 = full_line(i), full_line(i + 1)
        for e in range(16):
            out = pair(ids[l1, e], ids[l2, e], beside(l1, l2))
            sums[l1] += out[0:8, 0:128]
            sums[l2] += out[8:16, 128:256]

    def four(b, _):
        full(4 * b)
        full(4 * b + 2)
        return 0

    fours = jnp.where(heavy == 1, 5, 3)
    lax.fori_loop(0, fours, four, 0)
    full(4 * fours)
    for e in range(BLOCK):
        unit_of[n + e] = lines << 6

    def block(start, units):
        for u in range(0, units, 2):
            i = start + u
            c1, c2 = unit_of[i], unit_of[i + 1]
            l1, l2 = c1 >> 6, c2 >> 6
            out = pair(c1 & (NTILE - 1), c2 & (NTILE - 1), beside(l1, l2))
            sums[l1] += out[0:8, 0:128]
            sums[l2] += out[8:16, 128:256]
        return 0

    twos = n >> 6
    lax.fori_loop(0, twos, lambda g, _: block(g * 2 * BLOCK, 2 * BLOCK), 0)
    whole = (n + BLOCK // 2 - 1) >> 5
    lax.fori_loop(2 * twos, whole, lambda g, _: block(g * BLOCK, BLOCK), 0)
    lax.fori_loop(0, jnp.where(n > whole * BLOCK, 1, 0), lambda g, _: block(whole * BLOCK, BLOCK // 2), 0)

    for copy in fetches[2:]:
        copy.wait()
    for k in range(6):
        state[k] = motion[k] + TIME_STEP * accelerations[k][0, 0]
    for i in range(lines):
        v = sums[i]
        v = v + pltpu.roll(v, 5, 0)
        for c in range(3):
            if i < LINES:
                shift[c, i // 8, i % 8 : i % 8 + 1, :] = v[c : c + 1, :]
            else:
                more_shift[c, i // 8 - 8, i % 8 : i % 8 + 1, :] = v[c : c + 1, :]
    for c in range(3):
        plane_edge[0, c] = nodes[c, 0]
        plane_edge[1, c] = nodes[c, 0] + shift[c, 0]
        for p in range(8):
            row_edge[0, c, p : p + 1, :] = nodes[c, p, 0:1, :]
            row_edge[1, c, p : p + 1, :] = nodes[c, p, 0:1, :] + shift[c, p, 0:1, :]


def pair_sums(role, ids, counts, motion, nodes, rigid, accelerations, feats, left_a, left_b, right):
    vmem = pl.BlockSpec(memory_space=pltpu.VMEM)
    smem = pl.BlockSpec(memory_space=pltpu.SMEM)
    lines = LINES + MORE
    units = 4 * LINES + 2 * BLOCK
    return pl.pallas_call(
        pair_kernel,
        out_shape=(
            jax.ShapeDtypeStruct((3, 8, 8, 128), F32),
            jax.ShapeDtypeStruct((3, 2, 8, 128), F32),
            jax.ShapeDtypeStruct((2, 3, 8, 128), F32),
            jax.ShapeDtypeStruct((2, 3, 8, 128), F32),
            jax.ShapeDtypeStruct((6,), F32),
        ),
        in_specs=[smem, vmem, vmem] + [pl.BlockSpec(memory_space=pltpu.HBM)] * 2 + [vmem] * 6,
        out_specs=(vmem,) * 4 + (smem,),
        scratch_shapes=[
            pltpu.VMEM((NTILE, 16, 128), BF16),
            pltpu.VMEM((NTILE, 16, 128), BF16),
            pltpu.VMEM((lines + 1, 8, 128), F32),
            pltpu.VMEM((3, 8, 8, 128), F32),
            pltpu.SMEM((units,), jnp.int32),
            pltpu.SMEM((LINES + MORE, 16), jnp.int32),
            pltpu.SMEM((8, 8), jnp.int32),
            pltpu.SMEM((6,), F32),
            pltpu.SemaphoreType.DMA((4,)),
        ],
        compiler_params=pltpu.CompilerParams(vmem_limit_bytes=VMEM_LIMIT),
        name="pairs",
    )(role, ids, counts, motion, nodes, rigid, accelerations, feats, left_a, left_b, right)


def exchange_kernel(more_shift, plane_edge, row_edge, back, planes, rows, corners, send, recv):
    x, y, z, core = place()
    slab = lax.axis_index("slab")
    heavy = is_heavy()
    last = XS * ZS * CORES

    def at(ds, dy):
        return {"slab": (slab + ds) & (last - 1), "ctrl": (y + dy) & (YS - 1)}

    barrier = pltpu.get_barrier_semaphore()
    greet = [at(1, 0), at(-1, 0), at(0, 1), at(0, -1), at(1, 1), at(-1, -1)]
    greet += [device(x + i, y, z, core) for i in (1, 2, 3)]
    for target in greet:
        pl.semaphore_signal(barrier, inc=1, device_id=target, device_id_type=MESH)
    pl.semaphore_wait(barrier, len(greet))

    def put(src, dst, slot, target):
        return pltpu.make_async_remote_copy(
            src_ref=src,
            dst_ref=dst,
            send_sem=send.at[slot],
            recv_sem=recv.at[slot],
            device_id=target,
            device_id_type=MESH,
        )

    def give(h):
        return pltpu.make_async_remote_copy(
            src_ref=more_shift,
            dst_ref=back.at[h],
            send_sem=send.at[3],
            recv_sem=recv.at[3 + h],
            device_id=device(heavy_x(z), y, z, core),
            device_id_type=MESH,
        )

    mine = (x - heavy_x(z) + 3) & (XS - 1)

    @pl.when(jnp.logical_not(heavy))
    def _():
        give(jnp.minimum(mine, 2)).start()

    edges = [
        put(plane_edge, corners, 2, at(-1, -1)),
        put(plane_edge, planes, 0, at(-1, 0)),
        put(row_edge, rows, 1, at(0, -1)),
    ]
    for copy in edges:
        copy.start()

    @pl.when(heavy)
    def _():
        for h in range(3):
            give(h).wait_recv()

    @pl.when(jnp.logical_not(heavy))
    def _():
        give(jnp.minimum(mine, 2)).wait_send()

    for copy in edges:
        copy.wait()


def exchange(more_shift, plane_edge, row_edge):
    hbm = pl.BlockSpec(memory_space=pl.ANY)
    edge = jax.ShapeDtypeStruct((2, 3, 8, 128), F32)
    return pl.pallas_call(
        exchange_kernel,
        out_shape=(jax.ShapeDtypeStruct((3, 3, 2, 8, 128), F32), edge, edge, edge),
        in_specs=[hbm] * 3,
        out_specs=(hbm,) * 4,
        scratch_shapes=[pltpu.SemaphoreType.DMA((4,)), pltpu.SemaphoreType.DMA((6,))],
        compiler_params=pltpu.CompilerParams(
            collective_id=1, has_side_effects=True, vmem_limit_bytes=VMEM_LIMIT
        ),
        name="exchange",
    )(more_shift, plane_edge, row_edge)


def volume_kernel(role, nodes, shift, back, planes, rows, corners, out_shift, volume, change):
    slab, y = role[1], role[2]
    out_shift[...] = shift[...]

    @pl.when(role[0] == 1)
    def _():
        row = iota((8, 128), 0)
        for h in range(3):
            for c in range(3):
                for i in range(2):
                    p = 1 + 2 * h + i
                    out_shift[c, p] = jnp.where(row == 0, shift[c, p], back[h, c, i])

    bottom = iota((8, 128), 0) == 7

    def faces(field, c, p):
        if p < 8:
            a = nodes[c, p]
            if field:
                a = a + out_shift[c, p]
            edge = rows[field, c, p : p + 1, :]
        else:
            a = planes[field, c]
            edge = corners[field, c, 0:1, :]
        b = jnp.where(bottom, edge, pltpu.roll(a, 7, 0))
        az = pltpu.roll(a, 127, 1)
        bz = pltpu.roll(b, 127, 1)
        near, far = a + b, az + bz
        return near + far, (b + bz) - (a + az), far - near

    row = iota((8, 128), 0) + y * 8
    inside = jnp.logical_and(row < 31, iota((8, 128), 1) < 127)
    held = {}
    for p in range(9):
        for field in range(2):
            for c in range(3):
                held[field, c, p % 2] = faces(field, c, p)
        if p == 0:
            continue
        both = []
        for field in range(2):
            now = [held[field, c, p % 2] for c in range(3)]
            before = [held[field, c, (p - 1) % 2] for c in range(3)]
            ex = [0.25 * (n[0] - b[0]) for n, b in zip(now, before)]
            ey = [0.25 * (n[1] + b[1]) for n, b in zip(now, before)]
            ez = [0.25 * (n[2] + b[2]) for n, b in zip(now, before)]
            both.append(
                ex[0] * (ey[1] * ez[2] - ey[2] * ez[1])
                + ex[1] * (ey[2] * ez[0] - ey[0] * ez[2])
                + ex[2] * (ey[0] * ez[1] - ey[1] * ez[0])
            )
        ok = jnp.logical_and(inside, slab * 8 + p - 1 < 1023)
        old, new = (jnp.where(ok, v, 0.0) for v in both)
        volume[p - 1] = new
        change[p - 1] = new - old


def volumes(role, nodes, shift, back, planes, rows, corners):
    vmem = pl.BlockSpec(memory_space=pltpu.VMEM)
    return pl.pallas_call(
        volume_kernel,
        out_shape=(
            jax.ShapeDtypeStruct((3, 8, 8, 128), F32),
            jax.ShapeDtypeStruct((8, 8, 128), F32),
            jax.ShapeDtypeStruct((8, 8, 128), F32),
        ),
        in_specs=[pl.BlockSpec(memory_space=pltpu.SMEM)] + [vmem] * 6,
        out_specs=(vmem,) * 3,
        compiler_params=pltpu.CompilerParams(vmem_limit_bytes=VMEM_LIMIT),
        name="volumes",
    )(role, nodes, shift, back, planes, rows, corners)


def local(
    face_pressure,
    face_area,
    face_center,
    motion,
    inverse_mass,
    control_points,
    control_modes,
    node_points,
    tile_list,
    tile_count,
):
    all_ids, counts, feats, left_a, left_b, right, rigid, accelerations = gather(
        control_points,
        control_modes.T,
        face_pressure.reshape(-1, 128),
        face_area,
        face_center,
        node_points,
        tile_list,
        tile_count,
        motion,
        inverse_mass,
    )
    role = jnp.stack(
        [is_heavy().astype(jnp.int32), lax.axis_index("slab").astype(jnp.int32), lax.axis_index("ctrl").astype(jnp.int32)]
    )
    shift, more_shift, plane_edge, row_edge, new_state = pair_sums(
        role,
        all_ids.reshape(LINES + MORE, 16),
        counts,
        *(pltpu.with_memory_space_constraint(v, pltpu.HBM) for v in (motion, node_points)),
        rigid,
        accelerations,
        feats,
        left_a,
        left_b,
        right,
    )
    back, planes, rows, corners = exchange(more_shift, plane_edge, row_edge)
    node_shift, volume, change = volumes(role, node_points, shift, back, planes, rows, corners)
    return node_shift, volume, change, new_state


def solution(mesh):
    placed = (
        P(("slab", "ctrl")),
        P(None, ("slab", "ctrl")),
        P(None, ("slab", "ctrl")),
        P(),
        P(),
        P(None, ("slab", "ctrl")),
        P(None, ("slab", "ctrl")),
        P(None, "slab", "ctrl", None),
        P("slab", "ctrl", None),
        P("slab", "ctrl"),
    )
    return jax.shard_map(
        local,
        mesh=mesh,
        in_specs=placed,
        out_specs=(
            P(None, "slab", "ctrl", None),
            P("slab", "ctrl", None),
            P("slab", "ctrl", None),
            P(),
        ),
        check_vma=False,
    )
```
